32 devices in a mesh: dp: 8 (over z, core), seq: 4 (over y, x).
Axes of the slice: x: 2, y: 2, z: 4, core: 2. Of those that a mesh axis runs over, the one named last changes fastest.
Arguments:
- inputs: bfloat16 [24, 512, 1024], P('dp', 'seq'), may hold values from -6 to 6
- w_query: bfloat16 [1024, 1024], P('dp'), may hold values from -0.1875 to 0.1875
- w_key: bfloat16 [1024, 1024], P('dp'), may hold values from -0.1875 to 0.1875
- w_value: bfloat16 [1024, 1024], P('dp'), may hold values from -0.1875 to 0.1875
- b_query: bfloat16 [1024], P('dp'), may hold values from -4 to 4
- b_value: bfloat16 [1024], P('dp'), may hold values from -0.75 to 0.75
- w_out: bfloat16 [1024, 1024], P('dp'), may hold values from -2.5 to 2.5
- b_out: bfloat16 [1024], P('dp'), may hold values from -4 to 4
- gain_one: bfloat16 [1024], P('dp'), may hold values from 0.5 to 1.5
- shift_one: bfloat16 [1024], P('dp'), may hold values from -4 to 4
- w_up: bfloat16 [1024, 4096], P('dp'), may hold values from -0.1875 to 0.1875
- b_up: bfloat16 [4096], P('dp'), may hold values from -6 to 6
- w_down: bfloat16 [4096, 1024], P('dp'), may hold values from -0.09375 to 0.09375
- b_down: bfloat16 [1024], P('dp'), may hold values from -4 to 4
- gain_two: bfloat16 [1024], P('dp'), may hold values from 0.5 to 1.5
- shift_two: bfloat16 [1024], P('dp'), may hold values from -4 to 4
- cotangent: bfloat16 [24, 512, 1024], P('dp', 'seq'), may hold values from -6 to 6
Outputs:
- output: bfloat16 [24, 512, 1024], P('dp', 'seq')
- grad_inputs: float32 [24, 512, 1024], P('dp', 'seq')
- grad_w_query: float32 [1024, 1024], P('dp')
- grad_w_key: float32 [1024, 1024], P('dp')
- grad_w_value: float32 [1024, 1024], P('dp')
- grad_b_query: float32 [1024], P('dp')
- grad_b_value: float32 [1024], P('dp')
- grad_w_out: float32 [1024, 1024], P('dp')
- grad_b_out: float32 [1024], P('dp')
- grad_gain_one: float32 [1024], P('dp')
- grad_shift_one: float32 [1024], P('dp')
- grad_w_up: float32 [1024, 4096], P('dp')
- grad_b_up: float32 [4096], P('dp')
- grad_w_down: float32 [4096, 1024], P('dp')
- grad_b_down: float32 [1024], P('dp')
- grad_gain_two: float32 [1024], P('dp')
- grad_shift_two: float32 [1024], P('dp')
The draws below stay inside these ranges and needn't reach their ends.
All inputs are finite; a program needn't handle non-finite values.
Results may differ from the reference program's by a relative error of at most 0.02.
Values may be sent and summed in bfloat16 or wider, within the bound.
No kernel may reach another device: no remote copies, remote signals or barrier semaphores. Data moves between devices by JAX's collectives and lax.ppermute only.
A program may use at most 192 MiB of HBM per device.

```python
import jax
import jax.numpy as jnp
from jax import lax

D = 1024
HEADS = 16
FF = 4096
HEAD_DIM = 64
LENGTH = 512
SEQS_GRP = 3
SEQS = 24
N_DP = 8


def block_levels(stream_key, shape, split, least, top_value):
    def one(position, blocks):
        draws = jax.random.uniform(jax.random.fold_in(jax.random.fold_in(stream_key, 6), position), (blocks,), jnp.float32, least / len(split), top_value / len(split))
        return jnp.repeat(jnp.exp(draws), shape[position] // blocks).reshape((-1,) + (1,) * (len(shape) - position - 1))

    gain = one(*split[0])
    for cut in split[1:]:
        gain = gain * one(*cut)
    return gain


def gaussian(stream_key, shape, width, reach, shards=(), dtype=jnp.bfloat16):
    factor_of = block_levels(stream_key, shape, shards, -0.22, 0.18) if shards else 1.0
    array = jax.random.normal(stream_key, shape, jnp.float32) * width * factor_of
    return jnp.minimum(jnp.maximum(array, -reach), reach).astype(dtype)


def setup_inputs(seed: int = 0) -> dict:
    keys = jax.random.split(jax.random.key(seed), 18)
    return {
        "inputs": gaussian(keys[0], (SEQS, LENGTH, D), 1.0, 6.0, ((0, 8), (1, 4))),
        "w_query": gaussian(keys[1], (D, D), D ** -0.5, 0.1875, ((0, 8),)),
        "w_key": gaussian(keys[2], (D, D), D ** -0.5, 0.1875, ((0, 8),)),
        "w_value": gaussian(keys[3], (D, D), D ** -0.5, 0.1875, ((0, 8),)),
        "b_query": gaussian(keys[4], (D,), 0.3, 4.0, ((0, 8),)),
        "b_value": gaussian(keys[5], (D,), 0.05, 0.75, ((0, 8),)),
        "w_out": gaussian(keys[6], (D, D), (max(1, 3 * D // LENGTH)) ** -0.5, 2.5, ((0, 8),)),
        "b_out": gaussian(keys[7], (D,), 0.3, 4.0, ((0, 8),)),
        "gain_one": jnp.clip(1.0 + 0.1 * jax.random.normal(keys[8], (D,), jnp.float32), 0.5, 1.5).astype(jnp.bfloat16),
        "shift_one": gaussian(keys[9], (D,), 0.3, 4.0, ((0, 8),)),
        "w_up": gaussian(keys[10], (D, FF), D ** -0.5, 0.1875, ((0, 8),)),
        "b_up": gaussian(keys[11], (FF,), 0.5, 6.0, ((0, 8),)),
        "w_down": gaussian(keys[12], (FF, D), FF ** -0.5, 0.09375, ((0, 8),)),
        "b_down": gaussian(keys[13], (D,), 0.3, 4.0, ((0, 8),)),
        "gain_two": jnp.clip(1.0 + 0.1 * jax.random.normal(keys[14], (D,), jnp.float32), 0.5, 1.5).astype(jnp.bfloat16),
        "shift_two": gaussian(keys[15], (D,), 0.3, 4.0, ((0, 8),)),
        "cotangent": gaussian(keys[16], (SEQS, LENGTH, D), 1.0, 6.0, ((0, 8), (1, 4))),
    }


@jax.custom_vjp
def low(v):
    return lax.optimization_barrier(v.astype(jnp.bfloat16)).astype(jnp.float32)

@jax.custom_vjp
def low_back(v):
    return v

def low_keep(v):
    return (low(v), None)

def low_pass(kept, grad):
    return (grad,)

def back_keep(v):
    return (v, None)

def back_low(kept, grad):
    return (low(grad),)
low.defvjp(low_keep, low_pass)
low_back.defvjp(back_keep, back_low)
EPSILON = 1e-12
PRECISE = lax.Precision.HIGHEST

def product(former, latter):
    return jnp.dot(former, latter, precision=PRECISE)

def normalize(hidden, gain_vec, offset):
    center = hidden - lax.optimization_barrier(jnp.mean(hidden, -1, keepdims=True))
    spread = lax.optimization_barrier(jnp.mean(center * center, -1, keepdims=True))
    return center * lax.rsqrt(spread + EPSILON) * gain_vec + offset

def attend(triple):
    queries, key_rows, values = triple
    four_dims = (LENGTH, HEADS, HEAD_DIM)
    scores = jnp.einsum('qhd,khd->hqk', queries.reshape(four_dims), key_rows.reshape(four_dims), precision=PRECISE) * HEAD_DIM ** (-0.5)
    scores = low_back(scores)
    portions = low(jax.nn.softmax(scores, axis=-1))
    context = jnp.einsum('hqk,khd->qhd', portions, values.reshape(four_dims), precision=PRECISE)
    return context.reshape(LENGTH, D)

def one_layer(parameters, seq_block):
    w_query, w_key, w_value, b_query, b_value, w_out, b_out, gain_one, shift_one, w_up, b_up, w_down, b_down, gain_two, shift_two = parameters
    flat_rows = seq_block.reshape(-1, D)
    three_dims = (SEQS_GRP, LENGTH, D)
    queries = low(low_back(product(flat_rows, w_query) + b_query))
    key_rows = low(low_back(product(flat_rows, w_key)))
    values = low(low_back(product(flat_rows, w_value) + b_value))
    context = lax.map(jax.checkpoint(attend), (queries.reshape(three_dims), key_rows.reshape(three_dims), values.reshape(three_dims)))
    context = low(low_back(context.reshape(-1, D)))
    branch = low_back(product(context, w_out) + b_out)
    first_sum = flat_rows + branch
    normed = normalize(first_sum, gain_one, shift_one)
    pre_active = low_back(product(low(normed), w_up) + b_up)
    active = low(jax.nn.gelu(pre_active, approximate=False))
    second_sum = normed + low_back(product(active, w_down) + b_down)
    return normalize(second_sum, gain_two, shift_two).reshape(seq_block.shape)

def add_pair(former, latter):
    return former + latter

def reference(inputs, w_query, w_key, w_value, b_query, b_value, w_out, b_out, gain_one, shift_one, w_up, b_up, w_down, b_down, gain_two, shift_two, cotangent):
    parameters = tuple((tensor.astype(jnp.float32) for tensor in (w_query, w_key, w_value, b_query, b_value, w_out, b_out, gain_one, shift_one, w_up, b_up, w_down, b_down, gain_two, shift_two)))
    blocks_in = inputs.astype(jnp.float32).reshape(N_DP, SEQS_GRP, LENGTH, D)
    blocks_cot = cotangent.astype(jnp.float32).reshape(N_DP, SEQS_GRP, LENGTH, D)

    def scan_step(running, operands):
        seq_block, seq_cot = operands
        result, pullback = jax.vjp(one_layer, parameters, seq_block)
        grad_params, grad_block = pullback(seq_cot)
        running = jax.tree.map(add_pair, running, grad_params)
        return (running, (result, grad_block))
    initial = tuple((jnp.zeros_like(tensor) for tensor in parameters))
    running, (results, grad_blocks) = lax.scan(scan_step, initial, (blocks_in, blocks_cot))
    output = results.reshape(SEQS, LENGTH, D).astype(jnp.bfloat16)
    grad_inputs = grad_blocks.reshape(SEQS, LENGTH, D)
    return (output, grad_inputs, running[0], running[1], running[2], running[3], running[4], running[5], running[6], running[7], running[8], running[9], running[10], running[11], running[12], running[13], running[14])
```

```python
import functools

import jax
import jax.numpy as jnp
import numpy as np
from jax import lax
from jax.experimental import pallas as pl
from jax.experimental.pallas import tpu as pltpu
from jax.sharding import PartitionSpec as P

HEAD_DIM = 64
EPSILON = 1e-12
BOTH = ("dp", "seq")
PAD = 16
F32 = jnp.float32
BF16 = jnp.bfloat16


def dot(former, latter, former_dim=1, latter_dim=0):
    return lax.dot_general(
        former,
        latter,
        (((former_dim,), (latter_dim,)), ((), ())),
        preferred_element_type=F32,
    )


def normalize(hidden, gain_vec, offset):
    center = hidden - jnp.mean(hidden, -1, keepdims=True)
    spread = jnp.mean(center * center, -1, keepdims=True)
    root = lax.rsqrt(spread + EPSILON)
    unit = center * root
    return unit * gain_vec + offset, unit, root


def normalize_back(unit, root, gain_vec, upstream):
    scaled = upstream * gain_vec
    first = jnp.mean(scaled, -1, keepdims=True)
    second = jnp.mean(scaled * unit, -1, keepdims=True)
    return (
        root * (scaled - first - unit * second),
        jnp.sum(upstream * unit, 0),
        jnp.sum(upstream, 0),
    )


class Plan:
    def __init__(self, n_dp, n_seq):
        self.n_dp, self.n_seq, self.n_z = n_dp, n_seq, n_dp // 2
        self.bits = n_seq.bit_length() - 1
        order = [0] + list(range(1, self.n_z, 2))
        order += list(range(2, self.n_z, 2))[::-1]
        self.order = order
        self.place = [order.index(z) for z in range(self.n_z)]
        self.core = self.pairs(lambda z, c, s: (z, 1 - c, s))
        self.ring = self.pairs(lambda z, c, s: (self.behind(z, -1), c, s))
        self.stage = [
            self.pairs(lambda z, c, s, k=k: (z, c, s ^ self.mask(c, 1 << k)))
            for k in range(self.bits)
        ]
        rows = []
        for dp in range(n_dp):
            for s in range(n_seq):
                z, c = dp // 2, dp % 2
                rows.append(
                    [self.behind(z, j) for j in range(self.n_z)]
                    + [s ^ self.mask(c, r) for r in range(n_seq)]
                    + [c, 1 - c]
                    + [s ^ self.mask(1 - c, r) for r in range(n_seq)]
                )
        self.table = np.asarray(rows, np.int32)

    def behind(self, z, j):
        return self.order[(self.place[z] - j) % self.n_z]

    def mask(self, c, r):
        out = 0
        for k in range(self.bits):
            if r >> k & 1:
                out |= 1 << ((k + c) % self.bits)
        return out

    def pairs(self, target):
        out = []
        for dp in range(self.n_dp):
            for s in range(self.n_seq):
                z, c, t = target(dp // 2, dp % 2, s)
                out.append((dp * self.n_seq + s, (2 * z + c) * self.n_seq + t))
        return out

    def row(self):
        here = lax.axis_index("dp") * self.n_seq + lax.axis_index("seq")
        return lax.dynamic_index_in_dim(jnp.asarray(self.table), here, 0, False)

    def swap(self, block):
        return lax.ppermute(block, BOTH, self.core)

    def around(self, block):
        out = [block]
        for _ in range(self.n_z - 1):
            out.append(lax.ppermute(out[-1], BOTH, self.ring))
        return out

    def gather(self, block):
        have = block[None]
        for k in range(self.bits):
            have = jnp.concatenate([have, lax.ppermute(have, BOTH, self.stage[k])], 0)
        return have

    def exchange(self, blocks):
        tail = blocks.shape[1:]
        for k in range(self.bits):
            split = blocks.reshape((-1, 2, 1 << k) + tail)
            come = lax.ppermute(split[:, 1], BOTH, self.stage[k])
            blocks = jnp.stack([split[:, 0], come], 1).reshape((-1,) + tail)
        return blocks

    def scatter(self, blocks):
        for k in reversed(range(self.bits)):
            half = 1 << k
            come = lax.ppermute(blocks[half:], BOTH, self.stage[k])
            blocks = (blocks[:half].astype(F32) + come.astype(F32)).astype(BF16)
        return blocks[0]

    def ring_scatter(self, part):
        moving = part(1 % self.n_z)
        for j in range(2, self.n_z + 1):
            come = lax.ppermute(moving, BOTH, self.ring)
            moving = (part(j % self.n_z).astype(F32) + come.astype(F32)).astype(BF16)
        return moving


def assemble(table, pieces, moves, outs):
    def kernel(table_ref, *refs):
        sources, targets, sems = refs[: len(pieces)], refs[len(pieces) : -1], refs[-1]
        copies = []
        for n, (i, src, o, at) in enumerate(moves):
            copies.append(
                pltpu.make_async_copy(
                    sources[i].at[src], targets[o].at[at(table_ref)], sems.at[n]
                )
            )
        for copy in copies:
            copy.start()
        for copy in copies:
            copy.wait()

    size = sum(int(np.prod(o.shape)) * o.dtype.itemsize for o in outs)
    return pl.pallas_call(
        kernel,
        out_shape=outs,
        in_specs=[pl.BlockSpec(memory_space=pltpu.SMEM)]
        + [pl.BlockSpec(memory_space=pl.ANY)] * len(pieces),
        out_specs=[pl.BlockSpec(memory_space=pltpu.VMEM)] * len(outs),
        scratch_shapes=[pltpu.SemaphoreType.DMA((len(moves),))],
        cost_estimate=pl.CostEstimate(
            flops=0, bytes_accessed=2 * size, transcendentals=0
        ),
    )(table, *pieces)


def at_rows(start, size):
    return pl.ds(pl.multiple_of(start, size), size)


def attend(query, key, value):
    scores = jnp.einsum("ghqd,ghkd->ghqk", query, key, preferred_element_type=F32)
    scores = scores * HEAD_DIM**-0.5
    row_max = jnp.max(scores, -1, keepdims=True)
    exponent = jnp.exp(scores - row_max)
    row_total = jnp.sum(exponent, -1, keepdims=True)
    portions = (exponent / row_total).astype(BF16)
    context = jnp.einsum("ghqk,ghkd->ghqd", portions, value, preferred_element_type=F32)
    return context.astype(BF16), row_max + jnp.log(row_total)


def attend_back(query, key, value, log_total, upstream):
    factor = HEAD_DIM**-0.5
    scores = jnp.einsum("ghqd,ghkd->ghqk", query, key, preferred_element_type=F32)
    portions = jnp.exp(scores * factor - log_total)
    low = portions.astype(BF16)
    grad_value = jnp.einsum("ghqk,ghqd->ghkd", low, upstream, preferred_element_type=F32)
    grad = jnp.einsum("ghqd,ghkd->ghqk", upstream, value, preferred_element_type=F32)
    grad = portions * (grad - jnp.sum(portions * grad, -1, keepdims=True))
    grad = grad.astype(BF16)
    grad_query = jnp.einsum("ghqk,ghkd->ghqd", grad, key, preferred_element_type=F32)
    grad_key = jnp.einsum("ghqk,ghqd->ghkd", grad, query, preferred_element_type=F32)
    return (
        (grad_query * factor).astype(BF16),
        (grad_key * factor).astype(BF16),
        grad_value.astype(BF16),
    )


def local(
    plan,
    inputs,
    w_query,
    w_key,
    w_value,
    b_query,
    b_value,
    w_out,
    b_out,
    gain_one,
    shift_one,
    w_up,
    b_up,
    w_down,
    b_down,
    gain_two,
    shift_two,
    cotangent,
):
    n_dp, n_seq, n_z = plan.n_dp, plan.n_seq, plan.n_z
    seqs, length, width = inputs.shape
    tokens = seqs * length
    own_rows, hidden = w_up.shape
    own_hidden = w_down.shape[0]
    half = hidden // 2
    cols = width // n_seq
    quarter = half // n_seq
    heads = cols // HEAD_DIM
    table = plan.row()
    behind = [table[j] for j in range(n_z)]
    member = [table[n_z + r] for r in range(n_seq)]
    core, other = table[n_z + n_seq], table[n_z + n_seq + 1]
    seq = member[0]
    BEHIND, MEMBER, CORE = 0, n_z, n_z + n_seq
    MEMBERS = (MEMBER, CORE + 2)

    all_inputs = plan.gather(inputs).reshape(n_seq * tokens, width)

    def own_cols(w):
        return lax.dynamic_slice_in_dim(w, seq * cols, cols, 1)

    vectors = jnp.concatenate(
        [b_query, b_value, b_out, gain_one, shift_one, b_down, gain_two, shift_two, b_up]
    )
    vec_rows = -(-vectors.shape[0] // (3 * cols))
    vectors = jnp.pad(vectors, (0, PAD * 3 * cols - vectors.shape[0]))
    first = jnp.concatenate(
        [
            jnp.concatenate([own_cols(w_query), own_cols(w_key), own_cols(w_value)], 1),
            vectors.reshape(PAD, 3 * cols),
        ],
        0,
    )
    mine = jnp.stack(plan.around(first))
    theirs = plan.swap(mine)
    moves = []
    for i in range(2):
        for j in range(n_z):
            moves.append(
                (
                    i,
                    (j, pl.ds(0, own_rows)),
                    0,
                    lambda t, i=i, j=j: (
                        at_rows((t[BEHIND + j] * 2 + t[CORE + i]) * own_rows, own_rows),
                    ),
                )
            )
            moves.append(
                (
                    i,
                    (j, pl.ds(own_rows, PAD)),
                    1,
                    lambda t, i=i, j=j: (
                        at_rows((t[BEHIND + j] * 2 + t[CORE + i]) * PAD, PAD),
                    ),
                )
            )
    w_qkv, vec = assemble(
        table,
        [mine, theirs],
        moves,
        [
            jax.ShapeDtypeStruct((width, 3 * cols), BF16),
            jax.ShapeDtypeStruct((n_dp * PAD, 3 * cols), BF16),
        ],
    )
    vec = vec.reshape(n_dp, PAD, 3 * cols)[:, :vec_rows].reshape(n_dp, -1)
    vec = vec.astype(F32)
    narrow = vec[:, : 8 * own_rows].reshape(n_dp, 8, own_rows)
    narrow = narrow.transpose(1, 0, 2).reshape(8, width)
    full_bq, full_bv, full_bo, full_g1, full_s1, full_bd, full_g2, full_s2 = narrow
    full_bu = vec[:, 8 * own_rows : 8 * own_rows + own_hidden].reshape(n_z, 2, own_hidden)
    half_bu = lax.dynamic_index_in_dim(full_bu, core, 1, False).reshape(half)

    def halves(w):
        parts = w.reshape(own_rows, n_z, 2, own_hidden)
        return [
            lax.dynamic_index_in_dim(parts, c, 2, False).reshape(own_rows, half)
            for c in (core, other)
        ]

    up_mine, up_theirs = halves(w_up)
    across = plan.swap(jnp.concatenate([up_theirs, w_out], 1))
    up_come, out_come = across[:, :half], across[:, half:]
    up_quarter = jnp.concatenate(
        [
            lax.dynamic_slice_in_dim(up_mine, seq * quarter, quarter, 1),
            lax.dynamic_slice_in_dim(up_come, seq * quarter, quarter, 1),
        ],
        0,
    )
    out_cols = own_cols(w_out)
    fold = own_rows // 2
    out_fold = jnp.concatenate([out_cols[:fold], out_cols[fold:]], 1)
    up_ring = plan.around(jnp.concatenate([up_quarter, out_fold], 0))
    up_all = plan.gather(jnp.stack(up_ring[1:]))
    out_all = plan.swap(up_all[:, :, 2 * own_rows :])
    pieces = [up_mine, up_come, up_all]
    moves = []
    whole = pl.ds(0, own_rows)
    for k in range(2):
        moves.append(
            (
                k,
                (whole,),
                0,
                lambda t, k=k: (
                    at_rows((t[BEHIND] * 2 + t[CORE + k]) * own_rows, own_rows),
                ),
            )
        )
        for j in range(1, n_z):
            for r in range(n_seq):
                moves.append(
                    (
                        2,
                        (r, j - 1, pl.ds(k * own_rows, own_rows)),
                        0,
                        lambda t, k=k, j=j, r=r: (
                            at_rows((t[BEHIND + j] * 2 + t[CORE + k]) * own_rows, own_rows),
                            at_rows(t[MEMBER + r] * quarter, quarter),
                        ),
                    )
                )
    (half_up,) = assemble(table, pieces, moves, [jax.ShapeDtypeStruct((width, half), BF16)])
    pieces = [w_out, out_come, up_all, out_all]
    moves = []
    for k in range(2):
        moves.append(
            (
                k,
                (whole,),
                0,
                lambda t, k=k: (
                    at_rows((t[BEHIND] * 2 + t[CORE + k]) * own_rows, own_rows),
                ),
            )
        )
        for j in range(1, n_z):
            for r in range(n_seq):
                for f in range(2):
                    moves.append(
                        (
                            2 + k,
                            (
                                r,
                                j - 1,
                                pl.ds(2 * own_rows * (1 - k), fold),
                                pl.ds(f * cols, cols),
                            ),
                            0,
                            lambda t, k=k, j=j, r=r, f=f: (
                                at_rows(
                                    (t[BEHIND + j] * 2 + t[CORE + k]) * own_rows + f * fold,
                                    fold,
                                ),
                                at_rows(t[MEMBERS[k] + r] * cols, cols),
                            ),
                        )
                    )
    (full_out,) = assemble(table, pieces, moves, [jax.ShapeDtypeStruct((width, width), BF16)])

    slab = own_hidden // n_seq
    down_ring = plan.around(lax.dynamic_slice_in_dim(w_down, seq * slab, slab, 0))
    down_all = plan.gather(jnp.stack(down_ring[1:]))
    moves = [(0, (pl.ds(0, own_hidden),), 0, lambda t: (at_rows(t[BEHIND] * own_hidden, own_hidden),))]
    for j in range(1, n_z):
        for r in range(n_seq):
            moves.append(
                (
                    1,
                    (r, j - 1),
                    0,
                    lambda t, j=j, r=r: (
                        at_rows(t[BEHIND + j] * own_hidden + t[MEMBER + r] * slab, slab),
                    ),
                )
            )
    (half_down,) = assemble(
        table, [w_down, down_all], moves, [jax.ShapeDtypeStruct((half, width), BF16)]
    )

    own_bias = jnp.concatenate(
        [
            lax.dynamic_slice_in_dim(full_bq, seq * cols, cols),
            jnp.zeros((cols,), F32),
            lax.dynamic_slice_in_dim(full_bv, seq * cols, cols),
        ]
    )
    qkv = (dot(all_inputs, w_qkv) + own_bias).astype(BF16)
    qkv = qkv.reshape(n_seq, seqs, length, 3, heads, HEAD_DIM).transpose(3, 1, 4, 0, 2, 5)
    qkv = qkv.reshape(3, seqs, heads, n_seq * length, HEAD_DIM)
    query, key, value = qkv[0], qkv[1], qkv[2]

    def to_rows(v):
        v = v.reshape(seqs, heads, n_seq, length, HEAD_DIM)
        return v.transpose(2, 0, 3, 1, 4).reshape(n_seq, tokens, cols)

    def to_heads(v):
        v = v.reshape(n_seq, seqs, length, heads, HEAD_DIM).transpose(1, 3, 0, 2, 4)
        return v.reshape(seqs, heads, n_seq * length, HEAD_DIM)

    head_context, log_total = attend(query, key, value)
    come = plan.exchange(to_rows(head_context))
    moves = [
        (0, (r,), 0, lambda t, r=r: (pl.ds(0, tokens), at_rows(t[MEMBER + r] * cols, cols)))
        for r in range(n_seq)
    ]
    (context,) = assemble(table, [come], moves, [jax.ShapeDtypeStruct((tokens, width), BF16)])

    flat = inputs.reshape(tokens, width).astype(F32)
    first_sum = flat + (dot(context, full_out) + full_bo)
    normed, unit_one, root_one = normalize(first_sum, full_g1, full_s1)
    normed_low = normed.astype(BF16)
    both_low = jnp.concatenate([normed_low, plan.swap(normed_low)], 0)

    pre_active = dot(both_low, half_up) + half_bu
    phi = jnp.exp(-0.5 * pre_active * pre_active) * (1.0 / np.sqrt(2.0 * np.pi))
    big_phi = 0.5 * (1.0 + lax.erf(pre_active * np.float32(np.sqrt(0.5))))
    active = (pre_active * big_phi).astype(BF16)
    slope = (big_phi + pre_active * phi).astype(BF16)

    def join(partial):
        return partial[:tokens] + plan.swap(partial[tokens:].astype(BF16)).astype(F32)

    second_sum = normed + (join(dot(active, half_down)) + full_bd)
    result, unit_two, root_two = normalize(second_sum, full_g2, full_s2)
    output = result.astype(BF16).reshape(inputs.shape)

    upstream = cotangent.reshape(tokens, width).astype(F32)
    grad_second, grad_g2, grad_s2 = normalize_back(unit_two, root_two, full_g2, upstream)
    branch_two = grad_second.astype(BF16)
    grad_bd = jnp.sum(branch_two.astype(F32), 0)
    both_two = jnp.concatenate([branch_two, plan.swap(branch_two)], 0)
    grad_pre = (dot(both_two, half_down, 1, 1) * slope.astype(F32)).astype(BF16)

    def pick(array, ids, axis):
        return jnp.stack([lax.dynamic_index_in_dim(array, i, axis, False) for i in ids])

    grad_down = dot(active, both_two, 0, 0).astype(BF16)
    grad_down = pick(grad_down.reshape(n_z, n_seq, slab, width), member, 1)
    grad_up = dot(both_low, grad_pre, 0, 0).astype(BF16)
    grad_up = pick(grad_up.reshape(n_z, 2 * own_rows, n_seq, quarter), member, 2)
    grad_down = plan.scatter(grad_down)
    grad_up = plan.scatter(grad_up)
    grad_bu = jnp.sum(grad_pre.astype(F32), 0)

    grad_normed = grad_second + join(dot(grad_pre, half_up, 1, 1))
    grad_first, grad_g1, grad_s1 = normalize_back(unit_one, root_one, full_g1, grad_normed)
    branch_one = grad_first.astype(BF16)
    grad_bo = jnp.sum(branch_one.astype(F32), 0)
    grad_context = dot(branch_one, full_out, 1, 1).astype(BF16)
    head_grad = to_heads(plan.exchange(pick(grad_context.reshape(tokens, n_seq, cols), member, 1)))

    grad_out = dot(context, branch_one, 0, 0).astype(BF16).reshape(n_z, 2, own_rows, width)
    keep = lax.dynamic_index_in_dim(grad_out, core, 1, False)
    come = plan.swap(lax.dynamic_index_in_dim(grad_out, other, 1, False))
    grad_out = (keep.astype(F32) + come.astype(F32)).astype(BF16)
    grad_out = plan.scatter(pick(grad_out.reshape(n_z, own_rows, n_seq, cols), member, 2))
    grad_out = jnp.concatenate([grad_out[:, :fold], grad_out[:, fold:]], 2)

    def rows_of(array):
        return lambda j: lax.dynamic_index_in_dim(array, behind[j], 0, False)

    grad_down = plan.ring_scatter(rows_of(grad_down))
    grad_down = plan.gather(grad_down)
    moves = [
        (0, (r,), 0, lambda t, r=r: (at_rows(t[MEMBER + r] * slab, slab),)) for r in range(n_seq)
    ]
    (grad_down,) = assemble(
        table, [grad_down], moves, [jax.ShapeDtypeStruct((own_hidden, width), BF16)]
    )
    grad_up = plan.ring_scatter(rows_of(jnp.concatenate([grad_up, grad_out], 1)))
    grad_out, grad_up = grad_up[2 * own_rows :], grad_up[: 2 * own_rows]
    grad_up = grad_up.reshape(2, own_rows, quarter)
    come = plan.swap(lax.dynamic_index_in_dim(grad_up, other, 0, False))
    keep = lax.dynamic_index_in_dim(grad_up, core, 0, False)
    grad_up = plan.gather(jnp.concatenate([keep, come, grad_out], 0))
    moves = []
    for r in range(n_seq):
        for k in range(2):
            for part in range(max(1, quarter // own_hidden)):
                moves.append(
                    (
                        0,
                        (r, pl.ds(k * own_rows, own_rows), pl.ds(part * own_hidden, own_hidden)),
                        0,
                        lambda t, r=r, k=k, part=part: (
                            pl.ds(0, own_rows),
                            at_rows(
                                (
                                    (t[MEMBER + r] * (quarter // own_hidden) + part) * 2
                                    + t[CORE + k]
                                )
                                * own_hidden,
                                own_hidden,
                            ),
                        ),
                    )
                )
        for f in range(2):
            moves.append(
                (
                    0,
                    (r, pl.ds(2 * own_rows, fold), pl.ds(f * cols, cols)),
                    1,
                    lambda t, r=r, f=f: (
                        pl.ds(f * fold, fold),
                        at_rows(t[MEMBER + r] * cols, cols),
                    ),
                )
            )
    grad_up, grad_out = assemble(
        table,
        [grad_up],
        moves,
        [
            jax.ShapeDtypeStruct((own_rows, hidden), BF16),
            jax.ShapeDtypeStruct((own_rows, width), BF16),
        ],
    )

    grads = attend_back(query, key, value, log_total, head_grad)
    grad_qkv = jnp.concatenate([to_rows(g) for g in grads], 2).reshape(n_seq * tokens, 3 * cols)
    partial = dot(grad_qkv, w_qkv, 1, 1).astype(BF16).reshape(n_seq, tokens, width)
    grad_inputs = grad_first + plan.scatter(partial).astype(F32)
    grad_w = dot(all_inputs, grad_qkv, 0, 0).astype(BF16)
    grad_b = jnp.sum(grad_qkv.astype(F32), 0)

    def widen(v):
        return lax.dynamic_update_slice_in_dim(jnp.zeros((width,), F32), v, seq * cols, 0)

    narrow = jnp.stack(
        [widen(grad_b[:cols]), widen(grad_b[2 * cols :]), grad_bo, grad_g1, grad_s1]
        + [grad_bd, grad_g2, grad_s2]
    )
    narrow = narrow.reshape(8, n_dp, own_rows).transpose(1, 0, 2).reshape(n_dp, 8 * own_rows)
    wide = jnp.zeros((n_z, 2, own_hidden), F32)
    wide = lax.dynamic_update_slice_in_dim(wide, grad_bu.reshape(n_z, 1, own_hidden), core, 1)
    vec = jnp.concatenate([narrow, wide.reshape(n_dp, own_hidden)], 1).astype(BF16)
    vec = jnp.pad(vec, ((0, 0), (0, PAD * 3 * cols - vec.shape[1])))
    last = jnp.concatenate(
        [
            grad_w.reshape(n_dp, own_rows, 3 * cols),
            vec.reshape(n_dp, PAD, 3 * cols),
        ],
        1,
    ).reshape(n_z, 2, own_rows + PAD, 3 * cols)
    come = plan.swap(lax.dynamic_index_in_dim(last, other, 1, False))
    keep = lax.dynamic_index_in_dim(last, core, 1, False)
    last = (keep.astype(F32) + come.astype(F32)).astype(BF16)
    last = plan.gather(plan.ring_scatter(rows_of(last)))
    moves = []
    for r in range(n_seq):
        for m in range(3):
            moves.append(
                (
                    0,
                    (r, pl.ds(0, own_rows), pl.ds(m * cols, cols)),
                    m,
                    lambda t, r=r: (pl.ds(0, own_rows), at_rows(t[MEMBER + r] * cols, cols)),
                )
            )
    grad_wq, grad_wk, grad_wv = assemble(
        table, [last], moves, [jax.ShapeDtypeStruct((own_rows, width), BF16)] * 3
    )
    vec = jnp.sum(last[:, own_rows : own_rows + vec_rows].astype(F32), 0).reshape(-1)
    small = vec[: 8 * own_rows].reshape(8, own_rows)
    return (
        output,
        grad_inputs.reshape(inputs.shape),
        grad_wq.astype(F32),
        grad_wk.astype(F32),
        grad_wv.astype(F32),
        small[0],
        small[1],
        grad_out.astype(F32),
        small[2],
        small[3],
        small[4],
        grad_up.astype(F32),
        vec[8 * own_rows : 8 * own_rows + own_hidden],
        grad_down.astype(F32),
        small[5],
        small[6],
        small[7],
    )


def solution(mesh):
    plan = Plan(mesh.shape["dp"], mesh.shape["seq"])
    rows, vector, token = P("dp", None), P("dp"), P("dp", "seq", None)
    weights = (rows,) * 3 + (vector,) * 2 + (rows,) + (vector,) * 3
    weights += (rows, vector, rows) + (vector,) * 3
    return jax.shard_map(
        functools.partial(local, plan),
        mesh=mesh,
        in_specs=(token,) + weights + (token,),
        out_specs=(token, token) + weights,
        check_vma=False,
    )
```

```python
import functools

import jax
import jax.numpy as jnp
import numpy as np
from jax import lax
from jax.experimental import pallas as pl
from jax.experimental.pallas import tpu as pltpu
from jax.sharding import PartitionSpec as P

HEAD_DIM = 64
PAIR = 2 * HEAD_DIM
EPSILON = 1e-12
BOTH = ("dp", "seq")
PAD = 16
MICROSECOND = 1_100_000_000
F32 = jnp.float32
BF16 = jnp.bfloat16
ANY = pl.BlockSpec(memory_space=pl.ANY)


def dot(former, latter, former_dim=1, latter_dim=0):
    return lax.dot_general(
        former,
        latter,
        (((former_dim,), (latter_dim,)), ((), ())),
        preferred_element_type=F32,
    )


class Plan:
    def __init__(self, n_dp, n_seq):
        self.n_dp, self.n_seq, self.n_z = n_dp, n_seq, n_dp // 2
        self.bits = n_seq.bit_length() - 1
        order = [0] + list(range(1, self.n_z, 2))
        order += list(range(2, self.n_z, 2))[::-1]
        self.order = order
        self.place = [order.index(z) for z in range(self.n_z)]
        self.core = self.pairs(lambda z, c, s: (z, 1 - c, s))
        self.toward = [
            self.pairs(lambda z, c, s, j=j: (self.behind(z, -j), c, s))
            for j in range(self.n_z)
        ]
        self.across = [
            self.pairs(lambda z, c, s, r=r: (z, c, s ^ self.mask(c, r)))
            for r in range(n_seq)
        ]
        self.stage = [
            self.pairs(lambda z, c, s, k=k: (z, c, s ^ self.mask(c, 1 << k)))
            for k in range(self.bits)
        ]
        rows = []
        for dp in range(n_dp):
            for s in range(n_seq):
                z, c = dp // 2, dp % 2
                rows.append(
                    [self.behind(z, j) for j in range(self.n_z)]
                    + [s ^ self.mask(c, r) for r in range(n_seq)]
                    + [c, 1 - c]
                    + [s ^ self.mask(1 - c, r) for r in range(n_seq)]
                )
        self.table = np.asarray(rows, np.int32)
        self.BEHIND, self.MEMBER = 0, self.n_z
        self.CORE = self.n_z + n_seq
        self.MEMBERS = (self.MEMBER, self.CORE + 2)

    def behind(self, z, j):
        return self.order[(self.place[z] - j) % self.n_z]

    def mask(self, c, r):
        out = 0
        for k in range(self.bits):
            if r >> k & 1:
                out |= 1 << ((k + c) % self.bits)
        return out

    def pairs(self, target):
        out = []
        for dp in range(self.n_dp):
            for s in range(self.n_seq):
                z, c, t = target(dp // 2, dp % 2, s)
                out.append((dp * self.n_seq + s, (2 * z + c) * self.n_seq + t))
        return out

    def row(self):
        here = lax.axis_index("dp") * self.n_seq + lax.axis_index("seq")
        return lax.dynamic_index_in_dim(jnp.asarray(self.table), here, 0, False)

    def swap(self, block):
        return lax.ppermute(block, BOTH, self.core)

    def share(self, block):
        return [block] + [lax.ppermute(block, BOTH, way) for way in self.across[1:]]

    def trade(self, blocks):
        return [blocks[0]] + [
            lax.ppermute(block, BOTH, way) for block, way in zip(blocks[1:], self.across[1:])
        ]

    def gather(self, block):
        near = block[None]
        for k in range(self.bits - 1):
            near = self.double(near, k)
        return near, lax.ppermute(near, BOTH, self.stage[self.bits - 1])

    def double(self, near, k):
        return jnp.concatenate([near, lax.ppermute(near, BOTH, self.stage[k])], 0)


def add(former, latter):
    return (former.astype(F32) + latter.astype(F32)).astype(BF16)


def after(value, *others):
    return lax.optimization_barrier((value,) + others)[0]


def shape(dims, dtype=BF16):
    return jax.ShapeDtypeStruct(tuple(dims), dtype)


def aligned(start, size):
    return pl.ds(pl.multiple_of(start, size), size)


def whole_block(dims):
    return pl.BlockSpec(tuple(dims), lambda *_: (0,) * len(dims))


def call(
    kernel, table, operands, in_specs, outs, out_specs, grid, scratch, micros, name, alias=None
):
    size = sum(int(np.prod(o.shape)) * o.dtype.itemsize for o in list(operands) + list(outs))
    return pl.pallas_call(
        kernel,
        out_shape=list(outs),
        grid_spec=pltpu.PrefetchScalarGridSpec(
            num_scalar_prefetch=1,
            grid=grid,
            in_specs=in_specs,
            out_specs=out_specs,
            scratch_shapes=scratch,
        ),
        cost_estimate=pl.CostEstimate(
            flops=micros * MICROSECOND, bytes_accessed=size, transcendentals=0
        ),
        input_output_aliases=alias or {},
        name=name,
    )(table, *operands)


def assemble(table, pieces, moves, outs, name):
    def kernel(table_ref, *refs):
        sources, targets, sems = refs[: len(pieces)], refs[len(pieces) : -1], refs[-1]
        copies = [
            pltpu.make_async_copy(
                sources[i].at[src(table_ref)], targets[o].at[at(table_ref)], sems.at[n]
            )
            for n, (i, src, o, at) in enumerate(moves)
        ]
        for copy in copies:
            copy.start()
        for copy in copies:
            copy.wait()

    return call(
        kernel,
        table,
        pieces,
        [ANY] * len(pieces),
        outs,
        [whole_block(o.shape) for o in outs],
        (1,),
        [pltpu.SemaphoreType.DMA((len(moves),))],
        2,
        name,
    )


def copies_of(moves, sems):
    return [pltpu.make_async_copy(src, at, sems.at[n]) for n, (src, at) in enumerate(moves)]


def lanes_of(half):
    lane = lax.broadcasted_iota(jnp.int32, (1, PAIR), 1)
    return lane < HEAD_DIM if half == 0 else lane >= HEAD_DIM


def only(block, half):
    return jnp.where(lanes_of(half), block, jnp.zeros_like(block))


def statistics(hidden):
    center = hidden - jnp.mean(hidden, -1, keepdims=True)
    spread = jnp.mean(center * center, -1, keepdims=True)
    root = lax.rsqrt(spread + EPSILON)
    return center * root, root


def norm_back(unit, root, gain_vec, upstream):
    scaled = upstream * gain_vec
    first = jnp.mean(scaled, -1, keepdims=True)
    second = jnp.mean(scaled * unit, -1, keepdims=True)
    return root * (scaled - first - unit * second)


def add_rows(target, row, value):
    target[row : row + 1, :] += jnp.sum(value, 0, keepdims=True)


def head_weights(plan, table, mine, theirs):
    n_z, n_dp = plan.n_z, plan.n_dp
    rows, lanes = mine.shape[1:]
    own_rows, cols3 = rows - PAD, lanes // 4 * 3
    width, span = n_dp * own_rows, lanes // 2

    def kernel(t, mine_ref, theirs_ref, w_ref, vec_ref, bias_ref, held, sems):
        moves = []
        for k, source in enumerate((mine_ref, theirs_ref)):
            for j in range(n_z):
                owner = 2 * t[plan.BEHIND + j] + t[plan.CORE + k]
                moves.append((source.at[j, pl.ds(own_rows, PAD)], held.at[owner]))
                moves.append(
                    (
                        source.at[j, pl.ds(0, own_rows), pl.ds(0, cols3)],
                        w_ref.at[aligned(owner * own_rows, own_rows)],
                    )
                )
        copies = copies_of(moves, sems)
        for copy in copies:
            copy.start()
        for copy in copies:
            copy.wait()
        for owner in range(n_dp):
            values = held[owner].astype(F32)
            at = pl.ds(owner * own_rows, own_rows)
            vec_ref[:, at] = values[:8, :own_rows]
            bias_ref[owner] = values[8:9, :span]

    outs = [shape((width, cols3)), shape((8, width), F32), shape((n_dp, 1, span), F32)]
    return call(
        kernel,
        table,
        [mine, theirs],
        [ANY] * 2,
        outs,
        [whole_block(o.shape) for o in outs],
        (1,),
        [pltpu.VMEM((n_dp, PAD, lanes), BF16), pltpu.SemaphoreType.DMA((4 * n_z,))],
        3,
        "head_weights",
    )


def attention_forward(plan, table, g, near, far, weights, vectors, before):
    n = plan.n_seq
    half, seqs, length, width = near.shape
    n_before = len(before)
    cols3 = weights.shape[1]
    cols = cols3 // 3
    total = n * length
    tile = 128
    scale = HEAD_DIM**-0.5

    def kernel(t, near_ref, far_ref, w_ref, vec_ref, *rest):
        qkv_ref, *parts, context = rest[n_before:]
        here = aligned(t[plan.MEMBER] * cols, cols)
        bias = jnp.concatenate(
            [vec_ref[0:1, here], jnp.zeros((1, cols), F32), vec_ref[1:2, here]], 1
        )
        for part, source in enumerate((near_ref, far_ref)):
            rows = source[...].reshape(half * length, width)
            out = dot(rows, w_ref[...]) + bias
            qkv_ref[part * half * length : (part + 1) * half * length, :] = out.astype(BF16)
        def each_pair(pair, carry):
            q_at = aligned(pair * PAIR, PAIR)
            key = qkv_ref[:, aligned(cols + pair * PAIR, PAIR)]
            value = qkv_ref[:, aligned(2 * cols + pair * PAIR, PAIR)]

            def each_tile(i, carry):
                rows = aligned(i * tile, tile)
                query = qkv_ref[rows, q_at] * jnp.asarray(scale, BF16)
                out = None
                for head in range(2):
                    scores = dot(only(query, head), key, 1, 1)
                    exponent = jnp.exp(scores - jnp.max(scores, -1, keepdims=True))
                    inverse = 1.0 / jnp.sum(exponent, -1, keepdims=True)
                    part = dot((exponent * inverse).astype(BF16), value)
                    out = part if head == 0 else jnp.where(lanes_of(0), out, part)
                context[rows, q_at] = out.astype(BF16)
                return carry

            lax.fori_loop(0, total // tile, each_tile, 0)
            return carry

        lax.fori_loop(0, cols // PAIR, each_pair, 0)
        for r in range(n):
            parts[r][0] = context[r * length : (r + 1) * length, :]

    block = pl.BlockSpec((half, 1, length, width), lambda i, t: (0, g, 0, 0))
    return call(
        kernel,
        table,
        [near, far, weights, vectors] + before,
        [block, block, whole_block(weights.shape), whole_block(vectors.shape)]
        + [ANY] * n_before,
        [shape((total, cols3))] + [shape((seqs, length, cols))] * n,
        [whole_block((total, cols3))]
        + [pl.BlockSpec((1, length, cols), lambda i, t: (g, 0, 0))] * n,
        (1,),
        [pltpu.VMEM((total, cols), BF16)],
        11,
        "attention_forward",
        {5 + i: 1 + i for i in range(n_before)},
    )


def attention_backward(plan, table, g, seqs, qkv, upstream, w_qkv, before):
    n = plan.n_seq
    half = n // 2
    width, cols3 = w_qkv.shape
    cols = cols3 // 3
    total = qkv.shape[0]
    length = total // n
    tile = min(256, total)
    scale = HEAD_DIM**-0.5
    n_before = len(before)

    def kernel(t, qkv_ref, w_ref, *rest):
        up_refs, rest = rest[:n], rest[n + n_before :]
        grad_ref, part_keep, part_send = rest[:3]
        up, key_acc, value_acc = rest[3:]
        for r in range(n):
            up[r * length : (r + 1) * length, :] = up_refs[r][0]
        def each_pair(pair, carry):
            q_at = aligned(pair * PAIR, PAIR)
            k_at = aligned(cols + pair * PAIR, PAIR)
            v_at = aligned(2 * cols + pair * PAIR, PAIR)
            value_acc[...] = jnp.zeros_like(value_acc)
            key_acc[...] = jnp.zeros_like(key_acc)

            def each_tile(i, carry):
                rows = aligned(i * tile, tile)
                query = qkv_ref[rows, q_at] * jnp.asarray(scale, BF16)
                above = up[rows, q_at]
                grad_query = None
                for head in range(2):
                    key = only(qkv_ref[:, k_at], head)
                    value = only(qkv_ref[:, v_at], head)
                    scores = dot(key, query, 1, 1)
                    exponent = jnp.exp(scores - jnp.max(scores, 0, keepdims=True))
                    portions = exponent * (1.0 / jnp.sum(exponent, 0, keepdims=True))
                    low = portions.astype(BF16)
                    slope = dot(value, above, 1, 1)
                    total_slope = jnp.sum(portions * slope, 0, keepdims=True)
                    slope = (portions * (slope - total_slope)).astype(BF16)
                    value_acc[...] += dot(low, only(above, head))
                    key_acc[...] += dot(slope, only(query, head))
                    q_part = dot(slope, key, 0, 0)
                    grad_query = q_part if head == 0 else grad_query + q_part
                grad_ref[0, rows, q_at] = (grad_query * scale).astype(BF16)
                return carry

            lax.fori_loop(0, total // tile, each_tile, 0)
            grad_ref[0, :, k_at] = key_acc[...].astype(BF16)
            grad_ref[0, :, v_at] = value_acc[...].astype(BF16)
            return carry

        lax.fori_loop(0, cols // PAIR, each_pair, 0)
        for r in range(n):
            target = part_keep if r < half else part_send
            rows = grad_ref[0, r * length : (r + 1) * length, :]
            target[r % half, 0] = dot(rows, w_ref[...], 1, 1).astype(BF16)

    part = (half, seqs, length, width)
    outs = [shape((seqs, total, cols3)), shape(part), shape(part)]
    block = pl.BlockSpec((half, 1, length, width), lambda i, t: (0, g, 0, 0))
    operands = [qkv, w_qkv] + upstream + before
    first = 1 + len(operands) - n_before
    return call(
        kernel,
        table,
        operands,
        [whole_block(qkv.shape), whole_block(w_qkv.shape)]
        + [pl.BlockSpec((1, length, cols), lambda i, t: (g, 0, 0))] * n
        + [ANY] * n_before,
        outs,
        [pl.BlockSpec((1, total, cols3), lambda i, t: (g, 0, 0)), block, block],
        (1,),
        [
            pltpu.VMEM((total, cols), BF16),
            pltpu.VMEM((total, PAIR), F32),
            pltpu.VMEM((total, PAIR), F32),
        ],
        11,
        "attention_backward",
        {first + i: i for i in range(n_before)},
    )


def head_weights_backward(plan, table, near, far, grad, narrow, wide):
    n, n_z = plan.n_seq, plan.n_z
    half, seqs, length, width = near.shape
    cols3 = grad.shape[2]
    own_rows = width // plan.n_dp
    total = n * length
    span = wide.shape[2]

    def kernel(t, near_ref, far_ref, grad_ref, narrow_ref, wide_ref, *rest):
        w_keep, w_send, w_acc, b_acc = rest
        step_id = pl.program_id(0)

        @pl.when(step_id == 0)
        def _():
            w_acc[...] = jnp.zeros_like(w_acc)
            b_acc[...] = jnp.zeros_like(b_acc)

        for part, source in enumerate((near_ref, far_ref)):
            rows = source[...].reshape(half * length, width)
            these = grad_ref[0, part * half * length : (part + 1) * half * length, :]
            w_acc[...] += dot(rows, these, 0, 0)
        b_acc[0:1, :] += jnp.sum(grad_ref[0].astype(F32), 0, keepdims=True)

        @pl.when(step_id == seqs - 1)
        def _():
            for target, k in ((w_keep, 0), (w_send, 1)):
                for z in range(n_z):
                    row = (2 * z + t[plan.CORE + k]) * own_rows
                    target[z, :own_rows, :] = w_acc[aligned(row, own_rows), :].astype(BF16)
                    here = (t[plan.MEMBER] == z).astype(F32)
                    last = lax.broadcasted_iota(jnp.int32, (8, cols3), 0) == 7
                    rows = jnp.where(
                        last, b_acc[0:1, :] * here, narrow_ref[2 * z + t[plan.CORE + k]]
                    )
                    target[z, own_rows : own_rows + 8, :] = rows.astype(BF16)
                    target[z, own_rows + 8 :, :] = jnp.zeros((PAD - 8, cols3), BF16)
                if k == 0:
                    for r in range(n):
                        rows = wide_ref[r].astype(BF16)
                        target[t[plan.MEMBER + r], own_rows + 8 :, :span] = rows

    block = pl.BlockSpec((half, 1, length, width), lambda g, t: (0, g, 0, 0))
    w_out = (n_z, own_rows + PAD, cols3)
    return call(
        kernel,
        table,
        [near, far, grad, narrow, wide],
        [
            block,
            block,
            pl.BlockSpec((1, total, cols3), lambda g, t: (g, 0, 0)),
            whole_block(narrow.shape),
            whole_block(wide.shape),
        ],
        [shape(w_out), shape(w_out)],
        [whole_block(w_out), whole_block(w_out)],
        (seqs,),
        [pltpu.VMEM((width, cols3), F32), pltpu.VMEM((8, cols3), F32)],
        8,
        "head_weights_backward",
    )


def output_norm(plan, table, pieces, inputs, vectors, w_out, come, near, far, others):
    n, n_z = plan.n_seq, plan.n_z
    half = n // 2
    tokens, width = inputs.shape
    own_rows = w_out.shape[0]
    cols = width // n
    tile = 128
    n_moves = 2 + 2 * (n_z - 1) * n

    def kernel(t, in_ref, vec_ref, w_ref, come_ref, near_ref, far_ref, on_ref, of_ref, *rest):
        refs, rest = rest[:n], rest[n:]
        sum_ref, norm_ref, low_ref, full_ref, sems = rest

        def row(z, k):
            return aligned((z * 2 + t[plan.CORE + k]) * own_rows, own_rows)

        moves = []
        for k, source in enumerate((w_ref, come_ref)):
            at = full_ref.at[row(t[plan.BEHIND], k)]
            lanes = source.shape[1] - width
            moves.append((source.at[pl.ds(0, own_rows), pl.ds(lanes, width)], at))
        for k, (first, second) in enumerate(((near_ref, far_ref), (on_ref, of_ref))):
            for j in range(1, n_z):
                for r in range(n):
                    source = first if r < half else second
                    at = full_ref.at[
                        row(t[plan.BEHIND + j], k),
                        aligned(t[plan.MEMBERS[k] + r] * cols, cols),
                    ]
                    moves.append((source.at[r % half, j - 1], at))
        copies = copies_of(moves, sems)
        for copy in copies:
            copy.start()
        for copy in copies:
            copy.wait()
        for i in range(tokens // tile):
            rows = pl.ds(i * tile, tile)
            total = in_ref[rows, :].astype(F32) + vec_ref[2:3, :]
            for r in range(n):
                weights = full_ref[aligned(t[plan.MEMBER + r] * cols, cols), :]
                total += dot(refs[r][rows, :], weights)
            unit, _ = statistics(total)
            normed = unit * vec_ref[3:4, :] + vec_ref[4:5, :]
            sum_ref[rows, :] = total
            norm_ref[rows, :] = normed
            low_ref[rows, :] = normed.astype(BF16)

    full = (tokens, width)
    return call(
        kernel,
        table,
        [inputs, vectors, w_out, come, near, far, *others, *pieces],
        [whole_block(full), whole_block(vectors.shape)]
        + [ANY] * 6
        + [whole_block(p.shape) for p in pieces],
        [shape(full, F32), shape(full, F32), shape(full), shape((width, width))],
        [whole_block(full)] * 3 + [whole_block((width, width))],
        (1,),
        [pltpu.SemaphoreType.DMA((n_moves,))],
        7,
        "output_norm",
    )


def flatten(remote):
    arrays, found = [], []
    for near, far in remote:
        found += [(len(arrays), i) for i in range(near.shape[1])]
        arrays += [near, far]
    return arrays, found


def gelu_parts(v):
    big = 0.5 + 0.5 * lax.erf(v * np.float32(np.sqrt(0.5)))
    small = jnp.exp(-0.5 * v * v) * np.float32(1.0 / np.sqrt(2.0 * np.pi))
    return v * big, big + v * small


def up_forward(plan, table, low, other_low, w_up, come, remote, bias):
    n, n_z = plan.n_seq, plan.n_z
    half = n // 2
    tokens, width = low.shape
    own_rows, hidden = w_up.shape
    quarter = hidden // 2 // n
    n_moves = 2 + n_z - 1
    tile = 128

    remote, found = flatten(remote)

    def kernel(t, low_ref, other_ref, up_ref, come_ref, bias_ref, *rest):
        remote_refs, rest = rest[: len(remote)], rest[len(remote) :]
        act_ref, slope_ref, w_hbm, w, sems, out_sem = rest
        step_id = pl.program_id(0)

        def moves(r):
            member = t[plan.MEMBER + r]
            z = t[plan.BEHIND]
            at = w.at[r]

            def row(k):
                return aligned((z * 2 + t[plan.CORE + k]) * own_rows, own_rows)

            lanes = aligned((member * 2 + t[plan.CORE]) * quarter, quarter)
            out = [(up_ref.at[:, lanes], at.at[row(0)])]
            lanes = aligned(member * quarter, quarter)
            out.append((come_ref.at[pl.ds(0, own_rows), lanes], at.at[row(1)]))
            for j in range(1, n_z):
                z_j = t[plan.BEHIND + j]
                a, i = found[j - 1]
                source = remote_refs[a + (r >= half)]
                for k in range(2):
                    rows = aligned((z_j * 2 + t[plan.CORE + k]) * own_rows, own_rows)
                    out.append(
                        (
                            source.at[r % half, i, pl.ds(k * own_rows, own_rows)],
                            at.at[rows],
                        )
                    )
            return out

        def copies(r):
            return copies_of(moves(r), sems.at[r])

        @pl.when(step_id == 0)
        def _():
            for r in range(n):
                for copy in copies(r):
                    copy.start()

        for r in range(n):

            @pl.when(step_id == r)
            def _(r=r):
                for copy in copies(r):
                    copy.wait()

        def out_copy(r):
            return pltpu.make_async_copy(w.at[r], w_hbm.at[r], out_sem.at[r])

        for r in range(n):

            @pl.when(step_id == r)
            def _(r=r):
                out_copy(r).start()

        weights = w.at[step_id]
        for part, source in enumerate((low_ref, other_ref)):

            def step(i, carry, part=part, source=source):
                rows = pl.ds(pl.multiple_of(i * tile, tile), tile)
                pre = dot(source[rows, :], weights[...]) + bias_ref[0]
                active, slope = gelu_parts(pre)
                rows = pl.ds(pl.multiple_of(part * tokens + i * tile, tile), tile)
                act_ref[0, rows, :] = active.astype(BF16)
                slope_ref[0, rows, :] = slope.astype(BF16)
                return carry

            lax.fori_loop(0, tokens // tile, step, 0)

        @pl.when(step_id == n - 1)
        def _():
            for r in range(n):
                out_copy(r).wait()

    big = (n, 2 * tokens, quarter)
    block = pl.BlockSpec((1, 2 * tokens, quarter), lambda r, t: (r, 0, 0))
    return call(
        kernel,
        table,
        [low, other_low, w_up, come, bias] + remote,
        [whole_block(low.shape)] * 2
        + [ANY] * 2
        + [
            pl.BlockSpec(
                (1, 1, quarter),
                lambda r, t: (2 * t[plan.MEMBER + r] + t[plan.CORE], 0, 0),
            )
        ]
        + [ANY] * len(remote),
        [shape(big), shape(big), shape((n, width, quarter))],
        [block, block, ANY],
        (n,),
        [
            pltpu.VMEM((n, width, quarter), BF16),
            pltpu.SemaphoreType.DMA((n, 2 + 2 * (n_z - 1))),
            pltpu.SemaphoreType.DMA((n,)),
        ],
        15,
        "up_forward",
    )


def down_forward(plan, table, active, w_down, remote):
    n, n_z = plan.n_seq, plan.n_z
    half = n // 2
    tokens = active.shape[1] // 2
    quarter = active.shape[2]
    own_hidden, width = w_down.shape
    cols = width // n

    remote, found = flatten(remote)

    def kernel(t, act_ref, down_ref, *rest):
        remote_refs, rest = rest[: len(remote)], rest[len(remote) :]
        own_ref, other_ref, w_hbm, w, acc, sems, out_sem = rest
        step_id = pl.program_id(0)
        out_copy = pltpu.make_async_copy(w, w_hbm, out_sem)

        @pl.when(step_id == 0)
        def _():
            moves = [
                (down_ref, w.at[aligned(t[plan.BEHIND] * own_hidden, own_hidden)])
            ]
            for j in range(1, n_z):
                rows = aligned(t[plan.BEHIND + j] * own_hidden, own_hidden)
                a, i = found[j - 1]
                for r in range(n):
                    source = remote_refs[a + (r >= half)]
                    lanes = aligned(t[plan.MEMBER + r] * cols, cols)
                    moves.append((source.at[r % half, i], w.at[rows, lanes]))
            copies = copies_of(moves, sems)
            for copy in copies:
                copy.start()
            acc[...] = jnp.zeros_like(acc)
            for copy in copies:
                copy.wait()
            out_copy.start()

        rows = aligned(t[plan.MEMBER + step_id] * quarter, quarter)
        acc[...] += dot(act_ref[0], w[rows, :])

        @pl.when(step_id == n - 1)
        def _():
            own_ref[...] = acc[:tokens, :]
            other_ref[...] = acc[tokens:, :].astype(BF16)
            out_copy.wait()

    full = (tokens, width)
    return call(
        kernel,
        table,
        [active, w_down] + remote,
        [pl.BlockSpec((1, 2 * tokens, quarter), lambda r, t: (r, 0, 0))]
        + [ANY] * (1 + len(remote)),
        [shape(full, F32), shape(full), shape((n * quarter, width))],
        [whole_block(full), whole_block(full), ANY],
        (n,),
        [
            pltpu.VMEM((n * quarter, width), BF16),
            pltpu.VMEM((2 * tokens, width), F32),
            pltpu.SemaphoreType.DMA((1 + (n_z - 1) * n,)),
            pltpu.SemaphoreType.DMA,
        ],
        10,
        "down_forward",
    )


def norm_two(table, normed, own, come, cotangent, vectors):
    tokens, width = normed.shape
    tile = 128

    def kernel(t, norm_ref, own_ref, come_ref, cot_ref, vec_ref, *rest):
        out_ref, grad_ref, low_ref, sums = rest

        @pl.when(pl.program_id(0) == 0)
        def _():
            sums[...] = jnp.zeros_like(sums)

        second = norm_ref[...] + (own_ref[...] + come_ref[...].astype(F32) + vec_ref[5:6, :])
        unit, root = statistics(second)
        gain = vec_ref[6:7, :]
        out_ref[...] = (unit * gain + vec_ref[7:8, :]).astype(BF16)
        above = cot_ref[...].astype(F32)
        grad = norm_back(unit, root, gain, above)
        low = grad.astype(BF16)
        grad_ref[...] = grad
        low_ref[...] = low
        add_rows(sums, 0, low.astype(F32))
        add_rows(sums, 1, above * unit)
        add_rows(sums, 2, above)

    block = pl.BlockSpec((tile, width), lambda i, t: (i, 0))
    full = (tokens, width)
    return call(
        kernel,
        table,
        [normed, own, come, cotangent, vectors],
        [block] * 4 + [whole_block(vectors.shape)],
        [shape(full), shape(full, F32), shape(full), shape((8, width), F32)],
        [block] * 3 + [whole_block((8, width))],
        (tokens // tile,),
        [],
        6,
        "norm_two",
    )


def ffn_backward(plan, table, low, other_low, w_down, w_up, slope):
    n = plan.n_seq
    tokens, width = low.shape
    quarter = slope.shape[2]

    def kernel(t, low_ref, other_ref, down_ref, up_ref, slope_ref, *rest):
        pre_ref, sum_ref, own_ref, come_ref, acc = rest
        step_id = pl.program_id(0)

        @pl.when(step_id == 0)
        def _():
            acc[...] = jnp.zeros_like(acc)

        sums = jnp.zeros((1, quarter), F32)
        for part, source in enumerate((low_ref, other_ref)):
            rows = pl.ds(part * tokens, tokens)
            grad = dot(source[...], down_ref[...], 1, 1) * slope_ref[0, rows, :].astype(F32)
            grad = grad.astype(BF16)
            pre_ref[0, rows, :] = grad
            sums += jnp.sum(grad.astype(F32), 0, keepdims=True)
            acc[rows, :] += dot(grad, up_ref[0], 1, 1)
        row = lax.broadcasted_iota(jnp.int32, (8, quarter), 0)
        sum_ref[0] = jnp.where(row == 0, sums, 0.0)

        @pl.when(step_id == n - 1)
        def _():
            own_ref[...] = acc[:tokens, :]
            come_ref[...] = acc[tokens:, :].astype(BF16)

    big = pl.BlockSpec((1, 2 * tokens, quarter), lambda r, t: (r, 0, 0))
    full = (tokens, width)
    return call(
        kernel,
        table,
        [low, other_low, w_down, w_up, slope],
        [whole_block(full)] * 2
        + [
            pl.BlockSpec((quarter, width), lambda r, t: (t[plan.MEMBER + r], 0)),
            pl.BlockSpec((1, width, quarter), lambda r, t: (r, 0, 0)),
            big,
        ],
        [shape(slope.shape), shape((n, 8, quarter), F32), shape(full, F32), shape(full)],
        [
            big,
            pl.BlockSpec((1, 8, quarter), lambda r, t: (r, 0, 0)),
            whole_block(full),
            whole_block(full),
        ],
        (n,),
        [pltpu.VMEM((2 * tokens, width), F32)],
        13,
        "ffn_backward",
    )


def down_weights(plan, table, active, low, other_low, base):
    n, n_z = plan.n_seq, plan.n_z
    half = n // 2
    tokens, width = low.shape
    quarter = active.shape[2]
    cols = width // n

    def kernel(t, act_ref, low_ref, other_ref, out_ref, grads):
        @pl.when(pl.program_id(0) == 0)
        def _():
            for r in range(half):
                lanes = aligned(t[plan.MEMBER + base + r] * cols, cols)
                here = pl.ds(r * cols, cols)
                grads[:tokens, here] = low_ref[:, lanes]
                grads[tokens:, here] = other_ref[:, lanes]

        total = dot(act_ref[0], grads[...], 0, 0)
        for r in range(half):
            out_ref[r, 0] = total[:, r * cols : (r + 1) * cols].astype(BF16)

    return call(
        kernel,
        table,
        [active, low, other_low],
        [pl.BlockSpec((1, 2 * tokens, quarter), lambda r, t: (r, 0, 0))]
        + [whole_block((tokens, width))] * 2,
        [shape((half, n_z, quarter, cols))],
        [
            pl.BlockSpec(
                (half, 1, quarter, cols), lambda r, t: (0, t[plan.MEMBER + r], 0, 0)
            )
        ],
        (n,),
        [pltpu.VMEM((2 * tokens, half * cols), BF16)],
        5,
        "down_weights",
    )[0]


def up_weights(plan, table, low, other_low, grad_pre, base):
    n, n_z = plan.n_seq, plan.n_z
    half = n // 2
    tokens, width = low.shape
    quarter = grad_pre.shape[2]
    own_rows = width // plan.n_dp

    def kernel(t, low_ref, other_ref, grad_ref, out_ref):
        for z in range(n_z):
            lanes = pl.ds(2 * z * own_rows, 2 * own_rows)
            total = dot(low_ref[:, lanes], grad_ref[0, :tokens, :], 0, 0)
            total += dot(other_ref[:, lanes], grad_ref[0, tokens:, :], 0, 0)
            total = total.astype(BF16)
            out_ref[0, z, :, :quarter] = total[:own_rows]
            out_ref[0, z, :, quarter:] = total[own_rows:]

    dims = (half, n_z, own_rows, 2 * quarter)
    return call(
        kernel,
        table,
        [low, other_low, grad_pre],
        [whole_block((tokens, width))] * 2
        + [pl.BlockSpec((1, 2 * tokens, quarter), lambda i, t: (base + i, 0, 0))],
        [shape(dims)],
        [pl.BlockSpec((1,) + dims[1:], lambda i, t: (i, 0, 0, 0))],
        (half,),
        [],
        6,
        "up_weights",
    )[0]


def norm_one_back(plan, table, grad_second, own, come, first_sum, vectors, w_out, sums_two):
    n = plan.n_seq
    tokens, width = own.shape
    cols = width // n
    tile = 128

    own_rows = width // plan.n_dp

    def kernel(t, grad_ref, own_ref, come_ref, sum_ref, vec_ref, w_ref, two_ref, *rest):
        first_ref, low_ref, narrow_ref = rest[:3]
        parts, sums = rest[3:-1], rest[-1]
        sums[0:3, :] = jnp.zeros((3, width), F32)
        sums[3:6, :] = two_ref[0:3, :]
        sums[6:8, :] = jnp.zeros((2, width), F32)
        for i in range(tokens // tile):
            rows = pl.ds(i * tile, tile)
            above = grad_ref[rows, :] + (own_ref[rows, :] + come_ref[rows, :].astype(F32))
            unit, root = statistics(sum_ref[rows, :])
            grad = norm_back(unit, root, vec_ref[3:4, :], above)
            low = grad.astype(BF16)
            first_ref[rows, :] = grad
            low_ref[rows, :] = low
            add_rows(sums, 0, low.astype(F32))
            add_rows(sums, 1, above * unit)
            add_rows(sums, 2, above)
            for r in range(n):
                weights = w_ref[aligned(t[plan.MEMBER + r] * cols, cols), :]
                parts[r][rows, :] = dot(low, weights, 1, 1).astype(BF16)
        narrow_ref[...] = jnp.zeros_like(narrow_ref)
        for owner in range(plan.n_dp):
            lanes = pl.ds(owner * own_rows, own_rows)
            narrow_ref[owner, :, 0:own_rows] = sums[:, lanes]

    full = (tokens, width)
    part = (tokens, cols)
    narrow = (plan.n_dp, 8, 3 * cols)
    return call(
        kernel,
        table,
        [grad_second, own, come, first_sum, vectors, w_out, sums_two],
        [whole_block(full)] * 4
        + [whole_block(v.shape) for v in (vectors, w_out, sums_two)],
        [shape(full, F32), shape(full), shape(narrow, F32)] + [shape(part)] * n,
        [whole_block(full)] * 2 + [whole_block(narrow)] + [whole_block(part)] * n,
        (1,),
        [pltpu.VMEM((8, width), F32)],
        8,
        "norm_one_back",
    )


def out_weights(plan, table, pieces, low):
    n, n_z = plan.n_seq, plan.n_z
    tokens, width = low.shape
    cols = width // n
    own_rows = width // plan.n_dp

    def kernel(t, low_ref, *rest):
        refs, (keep_ref, send_ref, both) = rest[:n], rest[n:]
        for r in range(n):
            z = t[plan.MEMBER + r]
            both[...] = dot(refs[r][...], low_ref[...], 0, 0).astype(BF16)
            for target, k in ((send_ref, 1), (keep_ref, 0)):
                rows = aligned(t[plan.CORE + k] * own_rows, own_rows)
                for s in range(n):
                    at = aligned(t[plan.MEMBERS[k] + s] * cols, cols)
                    target[s, z] = both[rows, at]

    dims = (n, n_z, own_rows, cols)
    return call(
        kernel,
        table,
        [low, *pieces],
        [whole_block(low.shape)] + [whole_block(p.shape) for p in pieces],
        [shape(dims), shape(dims)],
        [whole_block(dims)] * 2,
        (1,),
        [pltpu.VMEM((cols, width), BF16)],
        5,
        "out_weights",
    )


def parts_along_z(plan, table, keep, come):
    n_z = plan.n_z
    rows, lanes = keep.shape[1:]

    def kernel(t, keep_ref, come_ref, *outs):
        total = keep_ref[0].astype(F32) + come_ref[0].astype(F32)
        for j in range(n_z):

            @pl.when(pl.program_id(0) == j)
            def _(j=j):
                outs[j][...] = total.astype(BF16)

    def member(i, t):
        return (t[plan.BEHIND + (2 * n_z - 1 - i) % n_z], 0, 0)

    block = pl.BlockSpec((1, rows, lanes), member)
    return call(
        kernel,
        table,
        [keep, come],
        [block, block],
        [shape((rows, lanes))] * n_z,
        [whole_block((rows, lanes))] * n_z,
        (n_z,),
        [],
        2,
        "parts_along_z",
    )


def split_by_core(plan, table, pieces):
    rows, lanes = pieces[0].shape
    lanes //= 2
    n_pieces = len(pieces)

    def kernel(t, *refs):
        for target, k in zip(refs[n_pieces:], range(2)):
            at = aligned(t[plan.CORE + k] * lanes, lanes)
            total = refs[0][:, at].astype(F32)
            for ref in refs[1:n_pieces]:
                total += ref[:, at].astype(F32)
            target[...] = total.astype(BF16)

    return call(
        kernel,
        table,
        pieces,
        [whole_block(p.shape) for p in pieces],
        [shape((rows, lanes))] * 2,
        [whole_block((rows, lanes))] * 2,
        (1,),
        [],
        2,
        "split_by_core",
    )


def place(plan, table, pieces, outs, moves, name):
    n = plan.n_seq

    def kernel(t, *refs):
        sources, targets = refs[:n], refs[n:]
        for r in range(n):
            for src, o, at in moves:
                targets[o][:, at(t, r)] = sources[r][src].astype(F32)

    return call(
        kernel,
        table,
        pieces,
        [whole_block(p.shape) for p in pieces],
        [shape(o, F32) for o in outs],
        [whole_block(o) for o in outs],
        (1,),
        [],
        2,
        name,
    )


def local(
    plan,
    inputs,
    w_query,
    w_key,
    w_value,
    b_query,
    b_value,
    w_out,
    b_out,
    gain_one,
    shift_one,
    w_up,
    b_up,
    w_down,
    b_down,
    gain_two,
    shift_two,
    cotangent,
):
    n_dp, n, n_z = plan.n_dp, plan.n_seq, plan.n_z
    half = n // 2
    seqs, length, width = inputs.shape
    tokens = seqs * length
    own_rows, hidden = w_up.shape
    own_hidden = w_down.shape[0]
    cols = width // n
    cols3 = 3 * cols
    quarter = hidden // 2 // n
    assert n == n_z and quarter == own_hidden
    table = plan.row()
    core = lax.axis_index("dp") % 2

    narrow = jnp.stack(
        [b_query, b_value, b_out, gain_one, shift_one, b_down, gain_two, shift_two]
    )
    vec = jnp.concatenate(
        [
            jnp.pad(narrow, ((0, 0), (0, 4 * cols - own_rows))),
            jnp.pad(b_up[None], ((0, 7), (0, 4 * cols - own_hidden))),
        ],
        0,
    )

    def column_block(t):
        return (pl.ds(0, own_rows), aligned(t[plan.MEMBER] * cols, cols))

    moves = [
        (i, column_block, 0, lambda t, i=i: (pl.ds(0, own_rows), pl.ds(i * cols, cols)))
        for i in range(4)
    ]
    moves.append((4, lambda t: (pl.ds(0, PAD),), 0, lambda t: (pl.ds(own_rows, PAD),)))
    (first,) = assemble(
        table,
        [w_query, w_key, w_value, w_out, vec],
        moves,
        [shape((own_rows + PAD, 4 * cols))],
        "pack_first",
    )

    def straight(block, j):
        return lax.ppermute(block, BOTH, plan.toward[j])

    near_x = inputs[None]
    for k in range(plan.bits - 1):
        near_x = plan.double(near_x, k)
    mine = [first, straight(first, 1)]

    moves = []
    for z in range(n_z):
        moves.append(
            (
                0,
                lambda t, z=z: (
                    pl.ds(0, own_rows),
                    aligned((2 * z + t[plan.CORE + 1]) * quarter, quarter),
                ),
                0,
                lambda t, z=z: (pl.ds(0, own_rows), pl.ds(z * quarter, quarter)),
            )
        )
    moves.append(
        (
            1,
            lambda t: (pl.ds(0, own_rows),),
            0,
            lambda t: (pl.ds(0, own_rows), pl.ds(n * quarter, width)),
        )
    )
    (across,) = assemble(
        table,
        [after(w_up, mine[1]), w_out],
        moves,
        [shape((own_rows, n * quarter + width))],
        "pack_across",
    )
    come = plan.swap(across)

    top = plan.bits - 1

    def final(near, *ready):
        return near, lax.ppermute(after(near, *ready), BOTH, plan.stage[top])

    def begin(block, *ready):
        near = after(block, *ready)[None]
        for k in range(top - 1):
            near = plan.double(near, k)
        return near, lax.ppermute(near, BOTH, plan.stage[top - 1])

    def joined(started, *ready):
        return jnp.concatenate([after(started[0], *ready), started[1]], 0)

    def onward(block, *ready):
        return lax.ppermute(after(block, *ready), BOTH, plan.toward[1])

    ready = (near_x, mine[1])
    far_x = final(near_x, *ready)[1]
    mine += [straight(after(first, *ready), j) for j in range(2, n_z)]

    def rows_at(start, size):
        return lambda t: (pl.ds(start, size), pl.ds(0, quarter))

    moves = [
        (
            0,
            lambda t: (
                pl.ds(0, own_rows),
                aligned((2 * t[plan.MEMBER] + t[plan.CORE]) * quarter, quarter),
            ),
            0,
            rows_at(0, own_rows),
        ),
        (
            1,
            lambda t: (pl.ds(0, own_rows), aligned(t[plan.MEMBER] * quarter, quarter)),
            0,
            rows_at(own_rows, own_rows),
        ),
    ]
    moves.append(
        (
            2,
            lambda t: (pl.ds(0, own_hidden), aligned(t[plan.MEMBER] * cols, cols)),
            1,
            lambda t: (pl.ds(0, own_hidden),),
        )
    )
    second, down = assemble(
        table,
        [w_up, come, w_down],
        moves,
        [shape((2 * own_rows, quarter)), shape((own_hidden, cols))],
        "pack_second",
    )
    ups = [onward(second)]

    ready = (far_x, second) + tuple(mine[1:])
    mine_all = jnp.stack([after(piece, *ready) for piece in mine])
    theirs = plan.swap(mine_all)
    outs = jnp.stack([after(piece, *ready)[:own_rows, cols3:] for piece in mine[1:]])
    outs_started = begin(outs)
    ups.append(onward(ups[0], *ready))
    downs = [onward(down, *ready)]
    w_qkv, vectors, up_bias = head_weights(plan, table, mine_all, theirs)
    qkv = []

    def attend(g, before, *ready):
        out, *parts = attention_forward(
            plan, table, g, near_x, far_x, w_qkv, after(vectors, *ready), before
        )
        qkv.append(out)
        return parts

    parts = attend(0, [])

    near_out = joined(outs_started, parts[0])
    ready = (near_out, parts[0], ups[1], downs[0])
    outs = final(near_out, *ready)
    ups.append(onward(ups[1], *ready))
    downs.append(onward(downs[0], *ready))
    two_started = begin(jnp.stack([after(piece, *ready) for piece in ups[:2]]))
    parts = attend(1, parts, *ready)

    near_two = joined(two_started, parts[0])
    ready = (near_two, outs[1], ups[2], downs[1], parts[0])
    for j in range(3, n_z - 1):
        ups.append(onward(ups[-1]))
        downs.append(onward(downs[-1]))
    others = [plan.swap(after(part, *ready)) for part in outs]
    up_two = final(near_two, *ready)
    downs.append(onward(downs[-1], *ready))
    three_started = begin(jnp.stack([after(piece, *ready) for piece in ups[2:]]))
    for g in range(2, seqs):
        parts = attend(g, parts, *ready)

    pieces = [p.reshape(tokens, cols) for p in plan.trade(parts)]
    near_three = joined(three_started, parts[0])
    ready = (parts[0], up_two[1], near_three, downs[-1]) + tuple(others)
    downs = jnp.stack([after(piece, *ready) for piece in downs])
    ready += (downs,) + tuple(pieces)
    up_three = final(near_three, *ready)
    downs_started = begin(downs, *ready)
    first_sum, normed, low, full_out = output_norm(
        plan,
        table,
        pieces,
        after(inputs.reshape(tokens, width), downs),
        vectors,
        w_out,
        come,
        *outs,
        others,
    )

    other_low = plan.swap(low)
    near_down = joined(downs_started, low)
    ready = (other_low, up_three[1], near_down)
    down_all = final(near_down, *ready)
    active, slope, up_kept = up_forward(
        plan, table, after(low, *ready), other_low, w_up, come, [up_two, up_three], up_bias
    )
    own, away, down_kept = down_forward(plan, table, active, w_down, [down_all])
    output, grad_second, low_two, sums_two = norm_two(
        table, normed, own, plan.swap(away), cotangent.reshape(tokens, width), vectors
    )

    def begun(send, k, *ready):
        return lax.ppermute(after(send, *ready), BOTH, plan.stage[k])

    def summed(keep, come, k, *ready):
        low = (1 << k) // 2
        come = after(come, *ready)
        return add(keep[:low], come[:low]), add(keep[low:], come[low:])

    def middle(keep, come, *ready):
        keep, send = summed(keep, come, top, *ready)
        for k in reversed(range(1, top)):
            keep, send = summed(keep, begun(send, k), k)
        return keep, send

    other_two = plan.swap(low_two)
    down_send = down_weights(plan, table, active, low_two, other_two, half)
    down_come = begun(down_send, top)
    down_keep = down_weights(plan, table, active, after(low_two, down_send), other_two, 0)
    grad_pre, sums_up, own, away = ffn_backward(
        plan, table, after(low_two, down_keep), other_two, down_kept, up_kept, slope
    )
    away = plan.swap(away)
    low = after(low, own)
    up_send = up_weights(plan, table, low, other_low, grad_pre, half)
    up_come = begun(up_send, top)
    down_keep, down_send = middle(down_keep, down_come, up_send)
    down_last = begun(down_send, 0)
    up_keep = up_weights(plan, table, after(low, up_send, down_send), other_low, grad_pre, 0)
    grad_first, low_one, sums, *parts = norm_one_back(
        plan,
        table,
        grad_second,
        after(own, up_keep),
        away,
        first_sum,
        vectors,
        full_out,
        sums_two,
    )
    parts = plan.trade([p.reshape(seqs, length, cols) for p in parts])
    out_keep, out_send = out_weights(plan, table, pieces, low_one)
    out_come = plan.swap(out_send)
    def sent_along_z(keep, come, *ready):
        *away, own = parts_along_z(plan, table, after(keep, *ready), come)
        return [own] + [
            lax.ppermute(part, BOTH, way) for part, way in zip(away, plan.toward[1:])
        ]

    def total(terms, *ready):
        out = after(terms[0], *ready).astype(F32)
        for piece in terms[1:]:
            out += piece.astype(F32)
        return out.astype(BF16)

    def back(g, before, *ready):
        return attention_backward(
            plan, table, g, seqs, after(qkv[g], *ready), parts, w_qkv, before
        )

    ready = (out_keep, out_come, down_last, up_come) + tuple(parts)
    up_keep, up_send = middle(up_keep, up_come, *ready)
    up_last = begun(up_send, 0)
    down_along = sent_along_z(down_keep[0], down_last[0], *ready)
    out_come = after(out_come, *ready)
    out_kept = add(out_keep[:half], out_come[:half])
    out_sent = add(out_keep[half:], out_come[half:])
    out_first = begun(out_sent, top)
    shared = back(0, [], out_sent, up_send, *ready)
    out_kept, out_sent = middle(out_kept, out_first, shared[0])
    out_last = begun(out_sent, 0)
    grad_down = total(down_along, shared[0])
    ready = (grad_down, up_last, out_sent, shared[0])
    up_along = sent_along_z(up_keep[0], up_last[0], *ready)
    grad_down = plan.share(after(grad_down, *ready))
    shared = back(1, list(shared), *ready)
    ready = (out_last, shared[0]) + tuple(grad_down)
    out_along = sent_along_z(out_kept[0], out_last[0], *ready)
    for g in range(2, seqs):
        shared = back(g, list(shared), *ready)
    grad_qkv, part_keep, part_send = shared

    part_come = begun(part_send, top)
    up_along = [after(up_along[0], part_send)] + up_along[1:]
    up_kept, up_sent = split_by_core(plan, table, up_along)
    up_come = plan.swap(up_sent)
    last_keep, last_send = head_weights_backward(
        plan, table, near_x, far_x, after(grad_qkv, up_kept), sums, sums_up
    )
    last_come = plan.swap(last_send)
    ready = (last_keep, last_send)
    grad_up = jnp.concatenate(
        [after(up_kept, *ready), up_come, total(out_along, *ready)], 1
    )
    last_along = sent_along_z(last_keep, last_come)
    part_keep, part_send = middle(part_keep, part_come, last_come)
    part_last = begun(part_send, 0)
    grad_up = plan.share(after(grad_up, part_send))

    def lanes(size):
        return lambda t, r: aligned(t[plan.MEMBER + r] * size, size)

    grad_inputs = grad_first.reshape(inputs.shape) + (
        part_keep[0].astype(F32) + part_last[0].astype(F32)
    )
    (grad_down,) = place(
        plan,
        table,
        [after(v, part_send) for v in grad_down],
        [(own_hidden, width)],
        [((slice(None),), 0, lanes(cols))],
        "place_down",
    )
    grad_up, grad_out = place(
        plan,
        table,
        grad_up,
        [(own_rows, hidden), (own_rows, width)],
        [
            (
                (slice(None), pl.ds(k * quarter, quarter)),
                0,
                lambda t, r, k=k: aligned(
                    (2 * t[plan.MEMBER + r] + t[plan.CORE + k]) * quarter, quarter
                ),
            )
            for k in range(2)
        ]
        + [((slice(None), pl.ds(2 * quarter, cols)), 1, lanes(cols))],
        "place_up",
    )
    grad_last = plan.share(total(last_along, grad_down, grad_inputs))
    grad_wq, grad_wk, grad_wv = place(
        plan,
        table,
        grad_last,
        [(own_rows, width)] * 3,
        [
            ((pl.ds(0, own_rows), pl.ds(m * cols, cols)), m, lanes(cols))
            for m in range(3)
        ],
        "place_heads",
    )
    vec_out = sum(piece[own_rows:].astype(F32) for piece in grad_last)
    biases = vec_out[7].reshape(3, 2, own_rows)
    biases = jnp.where(core == 0, biases[:, 0], biases[:, 1])
    return (
        output.reshape(inputs.shape),
        grad_inputs,
        grad_wq,
        grad_wk,
        grad_wv,
        biases[0],
        biases[2],
        grad_out,
        vec_out[0, :own_rows],
        vec_out[1, :own_rows],
        vec_out[2, :own_rows],
        grad_up,
        vec_out[8, :own_hidden],
        grad_down,
        vec_out[3, :own_rows],
        vec_out[4, :own_rows],
        vec_out[5, :own_rows],
    )


def solution(mesh):
    plan = Plan(mesh.shape["dp"], mesh.shape["seq"])
    rows, vector, token = P("dp", None), P("dp"), P("dp", "seq", None)
    weights = (rows,) * 3 + (vector,) * 2 + (rows,) + (vector,) * 3
    weights += (rows, vector, rows) + (vector,) * 3
    return jax.shard_map(
        functools.partial(local, plan),
        mesh=mesh,
        in_specs=(token,) + weights + (token,),
        out_specs=(token, token) + weights,
        check_vma=False,
    )
```

```python
import functools

import jax
import jax.numpy as jnp
import numpy as np
from jax import lax
from jax.experimental import pallas as pl
from jax.experimental.pallas import tpu as pltpu
from jax.sharding import PartitionSpec as P

HEAD_DIM = 64
PAIR = 2 * HEAD_DIM
EPSILON = 1e-12
BOTH = ("dp", "seq")
PAD = 16
MICROSECOND = 1_100_000_000
F32 = jnp.float32
BF16 = jnp.bfloat16
ANY = pl.BlockSpec(memory_space=pl.ANY)


def dot(former, latter, former_dim=1, latter_dim=0):
    return lax.dot_general(
        former,
        latter,
        (((former_dim,), (latter_dim,)), ((), ())),
        preferred_element_type=F32,
    )


class Plan:
    def __init__(self, n_dp, n_seq):
        self.n_dp, self.n_seq, self.n_z = n_dp, n_seq, n_dp // 2
        self.bits = n_seq.bit_length() - 1
        order = [0] + list(range(1, self.n_z, 2))
        order += list(range(2, self.n_z, 2))[::-1]
        self.order = order
        self.place = [order.index(z) for z in range(self.n_z)]
        self.core = self.pairs(lambda z, c, s: (z, 1 - c, s))
        self.toward = [
            self.pairs(lambda z, c, s, j=j: (self.behind(z, -j), c, s))
            for j in range(self.n_z)
        ]
        self.z_bits = self.n_z.bit_length() - 1
        self.along = [
            self.pairs(lambda z, c, s, k=k: (z ^ 1 << k, c, s)) for k in range(self.z_bits)
        ]
        self.across = [
            self.pairs(lambda z, c, s, r=r: (z, c, s ^ self.mask(c, r)))
            for r in range(n_seq)
        ]
        self.stage = [
            self.pairs(lambda z, c, s, k=k: (z, c, s ^ self.mask(c, 1 << k)))
            for k in range(self.bits)
        ]
    def behind(self, z, j):
        return self.order[(self.place[z] - j) % self.n_z]

    def mask(self, c, r):
        out = 0
        for k in range(self.bits):
            if r >> k & 1:
                out |= 1 << ((k + c) % self.bits)
        return out

    def pairs(self, target):
        out = []
        for dp in range(self.n_dp):
            for s in range(self.n_seq):
                z, c, t = target(dp // 2, dp % 2, s)
                out.append((dp * self.n_seq + s, (2 * z + c) * self.n_seq + t))
        return out

    def swap(self, block):
        return lax.ppermute(block, BOTH, self.core)

    def trade(self, blocks):
        return [blocks[0]] + [
            lax.ppermute(block, BOTH, way) for block, way in zip(blocks[1:], self.across[1:])
        ]

    def exchange(self, keep, send):
        held = [(0, keep, 0)]
        for k in reversed(range(self.bits)):
            come = lax.ppermute(send, BOTH, self.stage[k])
            width = 1 << k
            held = held + [
                (mask | width, come, i * width) for i, (mask, _, _) in enumerate(held)
            ]
            if k:
                low = width // 2
                send = jnp.concatenate([a[i + low : i + width] for _, a, i in held], 0)
        return [(a, i) for _, a, i in sorted(held, key=lambda item: item[0])]

    def gather(self, block):
        near = block[None]
        for k in range(self.bits - 1):
            near = self.double(near, k)
        return near, lax.ppermute(near, BOTH, self.stage[self.bits - 1])

    def halfway(self, block, *ready):
        near = after(block, *ready)[None]
        for k in range(self.bits - 1):
            near = self.double(near, k)
        return near

    def final(self, near, *ready):
        return lax.ppermute(after(near, *ready), BOTH, self.stage[self.bits - 1])

    def double(self, near, k):
        return jnp.concatenate([near, lax.ppermute(near, BOTH, self.stage[k])], 0)


def add(former, latter):
    return (former.astype(F32) + latter.astype(F32)).astype(BF16)


def after(value, *others):
    return lax.optimization_barrier((value,) + others)[0]


class Here:
    def __init__(self, plan):
        self.plan = plan
        dp = lax.axis_index("dp")
        self.z, self.c, self.s = lax.div(dp, 2), lax.rem(dp, 2), lax.axis_index("seq")

    def core(self, k):
        return self.c if k == 0 else 1 - self.c

    def behind(self, j):
        n = self.plan.n_z
        half = lax.div(self.z, 2)
        odd = lax.rem(self.z, 2)
        place = jnp.where(odd == 1, half + 1, lax.rem(n - half, n))
        at = lax.rem(place - j + n, n)
        return jnp.where(at <= n // 2, jnp.maximum(2 * at - 1, 0), 2 * (n - at))

    def member(self, r, core):
        n, bits = self.plan.n_seq, self.plan.bits
        turned = ((r << 1) & (n - 1)) | (r >> (bits - 1))
        return self.s ^ (r + core * (turned - r))


def shape(dims, dtype=BF16):
    return jax.ShapeDtypeStruct(tuple(dims), dtype)


def distinct(found):
    arrays = []
    for array, _ in found:
        if not any(array is other for other in arrays):
            arrays.append(array)
    at = [([array is other for other in arrays].index(True), i) for array, i in found]
    return arrays, at


def turned(i, bits):
    return sum((i >> k & 1) << (bits - 1 - k) for k in range(bits))


def aligned(start, size):
    return pl.ds(pl.multiple_of(start, size), size)


def whole_block(dims):
    return pl.BlockSpec(tuple(dims), lambda *_: (0,) * len(dims))


def call(
    kernel, plan, operands, in_specs, outs, out_specs, grid, scratch, micros, name, alias=None
):
    size = sum(int(np.prod(o.shape)) * o.dtype.itemsize for o in list(operands) + list(outs))
    size = size if micros else 0

    def placed(spec):
        if spec.index_map is None:
            return spec
        return pl.BlockSpec(spec.block_shape, lambda *i: spec.index_map(*i, Here(plan)))

    return pl.pallas_call(
        lambda *refs: kernel(Here(plan), *refs),
        out_shape=list(outs),
        grid=grid,
        in_specs=[placed(spec) for spec in in_specs],
        out_specs=[placed(spec) for spec in out_specs],
        scratch_shapes=scratch,
        cost_estimate=pl.CostEstimate(
            flops=micros * MICROSECOND, bytes_accessed=size, transcendentals=0
        ),
        input_output_aliases=alias or {},
        name=name,
    )(*operands)


def assemble(table, pieces, moves, outs, name):
    def kernel(table_ref, *refs):
        sources, targets, sems = refs[: len(pieces)], refs[len(pieces) : -1], refs[-1]
        copies = [
            pltpu.make_async_copy(
                sources[i].at[src(table_ref)], targets[o].at[at(table_ref)], sems.at[n]
            )
            for n, (i, src, o, at) in enumerate(moves)
        ]
        for copy in copies:
            copy.start()
        for copy in copies:
            copy.wait()

    return call(
        kernel,
        table,
        pieces,
        [ANY] * len(pieces),
        outs,
        [whole_block(o.shape) for o in outs],
        (1,),
        [pltpu.SemaphoreType.DMA((len(moves),))],
        0,
        name,
    )


def copies_of(moves, sems):
    return [pltpu.make_async_copy(src, at, sems.at[n]) for n, (src, at) in enumerate(moves)]


def lanes_of(half):
    lane = lax.broadcasted_iota(jnp.int32, (1, PAIR), 1)
    return lane < HEAD_DIM if half == 0 else lane >= HEAD_DIM


def only(block, half):
    return jnp.where(lanes_of(half), block, jnp.zeros_like(block))


def statistics(hidden):
    center = hidden - jnp.mean(hidden, -1, keepdims=True)
    spread = jnp.mean(center * center, -1, keepdims=True)
    root = lax.rsqrt(spread + EPSILON)
    return center * root, root


def norm_back(unit, root, gain_vec, upstream):
    scaled = upstream * gain_vec
    first = jnp.mean(scaled, -1, keepdims=True)
    second = jnp.mean(scaled * unit, -1, keepdims=True)
    return root * (scaled - first - unit * second)


def add_rows(target, row, value):
    target[row : row + 1, :] += jnp.sum(value, 0, keepdims=True)


def head_weights(plan, table, mine, theirs):
    n_z, n_dp = plan.n_z, plan.n_dp
    rows, lanes = mine.shape[1:]
    own_rows, cols3 = rows - PAD, lanes // 4 * 3
    width, span = n_dp * own_rows, lanes // 2

    def kernel(t, mine_ref, theirs_ref, w_ref, vec_ref, bias_ref, held, sems):
        moves = []
        for k, source in enumerate((mine_ref, theirs_ref)):
            for j in range(n_z):
                owner = 2 * t.behind(j) + t.core(k)
                moves.append((source.at[j, pl.ds(own_rows, PAD)], held.at[owner]))
                moves.append(
                    (
                        source.at[j, pl.ds(0, own_rows), pl.ds(0, cols3)],
                        w_ref.at[aligned(owner * own_rows, own_rows)],
                    )
                )
        copies = copies_of(moves, sems)
        for copy in copies:
            copy.start()
        for copy in copies:
            copy.wait()
        for owner in range(n_dp):
            values = held[owner].astype(F32)
            at = pl.ds(owner * own_rows, own_rows)
            vec_ref[:, at] = values[:8, :own_rows]
            bias_ref[owner] = values[8:9, :span]

    outs = [shape((width, cols3)), shape((8, width), F32), shape((n_dp, 1, span), F32)]
    return call(
        kernel,
        table,
        [mine, theirs],
        [ANY] * 2,
        outs,
        [whole_block(o.shape) for o in outs],
        (1,),
        [pltpu.VMEM((n_dp, PAD, lanes), BF16), pltpu.SemaphoreType.DMA((4 * n_z,))],
        3,
        "head_weights",
    )


def attention_forward(plan, table, g, near, far, weights, vectors, before):
    n = plan.n_seq
    half, seqs, length, width = near.shape
    n_before = len(before)
    cols3 = weights.shape[1]
    cols = cols3 // 3
    total = n * length
    tile, chunk = min(512, total), min(256, total)
    lse = (cols // PAIR, 8, total)
    scale = HEAD_DIM**-0.5

    def kernel(t, near_ref, far_ref, w_ref, vec_ref, *rest):
        qkv_ref, keep_ref, send_ref, lse_ref, context = rest[n_before:]
        here = aligned(t.s * cols, cols)
        bias = jnp.concatenate(
            [vec_ref[0:1, here], jnp.zeros((1, cols), F32), vec_ref[1:2, here]], 1
        )
        for part, source in enumerate((near_ref, far_ref)):
            rows = source[...].reshape(half * length, width)
            out = dot(rows, w_ref[...]) + bias
            qkv_ref[part * half * length : (part + 1) * half * length, :] = out.astype(BF16)
        def each_pair(pair, carry):
            q_at = aligned(pair * PAIR, PAIR)
            k_at = aligned(cols + pair * PAIR, PAIR)
            value = qkv_ref[:, aligned(2 * cols + pair * PAIR, PAIR)]
            value = value.astype(F32).T.astype(BF16)

            def each_tile(i, carry):
                rows = aligned(i * tile, tile)
                query = qkv_ref[rows, q_at] * jnp.asarray(scale, BF16)
                out = []
                for head in range(2):
                    one = only(query, head)

                    def scores(c):
                        return dot(qkv_ref[pl.ds(c * chunk, chunk), k_at], one, 1, 1)

                    top = None
                    for c in range(total // chunk):
                        here = jnp.max(scores(c), 0, keepdims=True)
                        top = here if c == 0 else jnp.maximum(top, here)
                    for c in range(total // chunk):
                        exponent = jnp.exp(scores(c) - top)
                        here = jnp.sum(exponent, 0, keepdims=True)
                        these = value[
                            head * HEAD_DIM : (head + 1) * HEAD_DIM,
                            c * chunk : (c + 1) * chunk,
                        ]
                        part = dot(these, exponent.astype(BF16))
                        bottom = here if c == 0 else bottom + here
                        acc = part if c == 0 else acc + part
                    out.append(acc * (1.0 / bottom))
                    lse_ref[pair, head : head + 1, rows] = top + jnp.log(bottom)
                context[rows, q_at] = jnp.concatenate(out, 0).T.astype(BF16)
                return carry

            lax.fori_loop(0, total // tile, each_tile, 0)
            return carry

        lax.fori_loop(0, cols // PAIR, each_pair, 0)
        for r in range(n):
            target = keep_ref if r < half else send_ref
            target[r % half, 0] = context[r * length : (r + 1) * length, :]

    block = pl.BlockSpec((half, 1, length, width), lambda i, t: (0, g, 0, 0))
    return call(
        kernel,
        table,
        [near, far, weights, vectors] + before,
        [block, block, whole_block(weights.shape), whole_block(vectors.shape)]
        + [ANY] * n_before,
        [shape((total, cols3))]
        + [shape((half, seqs, length, cols))] * 2
        + [shape(lse, F32)],
        [whole_block((total, cols3))]
        + [pl.BlockSpec((half, 1, length, cols), lambda i, t: (0, g, 0, 0))] * 2
        + [whole_block(lse)],
        (1,),
        [pltpu.VMEM((total, cols), BF16)],
        6,
        "attention_forward",
        {4 + i: 1 + i for i in range(n_before)},
    )


def attention_backward(
    plan, table, g, seqs, qkv, lse, contexts, upstream, where, w_qkv, before
):
    n = plan.n_seq
    half = n // 2
    width, cols3 = w_qkv.shape
    cols = cols3 // 3
    total = qkv.shape[0]
    length = total // n
    tile, chunk = min(512, total), min(256, total)
    scale = HEAD_DIM**-0.5
    n_before, n_up = len(before), len(upstream)

    def kernel(t, qkv_ref, w_ref, lse_ref, near_ref, far_ref, *rest):
        up_refs, rest = rest[:n_up], rest[n_up + n_before :]
        grad_ref, part_keep, part_send = rest[:3]
        up, context, key_acc, value_acc = rest[3:]
        for r, (a, i) in enumerate(where):
            rows = pl.ds(r * length, length)
            up[rows, :] = up_refs[a][i, 0]
            context[rows, :] = (near_ref if r < half else far_ref)[r % half, 0]
        def each_pair(pair, carry):
            q_at = aligned(pair * PAIR, PAIR)
            k_at = aligned(cols + pair * PAIR, PAIR)
            v_at = aligned(2 * cols + pair * PAIR, PAIR)
            value_acc[...] = jnp.zeros_like(value_acc)
            key_acc[...] = jnp.zeros_like(key_acc)

            turned_key = qkv_ref[:, k_at].astype(F32).T.astype(BF16)

            def each_tile(i, carry):
                rows = aligned(i * tile, tile)
                query = qkv_ref[rows, q_at] * jnp.asarray(scale, BF16)
                above = up[rows, q_at]
                both = (above.astype(F32) * context[rows, q_at].astype(F32)).T
                out = []
                for head in range(2):
                    lanes = slice(head * HEAD_DIM, (head + 1) * HEAD_DIM)
                    inner = jnp.sum(both[lanes], 0, keepdims=True)
                    log_total = lse_ref[pair, head : head + 1, rows]
                    one, upper = only(query, head), only(above, head)
                    for c in range(total // chunk):
                        here = pl.ds(c * chunk, chunk)
                        portions = jnp.exp(dot(qkv_ref[here, k_at], one, 1, 1) - log_total)
                        slope = dot(qkv_ref[here, v_at], upper, 1, 1)
                        slope = (portions * (slope - inner)).astype(BF16)
                        value_acc[here, :] += dot(portions.astype(BF16), upper)
                        key_acc[here, :] += dot(slope, one)
                        these = turned_key[lanes, c * chunk : (c + 1) * chunk]
                        part = dot(these, slope)
                        acc = part if c == 0 else acc + part
                    out.append(acc * scale)
                grad_ref[0, rows, q_at] = jnp.concatenate(out, 0).T.astype(BF16)
                return carry

            lax.fori_loop(0, total // tile, each_tile, 0)
            grad_ref[0, :, k_at] = key_acc[...].astype(BF16)
            grad_ref[0, :, v_at] = value_acc[...].astype(BF16)
            return carry

        lax.fori_loop(0, cols // PAIR, each_pair, 0)
        for r in range(n):
            target = part_keep if r < half else part_send
            rows = grad_ref[0, r * length : (r + 1) * length, :]
            target[r % half, 0] = dot(rows, w_ref[...], 1, 1).astype(BF16)

    part = (half, seqs, length, width)
    outs = [shape((seqs, total, cols3)), shape(part), shape(part)]
    block = pl.BlockSpec((half, 1, length, width), lambda i, t: (0, g, 0, 0))
    operands = [qkv, w_qkv, lse, *contexts] + upstream + before
    first = len(operands) - n_before
    return call(
        kernel,
        table,
        operands,
        [whole_block(v.shape) for v in (qkv, w_qkv, lse)]
        + [pl.BlockSpec((half, 1, length, cols), lambda i, t: (0, g, 0, 0))] * 2
        + [
            pl.BlockSpec((v.shape[0], 1, length, cols), lambda i, t: (0, g, 0, 0))
            for v in upstream
        ]
        + [ANY] * n_before,
        outs,
        [pl.BlockSpec((1, total, cols3), lambda i, t: (g, 0, 0)), block, block],
        (1,),
        [
            pltpu.VMEM((total, cols), BF16),
            pltpu.VMEM((total, cols), BF16),
            pltpu.VMEM((total, PAIR), F32),
            pltpu.VMEM((total, PAIR), F32),
        ],
        8,
        "attention_backward",
        {first + i: i for i in range(n_before)},
    )


def head_weights_backward(plan, table, near, far, grad, narrow, wide):
    n, n_z = plan.n_seq, plan.n_z
    half, seqs, length, width = near.shape
    cols3 = grad.shape[2]
    own_rows = width // plan.n_dp
    total = n * length
    span = wide.shape[2]

    def kernel(t, near_ref, far_ref, grad_ref, narrow_ref, wide_ref, *rest):
        w_keep, w_send, w_acc, b_acc = rest
        step_id = pl.program_id(0)

        @pl.when(step_id == 0)
        def _():
            w_acc[...] = jnp.zeros_like(w_acc)
            b_acc[...] = jnp.zeros_like(b_acc)

        for part, source in enumerate((near_ref, far_ref)):
            rows = source[...].reshape(half * length, width)
            these = grad_ref[0, part * half * length : (part + 1) * half * length, :]
            w_acc[...] += dot(rows, these, 0, 0)
        b_acc[0:1, :] += jnp.sum(grad_ref[0].astype(F32), 0, keepdims=True)

        @pl.when(step_id == seqs - 1)
        def _():
            for target, k in ((w_keep, 0), (w_send, 1)):
                for z in range(n_z):
                    row = (2 * z + t.core(k)) * own_rows
                    target[z, :own_rows, :] = w_acc[aligned(row, own_rows), :].astype(BF16)
                    here = (t.s == z).astype(F32)
                    last = lax.broadcasted_iota(jnp.int32, (8, cols3), 0) == 7
                    rows = jnp.where(
                        last, b_acc[0:1, :] * here, narrow_ref[2 * z + t.core(k)]
                    )
                    target[z, own_rows : own_rows + 8, :] = rows.astype(BF16)
                    target[z, own_rows + 8 :, :] = jnp.zeros((PAD - 8, cols3), BF16)
                if k == 0:
                    for r in range(n):
                        rows = wide_ref[r].astype(BF16)
                        target[t.member(r, t.c), own_rows + 8 :, :span] = rows

    block = pl.BlockSpec((half, 1, length, width), lambda g, t: (0, g, 0, 0))
    w_out = (n_z, own_rows + PAD, cols3)
    return call(
        kernel,
        table,
        [near, far, grad, narrow, wide],
        [
            block,
            block,
            pl.BlockSpec((1, total, cols3), lambda g, t: (g, 0, 0)),
            whole_block(narrow.shape),
            whole_block(wide.shape),
        ],
        [shape(w_out), shape(w_out)],
        [whole_block(w_out), whole_block(w_out)],
        (seqs,),
        [pltpu.VMEM((width, cols3), F32), pltpu.VMEM((8, cols3), F32)],
        8,
        "head_weights_backward",
    )


def output_norm(plan, table, pieces, where, inputs, vectors, w_out, come, near, far, others):
    n, n_z = plan.n_seq, plan.n_z
    half = n // 2
    tokens, width = inputs.shape
    own_rows = w_out.shape[0]
    cols = width // n
    tile = 128
    n_moves = 2 + 2 * (n_z - 1) * n

    def kernel(t, in_ref, vec_ref, w_ref, come_ref, near_ref, far_ref, on_ref, of_ref, *rest):
        refs, rest = rest[: len(pieces)], rest[len(pieces) :]
        sum_ref, norm_ref, low_ref, full_ref, sems = rest

        def row(z, k):
            return aligned((z * 2 + t.core(k)) * own_rows, own_rows)

        moves = []
        for k, source in enumerate((w_ref, come_ref)):
            at = full_ref.at[row(t.behind(0), k)]
            lanes = source.shape[1] - width
            moves.append((source.at[pl.ds(0, own_rows), pl.ds(lanes, width)], at))
        for k, (first, second) in enumerate(((near_ref, far_ref), (on_ref, of_ref))):
            for j in range(1, n_z):
                for r in range(n):
                    source = first if r < half else second
                    at = full_ref.at[
                        row(t.behind(j), k),
                        aligned(t.member(r, t.core(k)) * cols, cols),
                    ]
                    moves.append((source.at[r % half, j - 1], at))
        copies = copies_of(moves, sems)
        for copy in copies:
            copy.start()
        for copy in copies:
            copy.wait()
        for i in range(tokens // tile):
            rows = pl.ds(i * tile, tile)
            total = in_ref[rows, :].astype(F32) + vec_ref[2:3, :]
            for r, (a, m) in enumerate(where):
                weights = full_ref[aligned(t.member(r, t.c) * cols, cols), :]
                total += dot(refs[a][m, rows, :], weights)
            unit, _ = statistics(total)
            normed = unit * vec_ref[3:4, :] + vec_ref[4:5, :]
            sum_ref[rows, :] = total
            norm_ref[rows, :] = normed
            low_ref[rows, :] = normed.astype(BF16)

    full = (tokens, width)
    return call(
        kernel,
        table,
        [inputs, vectors, w_out, come, near, far, *others, *pieces],
        [whole_block(full), whole_block(vectors.shape)]
        + [ANY] * 6
        + [whole_block(p.shape) for p in pieces],
        [shape(full, F32), shape(full, F32), shape(full), shape((width, width))],
        [whole_block(full)] * 3 + [whole_block((width, width))],
        (1,),
        [pltpu.SemaphoreType.DMA((n_moves,))],
        7,
        "output_norm",
    )


def flatten(remote):
    arrays, found = [], []
    for near, far in remote:
        found += [(len(arrays), i) for i in range(near.shape[1])]
        arrays += [near, far]
    return arrays, found


def gelu_parts(v):
    big = 0.5 + 0.5 * lax.erf(v * np.float32(np.sqrt(0.5)))
    small = jnp.exp(-0.5 * v * v) * np.float32(1.0 / np.sqrt(2.0 * np.pi))
    return v * big, big + v * small


def up_forward(plan, table, low, other_low, w_up, come, remote, bias):
    n, n_z = plan.n_seq, plan.n_z
    half = n // 2
    tokens, width = low.shape
    own_rows, hidden = w_up.shape
    quarter = hidden // 2 // n
    n_moves = 2 + n_z - 1
    tile = 128

    remote, found = flatten(remote)

    def kernel(t, low_ref, other_ref, up_ref, come_ref, bias_ref, *rest):
        remote_refs, rest = rest[: len(remote)], rest[len(remote) :]
        act_ref, slope_ref, w_hbm, w, sems, out_sem = rest
        step_id = pl.program_id(0)

        def moves(r):
            member = t.member(r, t.c)
            z = t.behind(0)
            at = w.at[r]

            def row(k):
                return aligned((z * 2 + t.core(k)) * own_rows, own_rows)

            lanes = aligned((member * 2 + t.c) * quarter, quarter)
            out = [(up_ref.at[:, lanes], at.at[row(0)])]
            lanes = aligned(member * quarter, quarter)
            out.append((come_ref.at[pl.ds(0, own_rows), lanes], at.at[row(1)]))
            for j in range(1, n_z):
                z_j = t.behind(j)
                a, i = found[j - 1]
                source = remote_refs[a + (r >= half)]
                for k in range(2):
                    rows = aligned((z_j * 2 + t.core(k)) * own_rows, own_rows)
                    out.append(
                        (
                            source.at[r % half, i, pl.ds(k * own_rows, own_rows)],
                            at.at[rows],
                        )
                    )
            return out

        def copies(r):
            return copies_of(moves(r), sems.at[r])

        @pl.when(step_id == 0)
        def _():
            for r in range(n):
                for copy in copies(r):
                    copy.start()

        for r in range(n):

            @pl.when(step_id == r)
            def _(r=r):
                for copy in copies(r):
                    copy.wait()

        def out_copy(r):
            return pltpu.make_async_copy(w.at[r], w_hbm.at[r], out_sem.at[r])

        for r in range(n):

            @pl.when(step_id == r)
            def _(r=r):
                out_copy(r).start()

        weights = w.at[step_id]
        for part, source in enumerate((low_ref, other_ref)):

            def step(i, carry, part=part, source=source):
                rows = pl.ds(pl.multiple_of(i * tile, tile), tile)
                pre = dot(source[rows, :], weights[...]) + bias_ref[0]
                active, slope = gelu_parts(pre)
                rows = pl.ds(pl.multiple_of(part * tokens + i * tile, tile), tile)
                act_ref[0, rows, :] = active.astype(BF16)
                slope_ref[0, rows, :] = slope.astype(BF16)
                return carry

            lax.fori_loop(0, tokens // tile, step, 0)

        @pl.when(step_id == n - 1)
        def _():
            for r in range(n):
                out_copy(r).wait()

    big = (n, 2 * tokens, quarter)
    block = pl.BlockSpec((1, 2 * tokens, quarter), lambda r, t: (r, 0, 0))
    return call(
        kernel,
        table,
        [low, other_low, w_up, come, bias] + remote,
        [whole_block(low.shape)] * 2
        + [ANY] * 2
        + [
            pl.BlockSpec(
                (1, 1, quarter),
                lambda r, t: (2 * t.member(r, t.c) + t.c, 0, 0),
            )
        ]
        + [ANY] * len(remote),
        [shape(big), shape(big), shape((n, width, quarter))],
        [block, block, ANY],
        (n,),
        [
            pltpu.VMEM((n, width, quarter), BF16),
            pltpu.SemaphoreType.DMA((n, 2 + 2 * (n_z - 1))),
            pltpu.SemaphoreType.DMA((n,)),
        ],
        15,
        "up_forward",
    )


def down_forward(plan, table, active, w_down, remote):
    n, n_z = plan.n_seq, plan.n_z
    half = n // 2
    tokens = active.shape[1] // 2
    quarter = active.shape[2]
    own_hidden, width = w_down.shape
    cols = width // n

    remote, found = flatten(remote)

    def kernel(t, act_ref, down_ref, *rest):
        remote_refs, rest = rest[: len(remote)], rest[len(remote) :]
        own_ref, other_ref, w_hbm, w, acc, sems, out_sem = rest
        step_id = pl.program_id(0)
        out_copy = pltpu.make_async_copy(w, w_hbm, out_sem)

        @pl.when(step_id == 0)
        def _():
            moves = [
                (down_ref, w.at[aligned(t.behind(0) * own_hidden, own_hidden)])
            ]
            for j in range(1, n_z):
                rows = aligned(t.behind(j) * own_hidden, own_hidden)
                a, i = found[j - 1]
                for r in range(n):
                    source = remote_refs[a + (r >= half)]
                    lanes = aligned(t.member(r, t.c) * cols, cols)
                    moves.append((source.at[r % half, i], w.at[rows, lanes]))
            copies = copies_of(moves, sems)
            for copy in copies:
                copy.start()
            acc[...] = jnp.zeros_like(acc)
            for copy in copies:
                copy.wait()
            out_copy.start()

        rows = aligned(t.member(step_id, t.c) * quarter, quarter)
        acc[...] += dot(act_ref[0], w[rows, :])

        @pl.when(step_id == n - 1)
        def _():
            own_ref[...] = acc[:tokens, :]
            other_ref[...] = acc[tokens:, :].astype(BF16)
            out_copy.wait()

    full = (tokens, width)
    return call(
        kernel,
        table,
        [active, w_down] + remote,
        [pl.BlockSpec((1, 2 * tokens, quarter), lambda r, t: (r, 0, 0))]
        + [ANY] * (1 + len(remote)),
        [shape(full, F32), shape(full), shape((n * quarter, width))],
        [whole_block(full), whole_block(full), ANY],
        (n,),
        [
            pltpu.VMEM((n * quarter, width), BF16),
            pltpu.VMEM((2 * tokens, width), F32),
            pltpu.SemaphoreType.DMA((1 + (n_z - 1) * n,)),
            pltpu.SemaphoreType.DMA,
        ],
        10,
        "down_forward",
    )


def norm_two(table, normed, own, come, cotangent, vectors):
    tokens, width = normed.shape
    tile = 128

    def kernel(t, norm_ref, own_ref, come_ref, cot_ref, vec_ref, *rest):
        out_ref, grad_ref, low_ref, sums = rest

        @pl.when(pl.program_id(0) == 0)
        def _():
            sums[...] = jnp.zeros_like(sums)

        second = norm_ref[...] + (own_ref[...] + come_ref[...].astype(F32) + vec_ref[5:6, :])
        unit, root = statistics(second)
        gain = vec_ref[6:7, :]
        out_ref[...] = (unit * gain + vec_ref[7:8, :]).astype(BF16)
        above = cot_ref[...].astype(F32)
        grad = norm_back(unit, root, gain, above)
        low = grad.astype(BF16)
        grad_ref[...] = grad
        low_ref[...] = low
        add_rows(sums, 0, low.astype(F32))
        add_rows(sums, 1, above * unit)
        add_rows(sums, 2, above)

    block = pl.BlockSpec((tile, width), lambda i, t: (i, 0))
    full = (tokens, width)
    return call(
        kernel,
        table,
        [normed, own, come, cotangent, vectors],
        [block] * 4 + [whole_block(vectors.shape)],
        [shape(full), shape(full, F32), shape(full), shape((8, width), F32)],
        [block] * 3 + [whole_block((8, width))],
        (tokens // tile,),
        [],
        6,
        "norm_two",
    )


def ffn_backward(plan, table, low, other_low, w_down, w_up, slope):
    n = plan.n_seq
    tokens, width = low.shape
    quarter = slope.shape[2]

    def kernel(t, low_ref, other_ref, down_ref, up_ref, slope_ref, *rest):
        pre_ref, sum_ref, own_ref, come_ref, acc = rest
        step_id = pl.program_id(0)

        @pl.when(step_id == 0)
        def _():
            acc[...] = jnp.zeros_like(acc)

        sums = jnp.zeros((1, quarter), F32)
        for part, source in enumerate((low_ref, other_ref)):
            rows = pl.ds(part * tokens, tokens)
            grad = dot(source[...], down_ref[...], 1, 1) * slope_ref[0, rows, :].astype(F32)
            grad = grad.astype(BF16)
            pre_ref[0, rows, :] = grad
            sums += jnp.sum(grad.astype(F32), 0, keepdims=True)
            acc[rows, :] += dot(grad, up_ref[0], 1, 1)
        row = lax.broadcasted_iota(jnp.int32, (8, quarter), 0)
        sum_ref[0] = jnp.where(row == 0, sums, 0.0)

        @pl.when(step_id == n - 1)
        def _():
            own_ref[...] = acc[:tokens, :]
            come_ref[...] = acc[tokens:, :].astype(BF16)

    big = pl.BlockSpec((1, 2 * tokens, quarter), lambda r, t: (r, 0, 0))
    full = (tokens, width)
    return call(
        kernel,
        table,
        [low, other_low, w_down, w_up, slope],
        [whole_block(full)] * 2
        + [
            pl.BlockSpec((quarter, width), lambda r, t: (t.member(r, t.c), 0)),
            pl.BlockSpec((1, width, quarter), lambda r, t: (r, 0, 0)),
            big,
        ],
        [shape(slope.shape), shape((n, 8, quarter), F32), shape(full, F32), shape(full)],
        [
            big,
            pl.BlockSpec((1, 8, quarter), lambda r, t: (r, 0, 0)),
            whole_block(full),
            whole_block(full),
        ],
        (n,),
        [pltpu.VMEM((2 * tokens, width), F32)],
        13,
        "ffn_backward",
    )


def down_weights(plan, table, active, low, other_low, base):
    n, n_z = plan.n_seq, plan.n_z
    half = n // 2
    tokens, width = low.shape
    quarter = active.shape[2]
    cols = width // n

    def kernel(t, act_ref, low_ref, other_ref, out_ref, grads):
        @pl.when(pl.program_id(0) == 0)
        def _():
            for r in range(half):
                lanes = aligned(t.member(base + r, t.c) * cols, cols)
                here = pl.ds(r * cols, cols)
                grads[:tokens, here] = low_ref[:, lanes]
                grads[tokens:, here] = other_ref[:, lanes]

        total = dot(act_ref[0], grads[...], 0, 0)
        for r in range(half):
            out_ref[r, 0] = total[:, r * cols : (r + 1) * cols].astype(BF16)

    return call(
        kernel,
        table,
        [active, low, other_low],
        [pl.BlockSpec((1, 2 * tokens, quarter), lambda r, t: (r, 0, 0))]
        + [whole_block((tokens, width))] * 2,
        [shape((half, n_z, quarter, cols))],
        [
            pl.BlockSpec(
                (half, 1, quarter, cols), lambda r, t: (0, t.member(r, t.c), 0, 0)
            )
        ],
        (n,),
        [pltpu.VMEM((2 * tokens, half * cols), BF16)],
        5,
        "down_weights",
    )[0]


def up_weights(plan, table, low, other_low, grad_pre, base):
    n, n_z = plan.n_seq, plan.n_z
    half = n // 2
    tokens, width = low.shape
    quarter = grad_pre.shape[2]
    own_rows = width // plan.n_dp

    def kernel(t, low_ref, other_ref, grad_ref, out_ref):
        for z in range(n_z):
            lanes = pl.ds(2 * z * own_rows, 2 * own_rows)
            total = dot(low_ref[:, lanes], grad_ref[0, :tokens, :], 0, 0)
            total += dot(other_ref[:, lanes], grad_ref[0, tokens:, :], 0, 0)
            total = total.astype(BF16)
            out_ref[0, z, :, :quarter] = total[:own_rows]
            out_ref[0, z, :, quarter:] = total[own_rows:]

    dims = (half, n_z, own_rows, 2 * quarter)
    return call(
        kernel,
        table,
        [low, other_low, grad_pre],
        [whole_block((tokens, width))] * 2
        + [pl.BlockSpec((1, 2 * tokens, quarter), lambda i, t: (base + i, 0, 0))],
        [shape(dims)],
        [pl.BlockSpec((1,) + dims[1:], lambda i, t: (i, 0, 0, 0))],
        (half,),
        [],
        6,
        "up_weights",
    )[0]


def norm_one_back(plan, table, grad_second, own, come, first_sum, vectors, w_out, sums_two):
    n = plan.n_seq
    tokens, width = own.shape
    cols = width // n
    tile = 128

    own_rows = width // plan.n_dp

    def kernel(t, grad_ref, own_ref, come_ref, sum_ref, vec_ref, w_ref, two_ref, *rest):
        first_ref, low_ref, narrow_ref = rest[:3]
        keep_ref, send_ref, sums = rest[3:]
        sums[0:3, :] = jnp.zeros((3, width), F32)
        sums[3:6, :] = two_ref[0:3, :]
        sums[6:8, :] = jnp.zeros((2, width), F32)
        for i in range(tokens // tile):
            rows = pl.ds(i * tile, tile)
            above = grad_ref[rows, :] + (own_ref[rows, :] + come_ref[rows, :].astype(F32))
            unit, root = statistics(sum_ref[rows, :])
            grad = norm_back(unit, root, vec_ref[3:4, :], above)
            low = grad.astype(BF16)
            first_ref[rows, :] = grad
            low_ref[rows, :] = low
            add_rows(sums, 0, low.astype(F32))
            add_rows(sums, 1, above * unit)
            add_rows(sums, 2, above)
            for r in range(n):
                weights = w_ref[aligned(t.member(r, t.c) * cols, cols), :]
                target = keep_ref if r < half else send_ref
                target[r % half, rows, :] = dot(low, weights, 1, 1).astype(BF16)
        narrow_ref[...] = jnp.zeros_like(narrow_ref)
        for owner in range(plan.n_dp):
            lanes = pl.ds(owner * own_rows, own_rows)
            narrow_ref[owner, :, 0:own_rows] = sums[:, lanes]

    full = (tokens, width)
    half = n // 2
    part = (half, tokens, cols)
    narrow = (plan.n_dp, 8, 3 * cols)
    return call(
        kernel,
        table,
        [grad_second, own, come, first_sum, vectors, w_out, sums_two],
        [whole_block(full)] * 4
        + [whole_block(v.shape) for v in (vectors, w_out, sums_two)],
        [shape(full, F32), shape(full), shape(narrow, F32)] + [shape(part)] * 2,
        [whole_block(full)] * 2 + [whole_block(narrow)] + [whole_block(part)] * 2,
        (1,),
        [pltpu.VMEM((8, width), F32)],
        8,
        "norm_one_back",
    )


def out_weights(plan, table, pieces, where, low):
    n, n_z = plan.n_seq, plan.n_z
    tokens, width = low.shape
    cols = width // n
    own_rows = width // plan.n_dp

    def kernel(t, low_ref, *rest):
        refs, (keep_ref, send_ref, both) = rest[: len(pieces)], rest[len(pieces) :]
        for r, (a, m) in enumerate(where):
            z = t.member(r, t.c)
            both[...] = dot(refs[a][m], low_ref[...], 0, 0).astype(BF16)
            for target, k in ((send_ref, 1), (keep_ref, 0)):
                rows = aligned(t.core(k) * own_rows, own_rows)
                for s in range(n):
                    at = aligned(t.member(s, t.core(k)) * cols, cols)
                    target[s, z] = both[rows, at]

    dims = (n, n_z, own_rows, cols)
    return call(
        kernel,
        table,
        [low, *pieces],
        [whole_block(low.shape)] + [whole_block(p.shape) for p in pieces],
        [shape(dims), shape(dims)],
        [whole_block(dims)] * 2,
        (1,),
        [pltpu.VMEM((cols, width), BF16)],
        0,
        "out_weights",
    )


def parts_along_z(plan, table, terms):
    n_z = plan.n_z
    rows = terms[0][0].shape[1]
    operands = [v for group in terms for v in group]
    lanes = sum(group[0].shape[2] for group in terms)

    def kernel(t, *refs):
        sources, outs = refs[: len(operands)], refs[len(operands) :]
        for j in range(n_z):

            @pl.when(pl.program_id(0) == j)
            def _(j=j):
                left, at = list(sources), 0
                target = outs[2 * j // n_z]
                for group in terms:
                    total = left.pop(0)[0].astype(F32)
                    for _ in group[1:]:
                        total += left.pop(0)[0].astype(F32)
                    end = at + total.shape[1]
                    target[j % (n_z // 2), :, at:end] = total.astype(BF16)
                    at = end

    def member(i, t):
        here = 0
        for k in range(plan.z_bits):
            here = here | ((i >> k) & 1) << (plan.z_bits - 1 - k)
        return (t.z ^ here, 0, 0)

    out = (n_z // 2, rows, lanes)
    return call(
        kernel,
        table,
        operands,
        [pl.BlockSpec((1,) + v.shape[1:], member) for v in operands],
        [shape(out)] * 2,
        [whole_block(out)] * 2,
        (n_z,),
        [],
        2,
        "parts_along_z",
    )


def split_by_core(plan, table, pieces, split):
    _, rows, lanes = pieces[0].shape
    half = split // 2
    n_pieces = len(pieces)

    def kernel(t, *refs):
        for k, target in enumerate(refs[n_pieces:]):
            size = half if k < 2 else lanes - split
            at = aligned(t.core(k) * half, half) if k < 2 else pl.ds(split, size)
            total = refs[0][0, :, at].astype(F32)
            for ref in refs[1:n_pieces]:
                total += ref[0, :, at].astype(F32)
            target[...] = total.astype(BF16)

    outs = [(rows, half), (rows, half), (rows, lanes - split)]
    return call(
        kernel,
        table,
        pieces,
        [whole_block(p.shape) for p in pieces],
        [shape(o) for o in outs],
        [whole_block(o) for o in outs],
        (1,),
        [],
        0,
        "split_by_core",
    )


def place(plan, table, near, far, outs, moves, name):
    n = plan.n_seq
    half = n // 2

    def kernel(t, near_ref, far_ref, *targets):
        for r in range(n):
            source = near_ref if r < half else far_ref
            for src, o, at in moves:
                targets[o][:, at(t, r)] = source[(r % half,) + src].astype(F32)

    return call(
        kernel,
        table,
        [near, far],
        [whole_block(near.shape)] * 2,
        [shape(o, F32) for o in outs],
        [whole_block(o) for o in outs],
        (1,),
        [],
        0,
        name,
    )


def local(
    plan,
    inputs,
    w_query,
    w_key,
    w_value,
    b_query,
    b_value,
    w_out,
    b_out,
    gain_one,
    shift_one,
    w_up,
    b_up,
    w_down,
    b_down,
    gain_two,
    shift_two,
    cotangent,
):
    n_dp, n, n_z = plan.n_dp, plan.n_seq, plan.n_z
    half = n // 2
    seqs, length, width = inputs.shape
    tokens = seqs * length
    own_rows, hidden = w_up.shape
    own_hidden = w_down.shape[0]
    cols = width // n
    cols3 = 3 * cols
    quarter = hidden // 2 // n
    assert n == n_z and quarter == own_hidden
    table = plan
    core = lax.axis_index("dp") % 2

    narrow = jnp.stack(
        [b_query, b_value, b_out, gain_one, shift_one, b_down, gain_two, shift_two]
    )
    vec = jnp.concatenate(
        [
            jnp.pad(narrow, ((0, 0), (0, 4 * cols - own_rows))),
            jnp.pad(b_up[None], ((0, 7), (0, 4 * cols - own_hidden))),
        ],
        0,
    )

    def column_block(t):
        return (pl.ds(0, own_rows), aligned(t.s * cols, cols))

    moves = [
        (i, column_block, 0, lambda t, i=i: (pl.ds(0, own_rows), pl.ds(i * cols, cols)))
        for i in range(4)
    ]
    moves.append((4, lambda t: (pl.ds(0, PAD),), 0, lambda t: (pl.ds(own_rows, PAD),)))
    (first,) = assemble(
        table,
        [w_query, w_key, w_value, w_out, vec],
        moves,
        [shape((own_rows + PAD, 4 * cols))],
        "pack_first",
    )

    def straight(block, j):
        return lax.ppermute(block, BOTH, plan.toward[j])

    near_x = inputs[None]
    for k in range(plan.bits - 1):
        near_x = plan.double(near_x, k)
    mine = [first, straight(first, 1)]

    top = plan.bits - 1

    def final(near, *ready):
        return near, lax.ppermute(after(near, *ready), BOTH, plan.stage[top])

    def begin(block, *ready):
        near = after(block, *ready)[None]
        for k in range(top - 1):
            near = plan.double(near, k)
        return near, lax.ppermute(near, BOTH, plan.stage[top - 1])

    def joined(started, *ready):
        return jnp.concatenate([after(started[0], *ready), started[1]], 0)

    def onward(block, *ready):
        return lax.ppermute(after(block, *ready), BOTH, plan.toward[1])

    ready = (near_x, mine[1])
    far_x = final(near_x, *ready)[1]
    mine.append(onward(mine[1], *ready))
    for j in range(3, n_z):
        mine.append(onward(mine[-1]))

    moves = []
    for z in range(n_z):
        moves.append(
            (
                0,
                lambda t, z=z: (
                    pl.ds(0, own_rows),
                    aligned((2 * z + (1 - t.c)) * quarter, quarter),
                ),
                0,
                lambda t, z=z: (pl.ds(0, own_rows), pl.ds(z * quarter, quarter)),
            )
        )
    moves.append(
        (
            1,
            lambda t: (pl.ds(0, own_rows),),
            0,
            lambda t: (pl.ds(0, own_rows), pl.ds(n * quarter, width)),
        )
    )
    (across,) = assemble(
        table,
        [after(w_up, mine[2]), w_out],
        moves,
        [shape((own_rows, n * quarter + width))],
        "pack_across",
    )
    come = plan.swap(across)


    def rows_at(start, size):
        return lambda t: (pl.ds(start, size), pl.ds(0, quarter))

    moves = [
        (
            0,
            lambda t: (
                pl.ds(0, own_rows),
                aligned((2 * t.s + t.c) * quarter, quarter),
            ),
            0,
            rows_at(0, own_rows),
        ),
        (
            1,
            lambda t: (pl.ds(0, own_rows), aligned(t.s * quarter, quarter)),
            0,
            rows_at(own_rows, own_rows),
        ),
    ]
    moves.append(
        (
            2,
            lambda t: (pl.ds(0, own_hidden), aligned(t.s * cols, cols)),
            1,
            lambda t: (pl.ds(0, own_hidden),),
        )
    )
    second, down = assemble(
        table,
        [w_up, come, w_down],
        moves,
        [shape((2 * own_rows, quarter)), shape((own_hidden, cols))],
        "pack_second",
    )
    ups = [onward(second)]

    ready = (far_x, ups[0]) + tuple(mine[1:])
    mine_all = jnp.stack([after(piece, *ready) for piece in mine])
    theirs = plan.swap(mine_all)
    outs = jnp.stack([after(piece, *ready)[:own_rows, cols3:] for piece in mine[1:]])
    outs_started = begin(outs)
    ups.append(onward(ups[0], *ready))
    downs = [onward(down, *ready)]
    w_qkv, vectors, up_bias = head_weights(plan, table, mine_all, theirs)
    qkv, lse = [], []

    def attend(g, before, *ready):
        out, *parts, total = attention_forward(
            plan, table, g, near_x, far_x, w_qkv, after(vectors, *ready), before
        )
        qkv.append(out)
        lse.append(total)
        return parts

    parts = attend(0, [])

    near_out = joined(outs_started, parts[0])
    ready = (near_out, parts[0], ups[1], downs[0])
    outs = final(near_out, *ready)
    ups.append(onward(ups[1], *ready))
    downs.append(onward(downs[0], *ready))
    two_started = begin(jnp.stack([after(piece, *ready) for piece in ups[:2]]))
    parts = attend(1, parts, *ready)

    near_two = joined(two_started, parts[0])
    ready = (near_two, outs[1], ups[2], downs[1], parts[0])
    for j in range(3, n_z - 1):
        ups.append(onward(ups[-1]))
        downs.append(onward(downs[-1]))
    others = [plan.swap(after(part, *ready)) for part in outs]
    up_two = final(near_two, *ready)
    downs.append(onward(downs[-1], *ready))
    three_started = begin(jnp.stack([after(piece, *ready) for piece in ups[2:]]))
    for g in range(2, seqs):
        parts = attend(g, parts, *ready)

    contexts = parts
    pieces, where = distinct(plan.exchange(*parts))
    pieces = [p.reshape(p.shape[0], tokens, cols) for p in pieces]
    near_three = joined(three_started, parts[0])
    ready = (parts[0], up_two[1], near_three, downs[-1]) + tuple(others)
    downs = jnp.stack([after(piece, *ready) for piece in downs])
    ready += (downs,) + tuple(pieces)
    up_three = final(near_three, *ready)
    downs_started = begin(downs, *ready)
    first_sum, normed, low, full_out = output_norm(
        plan,
        table,
        pieces,
        where,
        after(inputs.reshape(tokens, width), downs),
        vectors,
        w_out,
        come,
        *outs,
        others,
    )

    other_low = plan.swap(low)
    near_down = joined(downs_started, low)
    ready = (other_low, up_three[1], near_down)
    down_all = final(near_down, *ready)
    active, slope, up_kept = up_forward(
        plan, table, after(low, *ready), other_low, w_up, come, [up_two, up_three], up_bias
    )
    own, away, down_kept = down_forward(plan, table, active, w_down, [down_all])
    output, grad_second, low_two, sums_two = norm_two(
        table, normed, own, plan.swap(away), cotangent.reshape(tokens, width), vectors
    )

    def begun(send, k, *ready):
        return lax.ppermute(after(send, *ready), BOTH, plan.stage[k])

    def summed(keep, come, k, *ready):
        low = (1 << k) // 2
        come = after(come, *ready)
        return add(keep[:low], come[:low]), add(keep[low:], come[low:])

    def middle(keep, come, *ready):
        keep, send = summed(keep, come, top, *ready)
        for k in reversed(range(1, top)):
            keep, send = summed(keep, begun(send, k), k)
        return keep, send

    other_two = plan.swap(low_two)
    down_send = down_weights(plan, table, active, low_two, other_two, half)
    down_come = begun(down_send, top)
    down_keep = down_weights(plan, table, active, after(low_two, down_send), other_two, 0)
    grad_pre, sums_up, own, away = ffn_backward(
        plan, table, after(low_two, down_keep), other_two, down_kept, up_kept, slope
    )
    away = plan.swap(away)
    low = after(low, own)
    up_send = up_weights(plan, table, low, other_low, grad_pre, half)
    up_come = begun(up_send, top)
    down_keep, down_send = middle(down_keep, down_come, up_send)
    down_last = begun(down_send, 0)
    up_keep = up_weights(plan, table, after(low, up_send, down_send), other_low, grad_pre, 0)
    grad_first, low_one, sums, *parts = norm_one_back(
        plan,
        table,
        grad_second,
        after(own, up_keep),
        away,
        first_sum,
        vectors,
        full_out,
        sums_two,
    )
    found = plan.exchange(*[p.reshape(half, seqs, length, cols) for p in parts])
    parts, up_where = distinct(found)
    out_keep, out_send = out_weights(plan, table, pieces, where, low_one)
    out_come = plan.swap(out_send)
    def sent_along_z(terms, *ready):
        terms = [[after(group[0], *ready)] + group[1:] for group in terms]
        keep, send = parts_along_z(plan, table, terms)
        return keep, lax.ppermute(send, BOTH, plan.along[0])

    def on_along_z(keep, come, *ready):
        for way in plan.along[1:]:
            low = keep.shape[0] // 2
            come = after(come, *ready)
            sent = add(keep[low:], come[low:])
            keep = add(keep[:low], come[:low])
            come = lax.ppermute(sent, BOTH, way)
        return keep, come

    def total(keep, come, *ready):
        return add(after(keep, *ready), come)[0]

    def back(g, before, *ready):
        return attention_backward(
            plan,
            table,
            g,
            seqs,
            after(qkv[g], *ready),
            lse[g],
            contexts,
            parts,
            up_where,
            w_qkv,
            before,
        )

    ready = (out_keep, out_come, down_last, up_come) + tuple(parts)
    up_keep, up_send = middle(up_keep, up_come, *ready)
    up_last = begun(up_send, 0)
    out_come = after(out_come, up_send)
    outs = [add(out_keep[r], out_come[r]) for r in range(n)]
    down_along = sent_along_z([[down_keep[0], down_last[0]]], up_send)
    outs = plan.trade([after(v, down_along[0]) for v in outs])
    shared = back(0, [], down_along[0], up_send, outs[0], *ready)
    down_along = on_along_z(*down_along, shared[0])
    up_along = sent_along_z([[up_keep[0], up_last[0]], outs], shared[0])
    shared = back(1, list(shared), up_along[0], down_along[0])
    grad_down = total(*down_along, shared[0])
    up_along = on_along_z(*up_along, shared[0])
    down_near = plan.halfway(grad_down, up_along[0])
    for g in range(2, seqs):
        shared = back(g, list(shared), up_along[0], grad_down)
    grad_qkv, part_keep, part_send = shared

    part_come = begun(part_send, top)
    up_along = (after(up_along[0], grad_qkv), up_along[1])
    up_kept, up_sent, grad_out = split_by_core(plan, table, up_along, 2 * quarter)
    up_come = plan.swap(up_sent)
    down_far = plan.final(down_near, up_sent)
    last_keep, last_send = head_weights_backward(
        plan, table, near_x, far_x, after(grad_qkv, up_sent), sums, sums_up
    )
    last_come = plan.swap(last_send)
    last_along = sent_along_z([[last_keep, last_come]])
    up_kept = after(up_kept, last_along[0])
    up_near = plan.halfway(jnp.concatenate([up_kept, up_come, grad_out], 1))
    part_keep, part_send = middle(part_keep, part_come, last_along[0])
    part_last = begun(part_send, 0)
    last_along = on_along_z(*last_along, part_send)
    up_far = plan.final(up_near, last_along[0])

    def lanes(size):
        return lambda t, r: aligned(t.member(r, t.c) * size, size)

    grad_inputs = grad_first.reshape(inputs.shape) + (
        part_keep[0].astype(F32) + part_last[0].astype(F32)
    )
    (grad_down,) = place(
        plan,
        table,
        after(down_near, last_along[0]),
        down_far,
        [(own_hidden, width)],
        [((slice(None),), 0, lanes(cols))],
        "place_down",
    )
    grad_inputs = grad_first.reshape(inputs.shape) + (
        part_keep[0].astype(F32) + after(part_last[0], grad_down).astype(F32)
    )
    last_near = plan.halfway(total(*last_along, grad_inputs))
    last_far = plan.final(last_near)
    grad_up, grad_out = place(
        plan,
        table,
        after(up_near, last_near),
        up_far,
        [(own_rows, hidden), (own_rows, width)],
        [
            (
                (slice(None), pl.ds(k * quarter, quarter)),
                0,
                lambda t, r, k=k: aligned(
                    (2 * t.member(r, t.c) + t.core(k)) * quarter, quarter
                ),
            )
            for k in range(2)
        ]
        + [((slice(None), pl.ds(2 * quarter, cols)), 1, lanes(cols))],
        "place_up",
    )
    grad_wq, grad_wk, grad_wv = place(
        plan,
        table,
        last_near,
        last_far,
        [(own_rows, width)] * 3,
        [
            ((pl.ds(0, own_rows), pl.ds(m * cols, cols)), m, lanes(cols))
            for m in range(3)
        ],
        "place_heads",
    )
    vec_out = jnp.sum(last_near[:, own_rows:].astype(F32), 0)
    vec_out += jnp.sum(last_far[:, own_rows:].astype(F32), 0)
    biases = vec_out[7].reshape(3, 2, own_rows)
    biases = jnp.where(core == 0, biases[:, 0], biases[:, 1])
    return (
        output.reshape(inputs.shape),
        grad_inputs,
        grad_wq,
        grad_wk,
        grad_wv,
        biases[0],
        biases[2],
        grad_out,
        vec_out[0, :own_rows],
        vec_out[1, :own_rows],
        vec_out[2, :own_rows],
        grad_up,
        vec_out[8, :own_hidden],
        grad_down,
        vec_out[3, :own_rows],
        vec_out[4, :own_rows],
        vec_out[5, :own_rows],
    )


def solution(mesh):
    plan = Plan(mesh.shape["dp"], mesh.shape["seq"])
    rows, vector, token = P("dp", None), P("dp"), P("dp", "seq", None)
    weights = (rows,) * 3 + (vector,) * 2 + (rows,) + (vector,) * 3
    weights += (rows, vector, rows) + (vector,) * 3
    return jax.shard_map(
        functools.partial(local, plan),
        mesh=mesh,
        in_specs=(token,) + weights + (token,),
        out_specs=(token, token) + weights,
        check_vma=False,
    )
```

```python
import functools

import jax
import jax.numpy as jnp
import numpy as np
from jax import lax
from jax.experimental import pallas as pl
from jax.experimental.pallas import tpu as pltpu
from jax.sharding import PartitionSpec as P

HEAD_DIM = 64
PAIR = 2 * HEAD_DIM
EPSILON = 1e-12
BOTH = ("dp", "seq")
PAD = 16
MICROSECOND = 1_100_000_000
F32 = jnp.float32
BF16 = jnp.bfloat16
ANY = pl.BlockSpec(memory_space=pl.ANY)


def dot(former, latter, former_dim=1, latter_dim=0):
    return lax.dot_general(
        former,
        latter,
        (((former_dim,), (latter_dim,)), ((), ())),
        preferred_element_type=F32,
    )


class Plan:
    def __init__(self, n_dp, n_seq):
        self.n_dp, self.n_seq, self.n_z = n_dp, n_seq, n_dp // 2
        self.bits = n_seq.bit_length() - 1
        order = [0] + list(range(1, self.n_z, 2))
        order += list(range(2, self.n_z, 2))[::-1]
        self.order = order
        self.place = [order.index(z) for z in range(self.n_z)]
        self.core = self.pairs(lambda z, c, s: (z, 1 - c, s))
        self.toward = [
            self.pairs(lambda z, c, s, j=j: (self.behind(z, -j), c, s))
            for j in range(self.n_z)
        ]
        self.z_bits = self.n_z.bit_length() - 1
        self.along = [
            self.pairs(lambda z, c, s, k=k: (z ^ 1 << k, c, s)) for k in range(self.z_bits)
        ]
        self.across = [
            self.pairs(lambda z, c, s, r=r: (z, c, s ^ self.mask(c, r)))
            for r in range(n_seq)
        ]
        self.stage = [
            self.pairs(lambda z, c, s, k=k: (z, c, s ^ self.mask(c, 1 << k)))
            for k in range(self.bits)
        ]
    def behind(self, z, j):
        return self.order[(self.place[z] - j) % self.n_z]

    def mask(self, c, r):
        out = 0
        for k in range(self.bits):
            if r >> k & 1:
                out |= 1 << ((k + c) % self.bits)
        return out

    def pairs(self, target):
        out = []
        for dp in range(self.n_dp):
            for s in range(self.n_seq):
                z, c, t = target(dp // 2, dp % 2, s)
                out.append((dp * self.n_seq + s, (2 * z + c) * self.n_seq + t))
        return out

    def swap(self, block):
        return lax.ppermute(block, BOTH, self.core)

    def trade(self, blocks):
        return [blocks[0]] + [
            lax.ppermute(block, BOTH, way) for block, way in zip(blocks[1:], self.across[1:])
        ]

    def exchange(self, keep, send, *ready):
        held = [(0, keep, 0)]
        for k in reversed(range(self.bits)):
            come = after(lax.ppermute(send, BOTH, self.stage[k]), *ready)
            width, ready = 1 << k, ()
            held = held + [
                (mask | width, come, i * width) for i, (mask, _, _) in enumerate(held)
            ]
            if k:
                low = width // 2
                send = jnp.concatenate([a[i + low : i + width] for _, a, i in held], 0)
        return [(a, i) for _, a, i in sorted(held, key=lambda item: item[0])]

    def gather(self, block):
        near = block[None]
        for k in range(self.bits - 1):
            near = self.double(near, k)
        return near, lax.ppermute(near, BOTH, self.stage[self.bits - 1])

    def halfway(self, block, *ready):
        near = after(block, *ready)[None]
        for k in range(self.bits - 1):
            near = self.double(near, k)
        return near

    def final(self, near, *ready):
        return lax.ppermute(after(near, *ready), BOTH, self.stage[self.bits - 1])

    def double(self, near, k):
        return jnp.concatenate([near, lax.ppermute(near, BOTH, self.stage[k])], 0)


def add(former, latter):
    return (former.astype(F32) + latter.astype(F32)).astype(BF16)


def after(value, *others):
    return lax.optimization_barrier((value,) + others)[0]


class Here:
    def __init__(self, plan):
        self.plan = plan
        dp = lax.axis_index("dp")
        self.z, self.c, self.s = lax.div(dp, 2), lax.rem(dp, 2), lax.axis_index("seq")

    def core(self, k):
        return self.c if k == 0 else 1 - self.c

    def behind(self, j):
        n = self.plan.n_z
        half = lax.div(self.z, 2)
        odd = lax.rem(self.z, 2)
        place = jnp.where(odd == 1, half + 1, lax.rem(n - half, n))
        at = lax.rem(place - j + n, n)
        return jnp.where(at <= n // 2, jnp.maximum(2 * at - 1, 0), 2 * (n - at))

    def member(self, r, core):
        n, bits = self.plan.n_seq, self.plan.bits
        turned = ((r << 1) & (n - 1)) | (r >> (bits - 1))
        return self.s ^ (r + core * (turned - r))


def shape(dims, dtype=BF16):
    return jax.ShapeDtypeStruct(tuple(dims), dtype)


def distinct(found):
    arrays = []
    for array, _ in found:
        if not any(array is other for other in arrays):
            arrays.append(array)
    at = [([array is other for other in arrays].index(True), i) for array, i in found]
    return arrays, at


def turned(i, bits):
    return sum((i >> k & 1) << (bits - 1 - k) for k in range(bits))


def aligned(start, size):
    return pl.ds(pl.multiple_of(start, size), size)


def whole_block(dims):
    return pl.BlockSpec(tuple(dims), lambda *_: (0,) * len(dims))


def call(
    kernel, plan, operands, in_specs, outs, out_specs, grid, scratch, micros, name, alias=None
):
    size = sum(int(np.prod(o.shape)) * o.dtype.itemsize for o in list(operands) + list(outs))
    size = size if micros else 0

    def placed(spec):
        if spec.index_map is None:
            return spec
        return pl.BlockSpec(spec.block_shape, lambda *i: spec.index_map(*i, Here(plan)))

    return pl.pallas_call(
        lambda *refs: kernel(Here(plan), *refs),
        out_shape=list(outs),
        grid=grid,
        in_specs=[placed(spec) for spec in in_specs],
        out_specs=[placed(spec) for spec in out_specs],
        scratch_shapes=scratch,
        cost_estimate=pl.CostEstimate(
            flops=micros * MICROSECOND, bytes_accessed=size, transcendentals=0
        ),
        input_output_aliases=alias or {},
        name=name,
    )(*operands)


def assemble(table, pieces, moves, outs, name):
    def kernel(table_ref, *refs):
        sources, targets, sems = refs[: len(pieces)], refs[len(pieces) : -1], refs[-1]
        copies = [
            pltpu.make_async_copy(
                sources[i].at[src(table_ref)], targets[o].at[at(table_ref)], sems.at[n]
            )
            for n, (i, src, o, at) in enumerate(moves)
        ]
        for copy in copies:
            copy.start()
        for copy in copies:
            copy.wait()

    return call(
        kernel,
        table,
        pieces,
        [ANY] * len(pieces),
        outs,
        [whole_block(o.shape) for o in outs],
        (1,),
        [pltpu.SemaphoreType.DMA((len(moves),))],
        0,
        name,
    )


def copies_of(moves, sems):
    return [pltpu.make_async_copy(src, at, sems.at[n]) for n, (src, at) in enumerate(moves)]


def lanes_of(half):
    lane = lax.broadcasted_iota(jnp.int32, (1, PAIR), 1)
    return lane < HEAD_DIM if half == 0 else lane >= HEAD_DIM


def only(block, half):
    return jnp.where(lanes_of(half), block, jnp.zeros_like(block))


def statistics(hidden):
    center = hidden - jnp.mean(hidden, -1, keepdims=True)
    spread = jnp.mean(center * center, -1, keepdims=True)
    root = lax.rsqrt(spread + EPSILON)
    return center * root, root


def norm_back(unit, root, gain_vec, upstream):
    scaled = upstream * gain_vec
    first = jnp.mean(scaled, -1, keepdims=True)
    second = jnp.mean(scaled * unit, -1, keepdims=True)
    return root * (scaled - first - unit * second)


def add_rows(target, row, value):
    target[row : row + 1, :] += jnp.sum(value, 0, keepdims=True)


def head_weights(plan, table, mine, theirs):
    n_z, n_dp = plan.n_z, plan.n_dp
    rows, lanes = mine.shape[1:]
    own_rows, cols3 = rows - PAD, lanes // 4 * 3
    width, span = n_dp * own_rows, lanes // 2

    def kernel(t, mine_ref, theirs_ref, w_ref, vec_ref, bias_ref, held, sems):
        moves = []
        for k, source in enumerate((mine_ref, theirs_ref)):
            for j in range(n_z):
                owner = 2 * t.behind(j) + t.core(k)
                moves.append((source.at[j, pl.ds(own_rows, PAD)], held.at[owner]))
                moves.append(
                    (
                        source.at[j, pl.ds(0, own_rows), pl.ds(0, cols3)],
                        w_ref.at[aligned(owner * own_rows, own_rows)],
                    )
                )
        copies = copies_of(moves, sems)
        for copy in copies:
            copy.start()
        for copy in copies:
            copy.wait()
        for owner in range(n_dp):
            values = held[owner].astype(F32)
            at = pl.ds(owner * own_rows, own_rows)
            vec_ref[:, at] = values[:8, :own_rows]
            bias_ref[owner] = values[8:9, :span]

    outs = [shape((width, cols3)), shape((8, width), F32), shape((n_dp, 1, span), F32)]
    return call(
        kernel,
        table,
        [mine, theirs],
        [ANY] * 2,
        outs,
        [whole_block(o.shape) for o in outs],
        (1,),
        [pltpu.VMEM((n_dp, PAD, lanes), BF16), pltpu.SemaphoreType.DMA((4 * n_z,))],
        3,
        "head_weights",
    )


def attention_forward(plan, table, g, near, far, weights, vectors, before):
    n = plan.n_seq
    half, seqs, length, width = near.shape
    n_before = len(before)
    cols3 = weights.shape[1]
    cols = cols3 // 3
    total = n * length
    tile, chunk = min(512, total), min(256, total)
    lse = (cols // PAIR, 8, total)
    scale = HEAD_DIM**-0.5

    def kernel(t, near_ref, far_ref, w_ref, vec_ref, *rest):
        qkv_ref, keep_ref, send_ref, lse_ref, context = rest[n_before:]
        here = aligned(t.s * cols, cols)
        bias = jnp.concatenate(
            [vec_ref[0:1, here], jnp.zeros((1, cols), F32), vec_ref[1:2, here]], 1
        )
        for part, source in enumerate((near_ref, far_ref)):
            rows = source[...].reshape(half * length, width)
            out = dot(rows, w_ref[...]) + bias
            qkv_ref[part * half * length : (part + 1) * half * length, :] = out.astype(BF16)
        def each_pair(pair, carry):
            q_at = aligned(pair * PAIR, PAIR)
            k_at = aligned(cols + pair * PAIR, PAIR)
            value = qkv_ref[:, aligned(2 * cols + pair * PAIR, PAIR)]
            value = value.astype(F32).T.astype(BF16)

            def each_tile(i, carry):
                rows = aligned(i * tile, tile)
                query = qkv_ref[rows, q_at] * jnp.asarray(scale, BF16)
                out = []
                for head in range(2):
                    one = only(query, head)

                    def scores(c):
                        return dot(qkv_ref[pl.ds(c * chunk, chunk), k_at], one, 1, 1)

                    top = None
                    for c in range(total // chunk):
                        here = jnp.max(scores(c), 0, keepdims=True)
                        top = here if c == 0 else jnp.maximum(top, here)
                    for c in range(total // chunk):
                        exponent = jnp.exp(scores(c) - top)
                        here = jnp.sum(exponent, 0, keepdims=True)
                        these = value[
                            head * HEAD_DIM : (head + 1) * HEAD_DIM,
                            c * chunk : (c + 1) * chunk,
                        ]
                        part = dot(these, exponent.astype(BF16))
                        bottom = here if c == 0 else bottom + here
                        acc = part if c == 0 else acc + part
                    out.append(acc * (1.0 / bottom))
                    lse_ref[pair, head : head + 1, rows] = top + jnp.log(bottom)
                context[rows, q_at] = jnp.concatenate(out, 0).T.astype(BF16)
                return carry

            lax.fori_loop(0, total // tile, each_tile, 0)
            return carry

        lax.fori_loop(0, cols // PAIR, each_pair, 0)
        for r in range(n):
            target = keep_ref if r < half else send_ref
            target[r % half, 0] = context[r * length : (r + 1) * length, :]

    block = pl.BlockSpec((half, 1, length, width), lambda i, t: (0, g, 0, 0))
    return call(
        kernel,
        table,
        [near, far, weights, vectors] + before,
        [block, block, whole_block(weights.shape), whole_block(vectors.shape)]
        + [ANY] * n_before,
        [shape((total, cols3))]
        + [shape((half, seqs, length, cols))] * 2
        + [shape(lse, F32)],
        [whole_block((total, cols3))]
        + [pl.BlockSpec((half, 1, length, cols), lambda i, t: (0, g, 0, 0))] * 2
        + [whole_block(lse)],
        (1,),
        [pltpu.VMEM((total, cols), BF16)],
        6,
        "attention_forward",
        {4 + i: 1 + i for i in range(n_before)},
    )


def attention_backward(
    plan, table, g, seqs, qkv, lse, contexts, upstream, where, w_qkv, before
):
    n = plan.n_seq
    half = n // 2
    width, cols3 = w_qkv.shape
    cols = cols3 // 3
    total = qkv.shape[0]
    length = total // n
    tile, chunk = min(512, total), min(256, total)
    scale = HEAD_DIM**-0.5
    n_before, n_up = len(before), len(upstream)

    def kernel(t, qkv_ref, w_ref, lse_ref, near_ref, far_ref, *rest):
        up_refs, rest = rest[:n_up], rest[n_up + n_before :]
        grad_ref, part_keep, part_send = rest[:3]
        up, context, key_acc, value_acc = rest[3:]
        for r, (a, i) in enumerate(where):
            rows = pl.ds(r * length, length)
            up[rows, :] = up_refs[a][i, 0]
            context[rows, :] = (near_ref if r < half else far_ref)[r % half, 0]
        def each_pair(pair, carry):
            q_at = aligned(pair * PAIR, PAIR)
            k_at = aligned(cols + pair * PAIR, PAIR)
            v_at = aligned(2 * cols + pair * PAIR, PAIR)
            value_acc[...] = jnp.zeros_like(value_acc)
            key_acc[...] = jnp.zeros_like(key_acc)

            turned_key = qkv_ref[:, k_at].astype(F32).T.astype(BF16)

            def each_tile(i, carry):
                rows = aligned(i * tile, tile)
                query = qkv_ref[rows, q_at] * jnp.asarray(scale, BF16)
                above = up[rows, q_at]
                both = (above.astype(F32) * context[rows, q_at].astype(F32)).T
                out = []
                for head in range(2):
                    lanes = slice(head * HEAD_DIM, (head + 1) * HEAD_DIM)
                    inner = jnp.sum(both[lanes], 0, keepdims=True)
                    log_total = lse_ref[pair, head : head + 1, rows]
                    one, upper = only(query, head), only(above, head)
                    for c in range(total // chunk):
                        here = pl.ds(c * chunk, chunk)
                        portions = jnp.exp(dot(qkv_ref[here, k_at], one, 1, 1) - log_total)
                        slope = dot(qkv_ref[here, v_at], upper, 1, 1)
                        slope = (portions * (slope - inner)).astype(BF16)
                        value_acc[here, :] += dot(portions.astype(BF16), upper)
                        key_acc[here, :] += dot(slope, one)
                        these = turned_key[lanes, c * chunk : (c + 1) * chunk]
                        part = dot(these, slope)
                        acc = part if c == 0 else acc + part
                    out.append(acc * scale)
                grad_ref[0, rows, q_at] = jnp.concatenate(out, 0).T.astype(BF16)
                return carry

            lax.fori_loop(0, total // tile, each_tile, 0)
            grad_ref[0, :, k_at] = key_acc[...].astype(BF16)
            grad_ref[0, :, v_at] = value_acc[...].astype(BF16)
            return carry

        lax.fori_loop(0, cols // PAIR, each_pair, 0)
        for target, base in ((part_send, half), (part_keep, 0)):

            def each_part(r, carry, target=target, base=base):
                rows = grad_ref[0, aligned((base + r) * length, length), :]
                target[r, 0] = dot(rows, w_ref[...], 1, 1).astype(BF16)
                return carry

            lax.fori_loop(0, half, each_part, 0)

    part = (half, seqs, length, width)
    outs = [shape((seqs, total, cols3)), shape(part), shape(part)]
    block = pl.BlockSpec((half, 1, length, width), lambda i, t: (0, g, 0, 0))
    operands = [qkv, w_qkv, lse, *contexts] + upstream + before
    first = len(operands) - n_before
    return call(
        kernel,
        table,
        operands,
        [whole_block(v.shape) for v in (qkv, w_qkv, lse)]
        + [pl.BlockSpec((half, 1, length, cols), lambda i, t: (0, g, 0, 0))] * 2
        + [
            pl.BlockSpec((v.shape[0], 1, length, cols), lambda i, t: (0, g, 0, 0))
            for v in upstream
        ]
        + [ANY] * n_before,
        outs,
        [pl.BlockSpec((1, total, cols3), lambda i, t: (g, 0, 0)), block, block],
        (1,),
        [
            pltpu.VMEM((total, cols), BF16),
            pltpu.VMEM((total, cols), BF16),
            pltpu.VMEM((total, PAIR), F32),
            pltpu.VMEM((total, PAIR), F32),
        ],
        8,
        "attention_backward",
        {first + i: i for i in range(n_before)},
    )


def head_weights_backward(plan, table, near, far, grad, narrow, wide):
    n, n_z = plan.n_seq, plan.n_z
    half, seqs, length, width = near.shape
    cols3 = grad.shape[2]
    own_rows = width // plan.n_dp
    total = n * length
    span = wide.shape[2]

    def kernel(t, near_ref, far_ref, grad_ref, narrow_ref, wide_ref, *rest):
        w_keep, w_send, w_acc, b_acc = rest
        step_id = pl.program_id(0)

        @pl.when(step_id == 0)
        def _():
            w_acc[...] = jnp.zeros_like(w_acc)
            b_acc[...] = jnp.zeros_like(b_acc)

        for part, source in enumerate((near_ref, far_ref)):
            rows = source[...].reshape(half * length, width)
            these = grad_ref[0, part * half * length : (part + 1) * half * length, :]
            w_acc[...] += dot(rows, these, 0, 0)
        b_acc[0:1, :] += jnp.sum(grad_ref[0].astype(F32), 0, keepdims=True)

        @pl.when(step_id == seqs - 1)
        def _():
            for target, k in ((w_keep, 0), (w_send, 1)):
                for z in range(n_z):
                    row = (2 * z + t.core(k)) * own_rows
                    target[z, :own_rows, :] = w_acc[aligned(row, own_rows), :].astype(BF16)
                    here = (t.s == z).astype(F32)
                    last = lax.broadcasted_iota(jnp.int32, (8, cols3), 0) == 7
                    rows = jnp.where(
                        last, b_acc[0:1, :] * here, narrow_ref[2 * z + t.core(k)]
                    )
                    target[z, own_rows : own_rows + 8, :] = rows.astype(BF16)
                    target[z, own_rows + 8 :, :] = jnp.zeros((PAD - 8, cols3), BF16)
                if k == 0:
                    for r in range(n):
                        rows = wide_ref[r].astype(BF16)
                        target[t.member(r, t.c), own_rows + 8 :, :span] = rows

    block = pl.BlockSpec((half, 1, length, width), lambda g, t: (0, g, 0, 0))
    w_out = (n_z, own_rows + PAD, cols3)
    return call(
        kernel,
        table,
        [near, far, grad, narrow, wide],
        [
            block,
            block,
            pl.BlockSpec((1, total, cols3), lambda g, t: (g, 0, 0)),
            whole_block(narrow.shape),
            whole_block(wide.shape),
        ],
        [shape(w_out), shape(w_out)],
        [whole_block(w_out), whole_block(w_out)],
        (seqs,),
        [pltpu.VMEM((width, cols3), F32), pltpu.VMEM((8, cols3), F32)],
        8,
        "head_weights_backward",
    )


def output_norm(plan, table, pieces, where, inputs, vectors, w_out, come, near, far, others):
    n, n_z = plan.n_seq, plan.n_z
    half = n // 2
    tokens, width = inputs.shape
    own_rows = w_out.shape[0]
    cols = width // n
    tile = 128
    n_moves = 2 + 2 * (n_z - 1) * n

    def kernel(t, in_ref, vec_ref, w_ref, come_ref, near_ref, far_ref, on_ref, of_ref, *rest):
        refs, rest = rest[: len(pieces)], rest[len(pieces) :]
        sum_ref, norm_ref, low_ref, full_ref, sems = rest

        def row(z, k):
            return aligned((z * 2 + t.core(k)) * own_rows, own_rows)

        moves = []
        for k, source in enumerate((w_ref, come_ref)):
            at = full_ref.at[row(t.behind(0), k)]
            lanes = source.shape[1] - width
            moves.append((source.at[pl.ds(0, own_rows), pl.ds(lanes, width)], at))
        for k, (first, second) in enumerate(((near_ref, far_ref), (on_ref, of_ref))):
            for j in range(1, n_z):
                for r in range(n):
                    source = first if r < half else second
                    at = full_ref.at[
                        row(t.behind(j), k),
                        aligned(t.member(r, t.core(k)) * cols, cols),
                    ]
                    moves.append((source.at[r % half, j - 1], at))
        copies = copies_of(moves, sems)
        for copy in copies:
            copy.start()
        for copy in copies:
            copy.wait()

        def each_tile(i, carry):
            rows = aligned(i * tile, tile)
            total = in_ref[rows, :].astype(F32) + vec_ref[2:3, :]
            for r, (a, m) in enumerate(where):
                weights = full_ref[aligned(t.member(r, t.c) * cols, cols), :]
                total += dot(refs[a][m, rows, :], weights)
            unit, _ = statistics(total)
            normed = unit * vec_ref[3:4, :] + vec_ref[4:5, :]
            sum_ref[rows, :] = total
            norm_ref[rows, :] = normed
            low_ref[rows, :] = normed.astype(BF16)
            return carry

        lax.fori_loop(0, tokens // tile, each_tile, 0)

    full = (tokens, width)
    return call(
        kernel,
        table,
        [inputs, vectors, w_out, come, near, far, *others, *pieces],
        [whole_block(full), whole_block(vectors.shape)]
        + [ANY] * 6
        + [whole_block(p.shape) for p in pieces],
        [shape(full, F32), shape(full, F32), shape(full), shape((width, width))],
        [whole_block(full)] * 3 + [whole_block((width, width))],
        (1,),
        [pltpu.SemaphoreType.DMA((n_moves,))],
        7,
        "output_norm",
    )


def flatten(remote):
    arrays, found = [], []
    for near, far in remote:
        found += [(len(arrays), i) for i in range(near.shape[1])]
        arrays += [near, far]
    return arrays, found


def gelu_parts(v):
    big = 0.5 + 0.5 * lax.erf(v * np.float32(np.sqrt(0.5)))
    small = jnp.exp(-0.5 * v * v) * np.float32(1.0 / np.sqrt(2.0 * np.pi))
    return v * big, big + v * small


def up_forward(plan, table, low, other_low, w_up, come, remote, bias):
    n, n_z = plan.n_seq, plan.n_z
    half = n // 2
    tokens, width = low.shape
    own_rows, hidden = w_up.shape
    quarter = hidden // 2 // n
    n_moves = 2 + n_z - 1
    tile = 128

    remote, found = flatten(remote)

    def kernel(t, low_ref, other_ref, up_ref, come_ref, bias_ref, *rest):
        remote_refs, rest = rest[: len(remote)], rest[len(remote) :]
        act_ref, slope_ref, w_hbm, w, sems, out_sem = rest
        step_id = pl.program_id(0)

        def moves(r):
            member = t.member(r, t.c)
            z = t.behind(0)
            at = w.at[r]

            def row(k):
                return aligned((z * 2 + t.core(k)) * own_rows, own_rows)

            lanes = aligned((member * 2 + t.c) * quarter, quarter)
            out = [(up_ref.at[:, lanes], at.at[row(0)])]
            lanes = aligned(member * quarter, quarter)
            out.append((come_ref.at[pl.ds(0, own_rows), lanes], at.at[row(1)]))
            for j in range(1, n_z):
                z_j = t.behind(j)
                a, i = found[j - 1]
                source = remote_refs[a + (r >= half)]
                for k in range(2):
                    rows = aligned((z_j * 2 + t.core(k)) * own_rows, own_rows)
                    out.append(
                        (
                            source.at[r % half, i, pl.ds(k * own_rows, own_rows)],
                            at.at[rows],
                        )
                    )
            return out

        def copies(r):
            return copies_of(moves(r), sems.at[r])

        @pl.when(step_id == 0)
        def _():
            for r in range(n):
                for copy in copies(r):
                    copy.start()

        for r in range(n):

            @pl.when(step_id == r)
            def _(r=r):
                for copy in copies(r):
                    copy.wait()

        def out_copy(r):
            return pltpu.make_async_copy(w.at[r], w_hbm.at[r], out_sem.at[r])

        for r in range(n):

            @pl.when(step_id == r)
            def _(r=r):
                out_copy(r).start()

        weights = w.at[step_id]
        for part, source in enumerate((low_ref, other_ref)):

            def step(i, carry, part=part, source=source):
                rows = pl.ds(pl.multiple_of(i * tile, tile), tile)
                pre = dot(source[rows, :], weights[...]) + bias_ref[0]
                active, slope = gelu_parts(pre)
                rows = pl.ds(pl.multiple_of(part * tokens + i * tile, tile), tile)
                act_ref[0, rows, :] = active.astype(BF16)
                slope_ref[0, rows, :] = slope.astype(BF16)
                return carry

            lax.fori_loop(0, tokens // tile, step, 0)

        @pl.when(step_id == n - 1)
        def _():
            for r in range(n):
                out_copy(r).wait()

    big = (n, 2 * tokens, quarter)
    block = pl.BlockSpec((1, 2 * tokens, quarter), lambda r, t: (r, 0, 0))
    return call(
        kernel,
        table,
        [low, other_low, w_up, come, bias] + remote,
        [whole_block(low.shape)] * 2
        + [ANY] * 2
        + [
            pl.BlockSpec(
                (1, 1, quarter),
                lambda r, t: (2 * t.member(r, t.c) + t.c, 0, 0),
            )
        ]
        + [ANY] * len(remote),
        [shape(big), shape(big), shape((n, width, quarter))],
        [block, block, ANY],
        (n,),
        [
            pltpu.VMEM((n, width, quarter), BF16),
            pltpu.SemaphoreType.DMA((n, 2 + 2 * (n_z - 1))),
            pltpu.SemaphoreType.DMA((n,)),
        ],
        15,
        "up_forward",
    )


def down_forward(plan, table, active, w_down, remote):
    n, n_z = plan.n_seq, plan.n_z
    half = n // 2
    tokens = active.shape[1] // 2
    quarter = active.shape[2]
    own_hidden, width = w_down.shape
    cols = width // n

    remote, found = flatten(remote)

    def kernel(t, act_ref, down_ref, *rest):
        remote_refs, rest = rest[: len(remote)], rest[len(remote) :]
        own_ref, other_ref, w_hbm, w, acc, sems, out_sem = rest
        step_id = pl.program_id(0)
        out_copy = pltpu.make_async_copy(w, w_hbm, out_sem)

        @pl.when(step_id == 0)
        def _():
            moves = [
                (down_ref, w.at[aligned(t.behind(0) * own_hidden, own_hidden)])
            ]
            for j in range(1, n_z):
                rows = aligned(t.behind(j) * own_hidden, own_hidden)
                a, i = found[j - 1]
                for r in range(n):
                    source = remote_refs[a + (r >= half)]
                    lanes = aligned(t.member(r, t.c) * cols, cols)
                    moves.append((source.at[r % half, i], w.at[rows, lanes]))
            copies = copies_of(moves, sems)
            for copy in copies:
                copy.start()
            acc[...] = jnp.zeros_like(acc)
            for copy in copies:
                copy.wait()
            out_copy.start()

        rows = aligned(t.member(step_id, t.c) * quarter, quarter)
        acc[...] += dot(act_ref[0], w[rows, :])

        @pl.when(step_id == n - 1)
        def _():
            own_ref[...] = acc[:tokens, :]
            other_ref[...] = acc[tokens:, :].astype(BF16)
            out_copy.wait()

    full = (tokens, width)
    return call(
        kernel,
        table,
        [active, w_down] + remote,
        [pl.BlockSpec((1, 2 * tokens, quarter), lambda r, t: (r, 0, 0))]
        + [ANY] * (1 + len(remote)),
        [shape(full, F32), shape(full), shape((n * quarter, width))],
        [whole_block(full), whole_block(full), ANY],
        (n,),
        [
            pltpu.VMEM((n * quarter, width), BF16),
            pltpu.VMEM((2 * tokens, width), F32),
            pltpu.SemaphoreType.DMA((1 + (n_z - 1) * n,)),
            pltpu.SemaphoreType.DMA,
        ],
        10,
        "down_forward",
    )


def norm_two(table, normed, own, come, cotangent, vectors):
    tokens, width = normed.shape
    tile = 128

    def kernel(t, norm_ref, own_ref, come_ref, cot_ref, vec_ref, *rest):
        out_ref, grad_ref, low_ref, sums = rest

        @pl.when(pl.program_id(0) == 0)
        def _():
            sums[...] = jnp.zeros_like(sums)

        second = norm_ref[...] + (own_ref[...] + come_ref[...].astype(F32) + vec_ref[5:6, :])
        unit, root = statistics(second)
        gain = vec_ref[6:7, :]
        out_ref[...] = (unit * gain + vec_ref[7:8, :]).astype(BF16)
        above = cot_ref[...].astype(F32)
        grad = norm_back(unit, root, gain, above)
        low = grad.astype(BF16)
        grad_ref[...] = grad
        low_ref[...] = low
        add_rows(sums, 0, low.astype(F32))
        add_rows(sums, 1, above * unit)
        add_rows(sums, 2, above)

    block = pl.BlockSpec((tile, width), lambda i, t: (i, 0))
    full = (tokens, width)
    return call(
        kernel,
        table,
        [normed, own, come, cotangent, vectors],
        [block] * 4 + [whole_block(vectors.shape)],
        [shape(full), shape(full, F32), shape(full), shape((8, width), F32)],
        [block] * 3 + [whole_block((8, width))],
        (tokens // tile,),
        [],
        6,
        "norm_two",
    )


def ffn_backward(plan, table, low, other_low, w_down, w_up, slope):
    n = plan.n_seq
    tokens, width = low.shape
    quarter = slope.shape[2]

    def kernel(t, low_ref, other_ref, down_ref, up_ref, slope_ref, *rest):
        pre_ref, sum_ref, own_ref, come_ref, acc = rest
        step_id = pl.program_id(0)

        @pl.when(step_id == 0)
        def _():
            acc[...] = jnp.zeros_like(acc)

        sums = jnp.zeros((1, quarter), F32)
        for part, source in enumerate((low_ref, other_ref)):
            rows = pl.ds(part * tokens, tokens)
            grad = dot(source[...], down_ref[...], 1, 1) * slope_ref[0, rows, :].astype(F32)
            grad = grad.astype(BF16)
            pre_ref[0, rows, :] = grad
            sums += jnp.sum(grad.astype(F32), 0, keepdims=True)
            acc[rows, :] += dot(grad, up_ref[0], 1, 1)
        row = lax.broadcasted_iota(jnp.int32, (8, quarter), 0)
        sum_ref[0] = jnp.where(row == 0, sums, 0.0)

        @pl.when(step_id == n - 1)
        def _():
            own_ref[...] = acc[:tokens, :]
            come_ref[...] = acc[tokens:, :].astype(BF16)

    big = pl.BlockSpec((1, 2 * tokens, quarter), lambda r, t: (r, 0, 0))
    full = (tokens, width)
    return call(
        kernel,
        table,
        [low, other_low, w_down, w_up, slope],
        [whole_block(full)] * 2
        + [
            pl.BlockSpec((quarter, width), lambda r, t: (t.member(r, t.c), 0)),
            pl.BlockSpec((1, width, quarter), lambda r, t: (r, 0, 0)),
            big,
        ],
        [shape(slope.shape), shape((n, 8, quarter), F32), shape(full, F32), shape(full)],
        [
            big,
            pl.BlockSpec((1, 8, quarter), lambda r, t: (r, 0, 0)),
            whole_block(full),
            whole_block(full),
        ],
        (n,),
        [pltpu.VMEM((2 * tokens, width), F32)],
        13,
        "ffn_backward",
    )


def down_weights(plan, table, active, low, other_low, base):
    n, n_z = plan.n_seq, plan.n_z
    half = n // 2
    tokens, width = low.shape
    quarter = active.shape[2]
    cols = width // n

    def kernel(t, act_ref, low_ref, other_ref, out_ref, grads):
        @pl.when(pl.program_id(0) == 0)
        def _():
            for r in range(half):
                lanes = aligned(t.member(base + r, t.c) * cols, cols)
                here = pl.ds(r * cols, cols)
                grads[:tokens, here] = low_ref[:, lanes]
                grads[tokens:, here] = other_ref[:, lanes]

        total = dot(act_ref[0], grads[...], 0, 0)
        for r in range(half):
            out_ref[r, 0] = total[:, r * cols : (r + 1) * cols].astype(BF16)

    return call(
        kernel,
        table,
        [active, low, other_low],
        [pl.BlockSpec((1, 2 * tokens, quarter), lambda r, t: (r, 0, 0))]
        + [whole_block((tokens, width))] * 2,
        [shape((half, n_z, quarter, cols))],
        [
            pl.BlockSpec(
                (half, 1, quarter, cols), lambda r, t: (0, t.member(r, t.c), 0, 0)
            )
        ],
        (n,),
        [pltpu.VMEM((2 * tokens, half * cols), BF16)],
        5,
        "down_weights",
    )[0]


def up_weights(plan, table, low, other_low, grad_pre, base):
    n, n_z = plan.n_seq, plan.n_z
    half = n // 2
    tokens, width = low.shape
    quarter = grad_pre.shape[2]
    own_rows = width // plan.n_dp

    def kernel(t, low_ref, other_ref, grad_ref, out_ref):
        for z in range(n_z):
            lanes = pl.ds(2 * z * own_rows, 2 * own_rows)
            total = dot(low_ref[:, lanes], grad_ref[0, :tokens, :], 0, 0)
            total += dot(other_ref[:, lanes], grad_ref[0, tokens:, :], 0, 0)
            total = total.astype(BF16)
            out_ref[0, z, :, :quarter] = total[:own_rows]
            out_ref[0, z, :, quarter:] = total[own_rows:]

    dims = (half, n_z, own_rows, 2 * quarter)
    return call(
        kernel,
        table,
        [low, other_low, grad_pre],
        [whole_block((tokens, width))] * 2
        + [pl.BlockSpec((1, 2 * tokens, quarter), lambda i, t: (base + i, 0, 0))],
        [shape(dims)],
        [pl.BlockSpec((1,) + dims[1:], lambda i, t: (i, 0, 0, 0))],
        (half,),
        [],
        6,
        "up_weights",
    )[0]


def norm_one_back(plan, table, grad_second, own, come, first_sum, vectors, w_out, sums_two):
    n = plan.n_seq
    tokens, width = own.shape
    cols = width // n
    tile = 128

    own_rows = width // plan.n_dp

    def kernel(t, grad_ref, own_ref, come_ref, sum_ref, vec_ref, w_ref, two_ref, *rest):
        first_ref, low_ref, narrow_ref = rest[:3]
        keep_ref, send_ref, sums = rest[3:]
        sums[0:3, :] = jnp.zeros((3, width), F32)
        sums[3:6, :] = two_ref[0:3, :]
        sums[6:8, :] = jnp.zeros((2, width), F32)

        def each_tile(i, carry):
            rows = aligned(i * tile, tile)
            above = grad_ref[rows, :] + (own_ref[rows, :] + come_ref[rows, :].astype(F32))
            unit, root = statistics(sum_ref[rows, :])
            grad = norm_back(unit, root, vec_ref[3:4, :], above)
            low = grad.astype(BF16)
            first_ref[rows, :] = grad
            low_ref[rows, :] = low
            add_rows(sums, 0, low.astype(F32))
            add_rows(sums, 1, above * unit)
            add_rows(sums, 2, above)
            for r in range(n):
                weights = w_ref[aligned(t.member(r, t.c) * cols, cols), :]
                target = keep_ref if r < half else send_ref
                target[r % half, rows, :] = dot(low, weights, 1, 1).astype(BF16)
            return carry

        lax.fori_loop(0, tokens // tile, each_tile, 0)
        narrow_ref[...] = jnp.zeros_like(narrow_ref)
        for owner in range(plan.n_dp):
            lanes = pl.ds(owner * own_rows, own_rows)
            narrow_ref[owner, :, 0:own_rows] = sums[:, lanes]

    full = (tokens, width)
    half = n // 2
    part = (half, tokens, cols)
    narrow = (plan.n_dp, 8, 3 * cols)
    return call(
        kernel,
        table,
        [grad_second, own, come, first_sum, vectors, w_out, sums_two],
        [whole_block(full)] * 4
        + [whole_block(v.shape) for v in (vectors, w_out, sums_two)],
        [shape(full, F32), shape(full), shape(narrow, F32)] + [shape(part)] * 2,
        [whole_block(full)] * 2 + [whole_block(narrow)] + [whole_block(part)] * 2,
        (1,),
        [pltpu.VMEM((8, width), F32)],
        8,
        "norm_one_back",
    )


def out_weights(plan, table, pieces, where, low):
    n, n_z = plan.n_seq, plan.n_z
    tokens, width = low.shape
    cols = width // n
    own_rows = width // plan.n_dp

    def kernel(t, low_ref, *rest):
        refs, (keep_ref, send_ref, both) = rest[: len(pieces)], rest[len(pieces) :]
        for r, (a, m) in enumerate(where):
            z = t.member(r, t.c)
            both[...] = dot(refs[a][m], low_ref[...], 0, 0).astype(BF16)
            for target, k in ((send_ref, 1), (keep_ref, 0)):
                rows = aligned(t.core(k) * own_rows, own_rows)
                for s in range(n):
                    at = aligned(t.member(s, t.core(k)) * cols, cols)
                    target[s, z] = both[rows, at]

    dims = (n, n_z, own_rows, cols)
    return call(
        kernel,
        table,
        [low, *pieces],
        [whole_block(low.shape)] + [whole_block(p.shape) for p in pieces],
        [shape(dims), shape(dims)],
        [whole_block(dims)] * 2,
        (1,),
        [pltpu.VMEM((cols, width), BF16)],
        0,
        "out_weights",
    )


def parts_along_z(plan, table, terms):
    n_z = plan.n_z
    rows = terms[0][0].shape[1]
    operands = [v for group in terms for v in group]
    lanes = sum(group[0].shape[2] for group in terms)

    def kernel(t, *refs):
        sources, outs = refs[: len(operands)], refs[len(operands) :]
        for j in range(n_z):

            @pl.when(pl.program_id(0) == j)
            def _(j=j):
                left, at = list(sources), 0
                target = outs[2 * j // n_z]
                for group in terms:
                    total = left.pop(0)[0].astype(F32)
                    for _ in group[1:]:
                        total += left.pop(0)[0].astype(F32)
                    end = at + total.shape[1]
                    target[j % (n_z // 2), :, at:end] = total.astype(BF16)
                    at = end

    def member(i, t):
        here = 0
        for k in range(plan.z_bits):
            here = here | ((i >> k) & 1) << (plan.z_bits - 1 - k)
        return (t.z ^ here, 0, 0)

    out = (n_z // 2, rows, lanes)
    return call(
        kernel,
        table,
        operands,
        [pl.BlockSpec((1,) + v.shape[1:], member) for v in operands],
        [shape(out)] * 2,
        [whole_block(out)] * 2,
        (n_z,),
        [],
        2,
        "parts_along_z",
    )


def split_by_core(plan, table, pieces, split):
    _, rows, lanes = pieces[0].shape
    half = split // 2
    n_pieces = len(pieces)

    def kernel(t, *refs):
        for k, target in enumerate(refs[n_pieces:]):
            size = half if k < 2 else lanes - split
            at = aligned(t.core(k) * half, half) if k < 2 else pl.ds(split, size)
            total = refs[0][0, :, at].astype(F32)
            for ref in refs[1:n_pieces]:
                total += ref[0, :, at].astype(F32)
            target[...] = total.astype(BF16)

    outs = [(rows, half), (rows, half), (rows, lanes - split)]
    return call(
        kernel,
        table,
        pieces,
        [whole_block(p.shape) for p in pieces],
        [shape(o) for o in outs],
        [whole_block(o) for o in outs],
        (1,),
        [],
        0,
        "split_by_core",
    )


def place(plan, table, near, far, outs, moves, name):
    n = plan.n_seq
    half = n // 2

    def kernel(t, near_ref, far_ref, *targets):
        for r in range(n):
            source = near_ref if r < half else far_ref
            for src, o, at in moves:
                targets[o][:, at(t, r)] = source[(r % half,) + src].astype(F32)

    return call(
        kernel,
        table,
        [near, far],
        [whole_block(near.shape)] * 2,
        [shape(o, F32) for o in outs],
        [whole_block(o) for o in outs],
        (1,),
        [],
        0,
        name,
    )


def local(
    plan,
    inputs,
    w_query,
    w_key,
    w_value,
    b_query,
    b_value,
    w_out,
    b_out,
    gain_one,
    shift_one,
    w_up,
    b_up,
    w_down,
    b_down,
    gain_two,
    shift_two,
    cotangent,
):
    n_dp, n, n_z = plan.n_dp, plan.n_seq, plan.n_z
    half = n // 2
    seqs, length, width = inputs.shape
    tokens = seqs * length
    own_rows, hidden = w_up.shape
    own_hidden = w_down.shape[0]
    cols = width // n
    cols3 = 3 * cols
    quarter = hidden // 2 // n
    assert n == n_z and quarter == own_hidden
    table = plan
    core = lax.axis_index("dp") % 2

    narrow = jnp.stack(
        [b_query, b_value, b_out, gain_one, shift_one, b_down, gain_two, shift_two]
    )
    vec = jnp.concatenate(
        [
            jnp.pad(narrow, ((0, 0), (0, 4 * cols - own_rows))),
            jnp.pad(b_up[None], ((0, 7), (0, 4 * cols - own_hidden))),
        ],
        0,
    )

    def column_block(t):
        return (pl.ds(0, own_rows), aligned(t.s * cols, cols))

    moves = [
        (i, column_block, 0, lambda t, i=i: (pl.ds(0, own_rows), pl.ds(i * cols, cols)))
        for i in range(4)
    ]
    moves.append((4, lambda t: (pl.ds(0, PAD),), 0, lambda t: (pl.ds(own_rows, PAD),)))
    (first,) = assemble(
        table,
        [w_query, w_key, w_value, w_out, vec],
        moves,
        [shape((own_rows + PAD, 4 * cols))],
        "pack_first",
    )

    def straight(block, j):
        return lax.ppermute(block, BOTH, plan.toward[j])

    near_x = inputs[None]
    for k in range(plan.bits - 1):
        near_x = plan.double(near_x, k)
    mine = [first, straight(first, 1)]

    top = plan.bits - 1

    def final(near, *ready):
        return near, lax.ppermute(after(near, *ready), BOTH, plan.stage[top])

    def begin(block, *ready):
        near = after(block, *ready)[None]
        for k in range(top - 1):
            near = plan.double(near, k)
        return near, lax.ppermute(near, BOTH, plan.stage[top - 1])

    def joined(started, *ready):
        return jnp.concatenate([after(started[0], *ready), started[1]], 0)

    def onward(block, *ready):
        return lax.ppermute(after(block, *ready), BOTH, plan.toward[1])

    ready = (near_x, mine[1])
    far_x = final(near_x, *ready)[1]
    mine.append(onward(mine[1], *ready))
    for j in range(3, n_z):
        mine.append(onward(mine[-1]))

    moves = []
    for z in range(n_z):
        moves.append(
            (
                0,
                lambda t, z=z: (
                    pl.ds(0, own_rows),
                    aligned((2 * z + (1 - t.c)) * quarter, quarter),
                ),
                0,
                lambda t, z=z: (pl.ds(0, own_rows), pl.ds(z * quarter, quarter)),
            )
        )
    moves.append(
        (
            1,
            lambda t: (pl.ds(0, own_rows),),
            0,
            lambda t: (pl.ds(0, own_rows), pl.ds(n * quarter, width)),
        )
    )
    (across,) = assemble(
        table,
        [after(w_up, mine[2]), w_out],
        moves,
        [shape((own_rows, n * quarter + width))],
        "pack_across",
    )
    come = plan.swap(across)


    def rows_at(start, size):
        return lambda t: (pl.ds(start, size), pl.ds(0, quarter))

    moves = [
        (
            0,
            lambda t: (
                pl.ds(0, own_rows),
                aligned((2 * t.s + t.c) * quarter, quarter),
            ),
            0,
            rows_at(0, own_rows),
        ),
        (
            1,
            lambda t: (pl.ds(0, own_rows), aligned(t.s * quarter, quarter)),
            0,
            rows_at(own_rows, own_rows),
        ),
    ]
    moves.append(
        (
            2,
            lambda t: (pl.ds(0, own_hidden), aligned(t.s * cols, cols)),
            1,
            lambda t: (pl.ds(0, own_hidden),),
        )
    )
    second, down = assemble(
        table,
        [w_up, come, w_down],
        moves,
        [shape((2 * own_rows, quarter)), shape((own_hidden, cols))],
        "pack_second",
    )
    ups = [onward(second)]

    ready = (far_x, ups[0]) + tuple(mine[1:])
    mine_all = jnp.stack([after(piece, *ready) for piece in mine])
    theirs = plan.swap(mine_all)
    outs = jnp.stack([after(piece, *ready)[:own_rows, cols3:] for piece in mine[1:]])
    outs_started = begin(outs)
    ups.append(onward(ups[0], *ready))
    downs = [onward(down, *ready)]
    w_qkv, vectors, up_bias = head_weights(plan, table, mine_all, theirs)
    qkv, lse = [], []

    def attend(g, before, *ready):
        out, *parts, total = attention_forward(
            plan, table, g, near_x, far_x, w_qkv, after(vectors, *ready), before
        )
        qkv.append(out)
        lse.append(total)
        return parts

    parts = attend(0, [])

    near_out = joined(outs_started, parts[0])
    ready = (near_out, parts[0], ups[1], downs[0])
    outs = final(near_out, *ready)
    ups.append(onward(ups[1], *ready))
    downs.append(onward(downs[0], *ready))
    two_started = begin(jnp.stack([after(piece, *ready) for piece in ups[:2]]))
    parts = attend(1, parts, *ready)

    near_two = joined(two_started, parts[0])
    ready = (near_two, outs[1], ups[2], downs[1], parts[0])
    for j in range(3, n_z - 1):
        ups.append(onward(ups[-1]))
        downs.append(onward(downs[-1]))
    others = [plan.swap(after(part, *ready)) for part in outs]
    up_two = final(near_two, *ready)
    downs.append(onward(downs[-1], *ready))
    three_started = begin(jnp.stack([after(piece, *ready) for piece in ups[2:]]))
    for g in range(2, seqs):
        parts = attend(g, parts, *ready)

    contexts = parts
    send = after(parts[1], up_two[1], three_started[1], *others)
    near_three = joined(three_started, send)
    up_three = final(near_three)
    pieces, where = distinct(plan.exchange(parts[0], send))
    pieces = [p.reshape(p.shape[0], tokens, cols) for p in pieces]
    downs = jnp.stack([after(piece, near_three) for piece in downs])
    downs_started = begin(downs, *pieces)
    first_sum, normed, low, full_out = output_norm(
        plan,
        table,
        pieces,
        where,
        after(inputs.reshape(tokens, width), downs),
        vectors,
        w_out,
        come,
        *outs,
        others,
    )

    other_low = plan.swap(after(low, up_three[1]))
    near_down = joined(downs_started, low)
    ready = (other_low, up_three[1], near_down)
    down_all = final(near_down, *ready)
    active, slope, up_kept = up_forward(
        plan, table, after(low, *ready), other_low, w_up, come, [up_two, up_three], up_bias
    )
    own, away, down_kept = down_forward(plan, table, active, w_down, [down_all])
    output, grad_second, low_two, sums_two = norm_two(
        table, normed, own, plan.swap(away), cotangent.reshape(tokens, width), vectors
    )

    def begun(send, k, *ready):
        return lax.ppermute(after(send, *ready), BOTH, plan.stage[k])

    def summed(keep, come, k, *ready):
        low = (1 << k) // 2
        come = after(come, *ready)
        return add(keep[:low], come[:low]), add(keep[low:], come[low:])

    def middle(keep, come, *ready):
        keep, send = summed(keep, come, top, *ready)
        for k in reversed(range(1, top)):
            keep, send = summed(keep, begun(send, k), k)
        return keep, send

    other_two = plan.swap(low_two)
    down_send = down_weights(plan, table, active, low_two, other_two, half)
    down_come = begun(down_send, top)
    down_keep = down_weights(plan, table, active, after(low_two, down_send), other_two, 0)
    grad_pre, sums_up, own, away = ffn_backward(
        plan, table, after(low_two, down_keep), other_two, down_kept, up_kept, slope
    )
    away = plan.swap(away)
    low = after(low, own)
    up_send = up_weights(plan, table, low, other_low, grad_pre, half)
    down_keep, down_send = middle(down_keep, down_come, up_send)
    down_last = begun(down_send, 0)
    grad_first, low_one, sums, *parts = norm_one_back(
        plan,
        table,
        grad_second,
        after(own, down_send),
        away,
        first_sum,
        vectors,
        full_out,
        sums_two,
    )
    up_keep = up_weights(plan, table, after(low, low_one), other_low, grad_pre, 0)
    parts = [p.reshape(half, seqs, length, cols) for p in parts]
    found = plan.exchange(parts[0], after(parts[1], down_last), up_keep)
    out_keep, out_send = out_weights(
        plan, table, pieces, where, after(low_one, found[half][0])
    )
    parts, up_where = distinct(found)
    parts = [after(part, out_keep) for part in parts]
    out_come = plan.swap(after(out_send, *parts))

    def sent_along_z(terms, *ready):
        terms = [[after(group[0], *ready)] + group[1:] for group in terms]
        keep, send = parts_along_z(plan, table, terms)
        return keep, lax.ppermute(send, BOTH, plan.along[0])

    def on_along_z(keep, come, *ready):
        for way in plan.along[1:]:
            low = keep.shape[0] // 2
            come = after(come, *ready)
            sent = add(keep[low:], come[low:])
            keep = add(keep[:low], come[:low])
            come = lax.ppermute(sent, BOTH, way)
        return keep, come

    def total(keep, come, *ready):
        return add(after(keep, *ready), come)[0]

    def back(g, before, *ready):
        return attention_backward(
            plan,
            table,
            g,
            seqs,
            after(qkv[g], *ready),
            lse[g],
            contexts,
            parts,
            up_where,
            w_qkv,
            before,
        )

    ready = (out_keep, out_come) + tuple(parts)
    up_come = begun(up_send, top, *ready)
    out_come = after(out_come, *ready)
    out_sent = add(out_keep[half:], out_come[half:])
    out_first = begun(out_sent, top)
    out_kept = add(out_keep[:half], out_come[:half])
    shared = back(0, [], out_sent, out_kept, *ready)
    down_along = sent_along_z([[down_keep[0], down_last[0]]], shared[0])
    shared = back(1, list(shared), down_along[0])
    up_keep, up_send = middle(up_keep, up_come, shared[0])
    up_last = begun(up_send, 0)
    down_along = on_along_z(*down_along, up_send)
    out_kept, out_sent = middle(out_kept, out_first, up_send)
    out_last = begun(out_sent, 0)
    for g in range(2, seqs):
        shared = back(g, list(shared), up_send, out_sent, down_along[0])
    grad_qkv, part_keep, part_send = shared
    up_along = sent_along_z(
        [[up_keep[0], up_last[0]], [out_kept[0], out_last[0]]], grad_qkv
    )

    part_come = begun(part_send, top, up_along[0])
    down_started = begin(total(*down_along, up_along[0]))
    last_keep, last_send = head_weights_backward(
        plan, table, near_x, far_x, after(grad_qkv, up_along[0], down_started[0]), sums, sums_up
    )
    down_near = joined(down_started, last_keep)
    down_far = plan.final(down_near)
    up_along = on_along_z(*up_along, last_keep)
    last_come = plan.swap(last_send)
    last_along = sent_along_z([[last_keep, last_come]], up_along[0])
    part_keep, part_send = middle(part_keep, part_come, last_along[0])
    part_last = begun(part_send, 0)

    def lanes(size):
        return lambda t, r: aligned(t.member(r, t.c) * size, size)

    grad_inputs = grad_first.reshape(inputs.shape) + (
        part_keep[0].astype(F32) + part_last[0].astype(F32)
    )
    (grad_down,) = place(
        plan,
        table,
        after(down_near, part_send),
        down_far,
        [(own_hidden, width)],
        [((slice(None),), 0, lanes(cols))],
        "place_down",
    )
    last_along = on_along_z(*last_along, part_last, grad_down)
    up_along = (after(up_along[0], last_along[0]), up_along[1])
    up_kept, up_sent, grad_out = split_by_core(plan, table, up_along, 2 * quarter)
    up_come = plan.swap(up_sent)
    up_near = plan.halfway(jnp.concatenate([up_kept, up_come, grad_out], 1))
    up_far = plan.final(up_near)
    grad_inputs = grad_first.reshape(inputs.shape) + (
        part_keep[0].astype(F32) + after(part_last[0], up_near).astype(F32)
    )
    last_near = plan.halfway(total(*last_along, grad_inputs))
    last_far = plan.final(last_near)
    grad_up, grad_out = place(
        plan,
        table,
        after(up_near, last_near),
        up_far,
        [(own_rows, hidden), (own_rows, width)],
        [
            (
                (slice(None), pl.ds(k * quarter, quarter)),
                0,
                lambda t, r, k=k: aligned(
                    (2 * t.member(r, t.c) + t.core(k)) * quarter, quarter
                ),
            )
            for k in range(2)
        ]
        + [((slice(None), pl.ds(2 * quarter, cols)), 1, lanes(cols))],
        "place_up",
    )
    grad_wq, grad_wk, grad_wv = place(
        plan,
        table,
        last_near,
        last_far,
        [(own_rows, width)] * 3,
        [
            ((pl.ds(0, own_rows), pl.ds(m * cols, cols)), m, lanes(cols))
            for m in range(3)
        ],
        "place_heads",
    )
    vec_out = jnp.sum(last_near[:, own_rows:].astype(F32), 0)
    vec_out += jnp.sum(last_far[:, own_rows:].astype(F32), 0)
    biases = vec_out[7].reshape(3, 2, own_rows)
    biases = jnp.where(core == 0, biases[:, 0], biases[:, 1])
    return (
        output.reshape(inputs.shape),
        grad_inputs,
        grad_wq,
        grad_wk,
        grad_wv,
        biases[0],
        biases[2],
        grad_out,
        vec_out[0, :own_rows],
        vec_out[1, :own_rows],
        vec_out[2, :own_rows],
        grad_up,
        vec_out[8, :own_hidden],
        grad_down,
        vec_out[3, :own_rows],
        vec_out[4, :own_rows],
        vec_out[5, :own_rows],
    )


def solution(mesh):
    plan = Plan(mesh.shape["dp"], mesh.shape["seq"])
    rows, vector, token = P("dp", None), P("dp"), P("dp", "seq", None)
    weights = (rows,) * 3 + (vector,) * 2 + (rows,) + (vector,) * 3
    weights += (rows, vector, rows) + (vector,) * 3
    return jax.shard_map(
        functools.partial(local, plan),
        mesh=mesh,
        in_specs=(token,) + weights + (token,),
        out_specs=(token, token) + weights,
        check_vma=False,
    )
```

```python
import functools

import jax
import jax.numpy as jnp
import numpy as np
from jax import lax
from jax.experimental import pallas as pl
from jax.experimental.pallas import tpu as pltpu
from jax.sharding import PartitionSpec as P

HEAD_DIM = 64
PAIR = 2 * HEAD_DIM
EPSILON = 1e-12
BOTH = ("dp", "seq")
PAD = 16
MICROSECOND = 600_000_000
F32 = jnp.float32
BF16 = jnp.bfloat16
ANY = pl.BlockSpec(memory_space=pl.ANY)


def dot(former, latter, former_dim=1, latter_dim=0):
    return lax.dot_general(
        former,
        latter,
        (((former_dim,), (latter_dim,)), ((), ())),
        preferred_element_type=F32,
    )


class Plan:
    def __init__(self, n_dp, n_seq):
        self.n_dp, self.n_seq, self.n_z = n_dp, n_seq, n_dp // 2
        self.bits = n_seq.bit_length() - 1
        order = [0] + list(range(1, self.n_z, 2))
        order += list(range(2, self.n_z, 2))[::-1]
        self.order = order
        self.place = [order.index(z) for z in range(self.n_z)]
        self.core = self.pairs(lambda z, c, s: (z, 1 - c, s))
        self.toward = [
            self.pairs(lambda z, c, s, j=j: (self.behind(z, -j), c, s))
            for j in range(self.n_z)
        ]
        self.z_bits = self.n_z.bit_length() - 1
        self.along = [
            self.pairs(lambda z, c, s, k=k: (z ^ 1 << k, c, s)) for k in range(self.z_bits)
        ]
        self.across = [
            self.pairs(lambda z, c, s, r=r: (z, c, s ^ self.mask(c, r)))
            for r in range(n_seq)
        ]
        self.stage = [
            self.pairs(lambda z, c, s, k=k: (z, c, s ^ self.mask(c, 1 << k)))
            for k in range(self.bits)
        ]
    def behind(self, z, j):
        return self.order[(self.place[z] - j) % self.n_z]

    def mask(self, c, r):
        out = 0
        for k in range(self.bits):
            if r >> k & 1:
                out |= 1 << ((k + c) % self.bits)
        return out

    def pairs(self, target):
        out = []
        for dp in range(self.n_dp):
            for s in range(self.n_seq):
                z, c, t = target(dp // 2, dp % 2, s)
                out.append((dp * self.n_seq + s, (2 * z + c) * self.n_seq + t))
        return out

    def swap(self, block):
        return lax.ppermute(block, BOTH, self.core)

    def trade(self, blocks):
        return [blocks[0]] + [
            lax.ppermute(block, BOTH, way) for block, way in zip(blocks[1:], self.across[1:])
        ]

    def exchange(self, keep, send, *ready):
        held = [(0, keep, 0)]
        for k in reversed(range(self.bits)):
            come = after(lax.ppermute(send, BOTH, self.stage[k]), *ready)
            width, ready = 1 << k, ()
            held = held + [
                (mask | width, come, i * width) for i, (mask, _, _) in enumerate(held)
            ]
            if k:
                low = width // 2
                send = jnp.concatenate([a[i + low : i + width] for _, a, i in held], 0)
        return [(a, i) for _, a, i in sorted(held, key=lambda item: item[0])]

    def gather(self, block):
        near = block[None]
        for k in range(self.bits - 1):
            near = self.double(near, k)
        return near, lax.ppermute(near, BOTH, self.stage[self.bits - 1])

    def halfway(self, block, *ready):
        near = after(block, *ready)[None]
        for k in range(self.bits - 1):
            near = self.double(near, k)
        return near

    def final(self, near, *ready):
        return lax.ppermute(after(near, *ready), BOTH, self.stage[self.bits - 1])

    def double(self, near, k):
        return jnp.concatenate([near, lax.ppermute(near, BOTH, self.stage[k])], 0)


def add(former, latter):
    return (former.astype(F32) + latter.astype(F32)).astype(BF16)


def after(value, *others):
    return lax.optimization_barrier((value,) + others)[0]


class Here:
    def __init__(self, plan):
        self.plan = plan
        dp = lax.axis_index("dp")
        self.z, self.c, self.s = lax.div(dp, 2), lax.rem(dp, 2), lax.axis_index("seq")

    def core(self, k):
        return self.c if k == 0 else 1 - self.c

    def behind(self, j):
        n = self.plan.n_z
        half = lax.div(self.z, 2)
        odd = lax.rem(self.z, 2)
        place = jnp.where(odd == 1, half + 1, lax.rem(n - half, n))
        at = lax.rem(place - j + n, n)
        return jnp.where(at <= n // 2, jnp.maximum(2 * at - 1, 0), 2 * (n - at))

    def member(self, r, core):
        n, bits = self.plan.n_seq, self.plan.bits
        turned = ((r << 1) & (n - 1)) | (r >> (bits - 1))
        return self.s ^ (r + core * (turned - r))


def shape(dims, dtype=BF16):
    return jax.ShapeDtypeStruct(tuple(dims), dtype)


def distinct(found):
    arrays = []
    for array, _ in found:
        if not any(array is other for other in arrays):
            arrays.append(array)
    at = [([array is other for other in arrays].index(True), i) for array, i in found]
    return arrays, at


def turned(i, bits):
    return sum((i >> k & 1) << (bits - 1 - k) for k in range(bits))


def aligned(start, size):
    return pl.ds(pl.multiple_of(start, size), size)


def whole_block(dims):
    return pl.BlockSpec(tuple(dims), lambda *_: (0,) * len(dims))


def call(
    kernel, plan, operands, in_specs, outs, out_specs, grid, scratch, micros, name, alias=None
):
    size = sum(int(np.prod(o.shape)) * o.dtype.itemsize for o in list(operands) + list(outs))
    size = size if micros else 0

    def placed(spec):
        if spec.index_map is None:
            return spec
        return pl.BlockSpec(spec.block_shape, lambda *i: spec.index_map(*i, Here(plan)))

    return pl.pallas_call(
        lambda *refs: kernel(Here(plan), *refs),
        out_shape=list(outs),
        grid=grid,
        in_specs=[placed(spec) for spec in in_specs],
        out_specs=[placed(spec) for spec in out_specs],
        scratch_shapes=scratch,
        cost_estimate=pl.CostEstimate(
            flops=micros * MICROSECOND, bytes_accessed=size, transcendentals=0
        ),
        input_output_aliases=alias or {},
        name=name,
    )(*operands)


def assemble(table, pieces, moves, outs, name):
    def kernel(table_ref, *refs):
        sources, targets, sems = refs[: len(pieces)], refs[len(pieces) : -1], refs[-1]
        copies = [
            pltpu.make_async_copy(
                sources[i].at[src(table_ref)], targets[o].at[at(table_ref)], sems.at[n]
            )
            for n, (i, src, o, at) in enumerate(moves)
        ]
        for copy in copies:
            copy.start()
        for copy in copies:
            copy.wait()

    return call(
        kernel,
        table,
        pieces,
        [ANY] * len(pieces),
        outs,
        [whole_block(o.shape) for o in outs],
        (1,),
        [pltpu.SemaphoreType.DMA((len(moves),))],
        0,
        name,
    )


def copies_of(moves, sems):
    return [pltpu.make_async_copy(src, at, sems.at[n]) for n, (src, at) in enumerate(moves)]


def lanes_of(half):
    lane = lax.broadcasted_iota(jnp.int32, (1, PAIR), 1)
    return lane < HEAD_DIM if half == 0 else lane >= HEAD_DIM


def only(block, half):
    return jnp.where(lanes_of(half), block, jnp.zeros_like(block))


def statistics(hidden):
    center = hidden - jnp.mean(hidden, -1, keepdims=True)
    spread = jnp.mean(center * center, -1, keepdims=True)
    root = lax.rsqrt(spread + EPSILON)
    return center * root, root


def norm_back(unit, root, gain_vec, upstream):
    scaled = upstream * gain_vec
    first = jnp.mean(scaled, -1, keepdims=True)
    second = jnp.mean(scaled * unit, -1, keepdims=True)
    return root * (scaled - first - unit * second)


def add_rows(target, row, value):
    target[row : row + 1, :] += jnp.sum(value, 0, keepdims=True)


def head_weights(plan, table, mine, theirs):
    n_z, n_dp = plan.n_z, plan.n_dp
    rows, lanes = mine.shape[1:]
    own_rows, cols3 = rows - PAD, lanes // 4 * 3
    width, span = n_dp * own_rows, lanes // 2

    def kernel(t, mine_ref, theirs_ref, w_ref, vec_ref, bias_ref, held, sems):
        moves = []
        for k, source in enumerate((mine_ref, theirs_ref)):
            for j in range(n_z):
                owner = 2 * t.behind(j) + t.core(k)
                moves.append((source.at[j, pl.ds(own_rows, PAD)], held.at[owner]))
                moves.append(
                    (
                        source.at[j, pl.ds(0, own_rows), pl.ds(0, cols3)],
                        w_ref.at[aligned(owner * own_rows, own_rows)],
                    )
                )
        copies = copies_of(moves, sems)
        for copy in copies:
            copy.start()
        for copy in copies:
            copy.wait()
        for owner in range(n_dp):
            values = held[owner].astype(F32)
            at = pl.ds(owner * own_rows, own_rows)
            vec_ref[:, at] = values[:8, :own_rows]
            bias_ref[owner] = values[8:9, :span]

    outs = [shape((width, cols3)), shape((8, width), F32), shape((n_dp, 1, span), F32)]
    return call(
        kernel,
        table,
        [mine, theirs],
        [ANY] * 2,
        outs,
        [whole_block(o.shape) for o in outs],
        (1,),
        [pltpu.VMEM((n_dp, PAD, lanes), BF16), pltpu.SemaphoreType.DMA((4 * n_z,))],
        3,
        "head_weights",
    )


def attention_forward(plan, table, g, near, far, weights, vectors, before):
    n = plan.n_seq
    half, seqs, length, width = near.shape
    n_before = len(before)
    cols3 = weights.shape[1]
    cols = cols3 // 3
    total = n * length
    tile, chunk = min(512, total), min(256, total)
    lse = (cols // PAIR, 8, total)
    scale = HEAD_DIM**-0.5

    def kernel(t, near_ref, far_ref, w_ref, vec_ref, *rest):
        qkv_ref, keep_ref, send_ref, lse_ref, context = rest[n_before:]
        here = aligned(t.s * cols, cols)
        bias = jnp.concatenate(
            [vec_ref[0:1, here], jnp.zeros((1, cols), F32), vec_ref[1:2, here]], 1
        )
        for part, source in enumerate((near_ref, far_ref)):
            rows = source[...].reshape(half * length, width)
            out = dot(rows, w_ref[...]) + bias
            qkv_ref[part * half * length : (part + 1) * half * length, :] = out.astype(BF16)
        def each_pair(pair, carry):
            q_at = aligned(pair * PAIR, PAIR)
            k_at = aligned(cols + pair * PAIR, PAIR)
            value = qkv_ref[:, aligned(2 * cols + pair * PAIR, PAIR)]
            value = value.astype(F32).T.astype(BF16)

            def each_tile(i, carry):
                rows = aligned(i * tile, tile)
                query = qkv_ref[rows, q_at] * jnp.asarray(scale, BF16)
                out = []
                for head in range(2):
                    one = only(query, head)

                    def scores(c):
                        return dot(qkv_ref[pl.ds(c * chunk, chunk), k_at], one, 1, 1)

                    top = None
                    for c in range(total // chunk):
                        here = jnp.max(scores(c), 0, keepdims=True)
                        top = here if c == 0 else jnp.maximum(top, here)
                    for c in range(total // chunk):
                        exponent = jnp.exp(scores(c) - top)
                        here = jnp.sum(exponent, 0, keepdims=True)
                        these = value[
                            head * HEAD_DIM : (head + 1) * HEAD_DIM,
                            c * chunk : (c + 1) * chunk,
                        ]
                        part = dot(these, exponent.astype(BF16))
                        bottom = here if c == 0 else bottom + here
                        acc = part if c == 0 else acc + part
                    out.append(acc * (1.0 / bottom))
                    lse_ref[pair, head : head + 1, rows] = top + jnp.log(bottom)
                context[rows, q_at] = jnp.concatenate(out, 0).T.astype(BF16)
                return carry

            lax.fori_loop(0, total // tile, each_tile, 0)
            return carry

        lax.fori_loop(0, cols // PAIR, each_pair, 0)
        for r in range(n):
            target = keep_ref if r < half else send_ref
            target[r % half, 0] = context[r * length : (r + 1) * length, :]

    block = pl.BlockSpec((half, 1, length, width), lambda i, t: (0, g, 0, 0))
    return call(
        kernel,
        table,
        [near, far, weights, vectors] + before,
        [block, block, whole_block(weights.shape), whole_block(vectors.shape)]
        + [ANY] * n_before,
        [shape((total, cols3))]
        + [shape((half, seqs, length, cols))] * 2
        + [shape(lse, F32)],
        [whole_block((total, cols3))]
        + [pl.BlockSpec((half, 1, length, cols), lambda i, t: (0, g, 0, 0))] * 2
        + [whole_block(lse)],
        (1,),
        [pltpu.VMEM((total, cols), BF16)],
        6,
        "attention_forward",
        {4 + i: 1 + i for i in range(n_before)},
    )


def attention_backward(
    plan, table, g, seqs, qkv, lse, contexts, upstream, where, w_qkv, before
):
    n = plan.n_seq
    half = n // 2
    width, cols3 = w_qkv.shape
    cols = cols3 // 3
    total = qkv.shape[0]
    length = total // n
    tile, chunk = min(512, total), min(256, total)
    scale = HEAD_DIM**-0.5
    n_before, n_up = len(before), len(upstream)

    def kernel(t, qkv_ref, w_ref, lse_ref, near_ref, far_ref, *rest):
        up_refs, rest = rest[:n_up], rest[n_up + n_before :]
        grad_ref, part_keep, part_send = rest[:3]
        up, context, key_acc, value_acc = rest[3:]
        for r, (a, i) in enumerate(where):
            rows = pl.ds(r * length, length)
            up[rows, :] = up_refs[a][i, 0]
            context[rows, :] = (near_ref if r < half else far_ref)[r % half, 0]
        def each_pair(pair, carry):
            q_at = aligned(pair * PAIR, PAIR)
            k_at = aligned(cols + pair * PAIR, PAIR)
            v_at = aligned(2 * cols + pair * PAIR, PAIR)
            value_acc[...] = jnp.zeros_like(value_acc)
            key_acc[...] = jnp.zeros_like(key_acc)

            turned_key = qkv_ref[:, k_at].astype(F32).T.astype(BF16)

            def each_tile(i, carry):
                rows = aligned(i * tile, tile)
                query = qkv_ref[rows, q_at] * jnp.asarray(scale, BF16)
                above = up[rows, q_at]
                both = (above.astype(F32) * context[rows, q_at].astype(F32)).T
                out = []
                for head in range(2):
                    lanes = slice(head * HEAD_DIM, (head + 1) * HEAD_DIM)
                    inner = jnp.sum(both[lanes], 0, keepdims=True)
                    log_total = lse_ref[pair, head : head + 1, rows]
                    one, upper = only(query, head), only(above, head)
                    for c in range(total // chunk):
                        here = pl.ds(c * chunk, chunk)
                        portions = jnp.exp(dot(qkv_ref[here, k_at], one, 1, 1) - log_total)
                        slope = dot(qkv_ref[here, v_at], upper, 1, 1)
                        slope = (portions * (slope - inner)).astype(BF16)
                        value_acc[here, :] += dot(portions.astype(BF16), upper)
                        key_acc[here, :] += dot(slope, one)
                        these = turned_key[lanes, c * chunk : (c + 1) * chunk]
                        part = dot(these, slope)
                        acc = part if c == 0 else acc + part
                    out.append(acc * scale)
                grad_ref[0, rows, q_at] = jnp.concatenate(out, 0).T.astype(BF16)
                return carry

            lax.fori_loop(0, total // tile, each_tile, 0)
            grad_ref[0, :, k_at] = key_acc[...].astype(BF16)
            grad_ref[0, :, v_at] = value_acc[...].astype(BF16)
            return carry

        lax.fori_loop(0, cols // PAIR, each_pair, 0)
        for target, base in ((part_send, half), (part_keep, 0)):

            def each_part(r, carry, target=target, base=base):
                rows = grad_ref[0, aligned((base + r) * length, length), :]
                target[r, 0] = dot(rows, w_ref[...], 1, 1).astype(BF16)
                return carry

            lax.fori_loop(0, half, each_part, 0)

    part = (half, seqs, length, width)
    outs = [shape((seqs, total, cols3)), shape(part), shape(part)]
    block = pl.BlockSpec((half, 1, length, width), lambda i, t: (0, g, 0, 0))
    operands = [qkv, w_qkv, lse, *contexts] + upstream + before
    first = len(operands) - n_before
    return call(
        kernel,
        table,
        operands,
        [whole_block(v.shape) for v in (qkv, w_qkv, lse)]
        + [pl.BlockSpec((half, 1, length, cols), lambda i, t: (0, g, 0, 0))] * 2
        + [
            pl.BlockSpec((v.shape[0], 1, length, cols), lambda i, t: (0, g, 0, 0))
            for v in upstream
        ]
        + [ANY] * n_before,
        outs,
        [pl.BlockSpec((1, total, cols3), lambda i, t: (g, 0, 0)), block, block],
        (1,),
        [
            pltpu.VMEM((total, cols), BF16),
            pltpu.VMEM((total, cols), BF16),
            pltpu.VMEM((total, PAIR), F32),
            pltpu.VMEM((total, PAIR), F32),
        ],
        8,
        "attention_backward",
        {first + i: i for i in range(n_before)},
    )


def head_weights_backward(plan, table, near, far, grad, narrow, wide):
    n, n_z = plan.n_seq, plan.n_z
    half, seqs, length, width = near.shape
    cols3 = grad.shape[2]
    own_rows = width // plan.n_dp
    total = n * length
    span = wide.shape[2]

    def kernel(t, near_ref, far_ref, grad_ref, narrow_ref, wide_ref, *rest):
        w_keep, w_send, w_acc, b_acc = rest
        step_id = pl.program_id(0)

        @pl.when(step_id == 0)
        def _():
            w_acc[...] = jnp.zeros_like(w_acc)
            b_acc[...] = jnp.zeros_like(b_acc)

        for part, source in enumerate((near_ref, far_ref)):
            rows = source[...].reshape(half * length, width)
            these = grad_ref[0, part * half * length : (part + 1) * half * length, :]
            w_acc[...] += dot(rows, these, 0, 0)
        b_acc[0:1, :] += jnp.sum(grad_ref[0].astype(F32), 0, keepdims=True)

        @pl.when(step_id == seqs - 1)
        def _():
            for target, k in ((w_keep, 0), (w_send, 1)):
                for z in range(n_z):
                    row = (2 * z + t.core(k)) * own_rows
                    target[z, :own_rows, :] = w_acc[aligned(row, own_rows), :].astype(BF16)
                    here = (t.s == z).astype(F32)
                    last = lax.broadcasted_iota(jnp.int32, (8, cols3), 0) == 7
                    rows = jnp.where(
                        last, b_acc[0:1, :] * here, narrow_ref[2 * z + t.core(k)]
                    )
                    target[z, own_rows : own_rows + 8, :] = rows.astype(BF16)
                    target[z, own_rows + 8 :, :] = jnp.zeros((PAD - 8, cols3), BF16)
                if k == 0:
                    for r in range(n):
                        rows = wide_ref[r].astype(BF16)
                        target[t.member(r, t.c), own_rows + 8 :, :span] = rows

    block = pl.BlockSpec((half, 1, length, width), lambda g, t: (0, g, 0, 0))
    w_out = (n_z, own_rows + PAD, cols3)
    return call(
        kernel,
        table,
        [near, far, grad, narrow, wide],
        [
            block,
            block,
            pl.BlockSpec((1, total, cols3), lambda g, t: (g, 0, 0)),
            whole_block(narrow.shape),
            whole_block(wide.shape),
        ],
        [shape(w_out), shape(w_out)],
        [whole_block(w_out), whole_block(w_out)],
        (seqs,),
        [pltpu.VMEM((width, cols3), F32), pltpu.VMEM((8, cols3), F32)],
        8,
        "head_weights_backward",
    )


def output_norm(plan, table, pieces, where, inputs, vectors, w_out, come, near, far, others):
    n, n_z = plan.n_seq, plan.n_z
    half = n // 2
    tokens, width = inputs.shape
    own_rows = w_out.shape[0]
    cols = width // n
    tile = 128
    n_moves = 2 + 2 * (n_z - 1) * n

    def kernel(t, in_ref, vec_ref, w_ref, come_ref, near_ref, far_ref, on_ref, of_ref, *rest):
        refs, rest = rest[: len(pieces)], rest[len(pieces) :]
        sum_ref, norm_ref, low_ref, full_ref, sems = rest

        def row(z, k):
            return aligned((z * 2 + t.core(k)) * own_rows, own_rows)

        moves = []
        for k, source in enumerate((w_ref, come_ref)):
            at = full_ref.at[row(t.behind(0), k)]
            lanes = source.shape[1] - width
            moves.append((source.at[pl.ds(0, own_rows), pl.ds(lanes, width)], at))
        for k, (first, second) in enumerate(((near_ref, far_ref), (on_ref, of_ref))):
            for j in range(1, n_z):
                for r in range(n):
                    source = first if r < half else second
                    at = full_ref.at[
                        row(t.behind(j), k),
                        aligned(t.member(r, t.core(k)) * cols, cols),
                    ]
                    moves.append((source.at[r % half, j - 1], at))
        copies = copies_of(moves, sems)
        for copy in copies:
            copy.start()
        for copy in copies:
            copy.wait()

        def each_tile(i, carry):
            rows = aligned(i * tile, tile)
            total = in_ref[rows, :].astype(F32) + vec_ref[2:3, :]
            for r, (a, m) in enumerate(where):
                weights = full_ref[aligned(t.member(r, t.c) * cols, cols), :]
                total += dot(refs[a][m, rows, :], weights)
            unit, _ = statistics(total)
            normed = unit * vec_ref[3:4, :] + vec_ref[4:5, :]
            sum_ref[rows, :] = total
            norm_ref[rows, :] = normed
            low_ref[rows, :] = normed.astype(BF16)
            return carry

        lax.fori_loop(0, tokens // tile, each_tile, 0)

    full = (tokens, width)
    return call(
        kernel,
        table,
        [inputs, vectors, w_out, come, near, far, *others, *pieces],
        [whole_block(full), whole_block(vectors.shape)]
        + [ANY] * 6
        + [whole_block(p.shape) for p in pieces],
        [shape(full, F32), shape(full, F32), shape(full), shape((width, width))],
        [whole_block(full)] * 3 + [whole_block((width, width))],
        (1,),
        [pltpu.SemaphoreType.DMA((n_moves,))],
        7,
        "output_norm",
    )


def flatten(remote):
    arrays, found = [], []
    for near, far in remote:
        found += [(len(arrays), i) for i in range(near.shape[1])]
        arrays += [near, far]
    return arrays, found


def gelu_parts(v):
    big = 0.5 + 0.5 * lax.erf(v * np.float32(np.sqrt(0.5)))
    small = jnp.exp(-0.5 * v * v) * np.float32(1.0 / np.sqrt(2.0 * np.pi))
    return v * big, big + v * small


def up_forward(plan, table, low, other_low, w_up, come, remote, bias):
    n, n_z = plan.n_seq, plan.n_z
    half = n // 2
    tokens, width = low.shape
    own_rows, hidden = w_up.shape
    quarter = hidden // 2 // n
    n_moves = 2 + n_z - 1
    tile = 128

    remote, found = flatten(remote)

    def kernel(t, low_ref, other_ref, up_ref, come_ref, bias_ref, *rest):
        remote_refs, rest = rest[: len(remote)], rest[len(remote) :]
        act_ref, slope_ref, w_hbm, w, sems, out_sem = rest
        step_id = pl.program_id(0)

        def moves(r):
            member = t.member(r, t.c)
            z = t.behind(0)
            at = w.at[r]

            def row(k):
                return aligned((z * 2 + t.core(k)) * own_rows, own_rows)

            lanes = aligned((member * 2 + t.c) * quarter, quarter)
            out = [(up_ref.at[:, lanes], at.at[row(0)])]
            lanes = aligned(member * quarter, quarter)
            out.append((come_ref.at[pl.ds(0, own_rows), lanes], at.at[row(1)]))
            for j in range(1, n_z):
                z_j = t.behind(j)
                a, i = found[j - 1]
                source = remote_refs[a + (r >= half)]
                for k in range(2):
                    rows = aligned((z_j * 2 + t.core(k)) * own_rows, own_rows)
                    out.append(
                        (
                            source.at[r % half, i, pl.ds(k * own_rows, own_rows)],
                            at.at[rows],
                        )
                    )
            return out

        def copies(r):
            return copies_of(moves(r), sems.at[r])

        @pl.when(step_id == 0)
        def _():
            for r in range(n):
                for copy in copies(r):
                    copy.start()

        for r in range(n):

            @pl.when(step_id == r)
            def _(r=r):
                for copy in copies(r):
                    copy.wait()

        def out_copy(r):
            return pltpu.make_async_copy(w.at[r], w_hbm.at[r], out_sem.at[r])

        for r in range(n):

            @pl.when(step_id == r)
            def _(r=r):
                out_copy(r).start()

        weights = w.at[step_id]
        for part, source in enumerate((low_ref, other_ref)):

            def step(i, carry, part=part, source=source):
                rows = pl.ds(pl.multiple_of(i * tile, tile), tile)
                pre = dot(source[rows, :], weights[...]) + bias_ref[0]
                active, slope = gelu_parts(pre)
                rows = pl.ds(pl.multiple_of(part * tokens + i * tile, tile), tile)
                act_ref[0, rows, :] = active.astype(BF16)
                slope_ref[0, rows, :] = slope.astype(BF16)
                return carry

            lax.fori_loop(0, tokens // tile, step, 0)

        @pl.when(step_id == n - 1)
        def _():
            for r in range(n):
                out_copy(r).wait()

    big = (n, 2 * tokens, quarter)
    block = pl.BlockSpec((1, 2 * tokens, quarter), lambda r, t: (r, 0, 0))
    return call(
        kernel,
        table,
        [low, other_low, w_up, come, bias] + remote,
        [whole_block(low.shape)] * 2
        + [ANY] * 2
        + [
            pl.BlockSpec(
                (1, 1, quarter),
                lambda r, t: (2 * t.member(r, t.c) + t.c, 0, 0),
            )
        ]
        + [ANY] * len(remote),
        [shape(big), shape(big), shape((n, width, quarter))],
        [block, block, ANY],
        (n,),
        [
            pltpu.VMEM((n, width, quarter), BF16),
            pltpu.SemaphoreType.DMA((n, 2 + 2 * (n_z - 1))),
            pltpu.SemaphoreType.DMA((n,)),
        ],
        15,
        "up_forward",
    )


def down_forward(plan, table, active, w_down, remote):
    n, n_z = plan.n_seq, plan.n_z
    half = n // 2
    tokens = active.shape[1] // 2
    quarter = active.shape[2]
    own_hidden, width = w_down.shape
    cols = width // n

    remote, found = flatten(remote)

    def kernel(t, act_ref, down_ref, *rest):
        remote_refs, rest = rest[: len(remote)], rest[len(remote) :]
        own_ref, other_ref, w_hbm, w, acc, sems, out_sem = rest
        step_id = pl.program_id(0)
        out_copy = pltpu.make_async_copy(w, w_hbm, out_sem)

        @pl.when(step_id == 0)
        def _():
            moves = [
                (down_ref, w.at[aligned(t.behind(0) * own_hidden, own_hidden)])
            ]
            for j in range(1, n_z):
                rows = aligned(t.behind(j) * own_hidden, own_hidden)
                a, i = found[j - 1]
                for r in range(n):
                    source = remote_refs[a + (r >= half)]
                    lanes = aligned(t.member(r, t.c) * cols, cols)
                    moves.append((source.at[r % half, i], w.at[rows, lanes]))
            copies = copies_of(moves, sems)
            for copy in copies:
                copy.start()
            acc[...] = jnp.zeros_like(acc)
            for copy in copies:
                copy.wait()
            out_copy.start()

        rows = aligned(t.member(step_id, t.c) * quarter, quarter)
        acc[...] += dot(act_ref[0], w[rows, :])

        @pl.when(step_id == n - 1)
        def _():
            own_ref[...] = acc[:tokens, :]
            other_ref[...] = acc[tokens:, :].astype(BF16)
            out_copy.wait()

    full = (tokens, width)
    return call(
        kernel,
        table,
        [active, w_down] + remote,
        [pl.BlockSpec((1, 2 * tokens, quarter), lambda r, t: (r, 0, 0))]
        + [ANY] * (1 + len(remote)),
        [shape(full, F32), shape(full), shape((n * quarter, width))],
        [whole_block(full), whole_block(full), ANY],
        (n,),
        [
            pltpu.VMEM((n * quarter, width), BF16),
            pltpu.VMEM((2 * tokens, width), F32),
            pltpu.SemaphoreType.DMA((1 + (n_z - 1) * n,)),
            pltpu.SemaphoreType.DMA,
        ],
        10,
        "down_forward",
    )


def norm_two(table, normed, own, come, cotangent, vectors):
    tokens, width = normed.shape
    tile = 128

    def kernel(t, norm_ref, own_ref, come_ref, cot_ref, vec_ref, *rest):
        out_ref, grad_ref, low_ref, sums = rest

        @pl.when(pl.program_id(0) == 0)
        def _():
            sums[...] = jnp.zeros_like(sums)

        second = norm_ref[...] + (own_ref[...] + come_ref[...].astype(F32) + vec_ref[5:6, :])
        unit, root = statistics(second)
        gain = vec_ref[6:7, :]
        out_ref[...] = (unit * gain + vec_ref[7:8, :]).astype(BF16)
        above = cot_ref[...].astype(F32)
        grad = norm_back(unit, root, gain, above)
        low = grad.astype(BF16)
        grad_ref[...] = grad
        low_ref[...] = low
        add_rows(sums, 0, low.astype(F32))
        add_rows(sums, 1, above * unit)
        add_rows(sums, 2, above)

    block = pl.BlockSpec((tile, width), lambda i, t: (i, 0))
    full = (tokens, width)
    return call(
        kernel,
        table,
        [normed, own, come, cotangent, vectors],
        [block] * 4 + [whole_block(vectors.shape)],
        [shape(full), shape(full, F32), shape(full), shape((8, width), F32)],
        [block] * 3 + [whole_block((8, width))],
        (tokens // tile,),
        [],
        6,
        "norm_two",
    )


def ffn_backward(plan, table, low, other_low, w_down, w_up, slope):
    n = plan.n_seq
    tokens, width = low.shape
    quarter = slope.shape[2]

    def kernel(t, low_ref, other_ref, down_ref, up_ref, slope_ref, *rest):
        pre_ref, sum_ref, own_ref, come_ref, acc = rest
        step_id = pl.program_id(0)

        @pl.when(step_id == 0)
        def _():
            acc[...] = jnp.zeros_like(acc)

        sums = jnp.zeros((1, quarter), F32)
        for part, source in enumerate((low_ref, other_ref)):
            rows = pl.ds(part * tokens, tokens)
            grad = dot(source[...], down_ref[...], 1, 1) * slope_ref[0, rows, :].astype(F32)
            grad = grad.astype(BF16)
            pre_ref[0, rows, :] = grad
            sums += jnp.sum(grad.astype(F32), 0, keepdims=True)
            acc[rows, :] += dot(grad, up_ref[0], 1, 1)
        row = lax.broadcasted_iota(jnp.int32, (8, quarter), 0)
        sum_ref[0] = jnp.where(row == 0, sums, 0.0)

        @pl.when(step_id == n - 1)
        def _():
            own_ref[...] = acc[:tokens, :]
            come_ref[...] = acc[tokens:, :].astype(BF16)

    big = pl.BlockSpec((1, 2 * tokens, quarter), lambda r, t: (r, 0, 0))
    full = (tokens, width)
    return call(
        kernel,
        table,
        [low, other_low, w_down, w_up, slope],
        [whole_block(full)] * 2
        + [
            pl.BlockSpec((quarter, width), lambda r, t: (t.member(r, t.c), 0)),
            pl.BlockSpec((1, width, quarter), lambda r, t: (r, 0, 0)),
            big,
        ],
        [shape(slope.shape), shape((n, 8, quarter), F32), shape(full, F32), shape(full)],
        [
            big,
            pl.BlockSpec((1, 8, quarter), lambda r, t: (r, 0, 0)),
            whole_block(full),
            whole_block(full),
        ],
        (n,),
        [pltpu.VMEM((2 * tokens, width), F32)],
        13,
        "ffn_backward",
    )


def down_weights(plan, table, active, low, other_low, base):
    n, n_z = plan.n_seq, plan.n_z
    half = n // 2
    tokens, width = low.shape
    quarter = active.shape[2]
    cols = width // n

    def kernel(t, act_ref, low_ref, other_ref, out_ref, grads):
        @pl.when(pl.program_id(0) == 0)
        def _():
            for r in range(half):
                lanes = aligned(t.member(base + r, t.c) * cols, cols)
                here = pl.ds(r * cols, cols)
                grads[:tokens, here] = low_ref[:, lanes]
                grads[tokens:, here] = other_ref[:, lanes]

        total = dot(act_ref[0], grads[...], 0, 0)
        for r in range(half):
            out_ref[r, 0] = total[:, r * cols : (r + 1) * cols].astype(BF16)

    return call(
        kernel,
        table,
        [active, low, other_low],
        [pl.BlockSpec((1, 2 * tokens, quarter), lambda r, t: (r, 0, 0))]
        + [whole_block((tokens, width))] * 2,
        [shape((half, n_z, quarter, cols))],
        [
            pl.BlockSpec(
                (half, 1, quarter, cols), lambda r, t: (0, t.member(r, t.c), 0, 0)
            )
        ],
        (n,),
        [pltpu.VMEM((2 * tokens, half * cols), BF16)],
        5,
        "down_weights",
    )[0]


def up_weights(plan, table, low, other_low, grad_pre, base):
    n, n_z = plan.n_seq, plan.n_z
    half = n // 2
    tokens, width = low.shape
    quarter = grad_pre.shape[2]
    own_rows = width // plan.n_dp

    def kernel(t, low_ref, other_ref, grad_ref, out_ref):
        for z in range(n_z):
            lanes = pl.ds(2 * z * own_rows, 2 * own_rows)
            total = dot(low_ref[:, lanes], grad_ref[0, :tokens, :], 0, 0)
            total += dot(other_ref[:, lanes], grad_ref[0, tokens:, :], 0, 0)
            total = total.astype(BF16)
            out_ref[0, z, :, :quarter] = total[:own_rows]
            out_ref[0, z, :, quarter:] = total[own_rows:]

    dims = (half, n_z, own_rows, 2 * quarter)
    return call(
        kernel,
        table,
        [low, other_low, grad_pre],
        [whole_block((tokens, width))] * 2
        + [pl.BlockSpec((1, 2 * tokens, quarter), lambda i, t: (base + i, 0, 0))],
        [shape(dims)],
        [pl.BlockSpec((1,) + dims[1:], lambda i, t: (i, 0, 0, 0))],
        (half,),
        [],
        6,
        "up_weights",
    )[0]


def norm_one_back(plan, table, grad_second, own, come, first_sum, vectors, w_out, sums_two):
    n = plan.n_seq
    tokens, width = own.shape
    cols = width // n
    tile = 128

    own_rows = width // plan.n_dp

    def kernel(t, grad_ref, own_ref, come_ref, sum_ref, vec_ref, w_ref, two_ref, *rest):
        first_ref, low_ref, narrow_ref = rest[:3]
        keep_ref, send_ref, sums = rest[3:]
        sums[0:3, :] = jnp.zeros((3, width), F32)
        sums[3:6, :] = two_ref[0:3, :]
        sums[6:8, :] = jnp.zeros((2, width), F32)

        def each_tile(i, carry):
            rows = aligned(i * tile, tile)
            above = grad_ref[rows, :] + (own_ref[rows, :] + come_ref[rows, :].astype(F32))
            unit, root = statistics(sum_ref[rows, :])
            grad = norm_back(unit, root, vec_ref[3:4, :], above)
            low = grad.astype(BF16)
            first_ref[rows, :] = grad
            low_ref[rows, :] = low
            add_rows(sums, 0, low.astype(F32))
            add_rows(sums, 1, above * unit)
            add_rows(sums, 2, above)
            for r in range(n):
                weights = w_ref[aligned(t.member(r, t.c) * cols, cols), :]
                target = keep_ref if r < half else send_ref
                target[r % half, rows, :] = dot(low, weights, 1, 1).astype(BF16)
            return carry

        lax.fori_loop(0, tokens // tile, each_tile, 0)
        narrow_ref[...] = jnp.zeros_like(narrow_ref)
        for owner in range(plan.n_dp):
            lanes = pl.ds(owner * own_rows, own_rows)
            narrow_ref[owner, :, 0:own_rows] = sums[:, lanes]

    full = (tokens, width)
    half = n // 2
    part = (half, tokens, cols)
    narrow = (plan.n_dp, 8, 3 * cols)
    return call(
        kernel,
        table,
        [grad_second, own, come, first_sum, vectors, w_out, sums_two],
        [whole_block(full)] * 4
        + [whole_block(v.shape) for v in (vectors, w_out, sums_two)],
        [shape(full, F32), shape(full), shape(narrow, F32)] + [shape(part)] * 2,
        [whole_block(full)] * 2 + [whole_block(narrow)] + [whole_block(part)] * 2,
        (1,),
        [pltpu.VMEM((8, width), F32)],
        8,
        "norm_one_back",
    )


def out_weights(plan, table, pieces, where, low):
    n, n_z = plan.n_seq, plan.n_z
    tokens, width = low.shape
    cols = width // n
    own_rows = width // plan.n_dp

    def kernel(t, low_ref, *rest):
        refs, (keep_ref, send_ref, both) = rest[: len(pieces)], rest[len(pieces) :]
        for r, (a, m) in enumerate(where):
            z = t.member(r, t.c)
            both[...] = dot(refs[a][m], low_ref[...], 0, 0).astype(BF16)
            for target, k in ((send_ref, 1), (keep_ref, 0)):
                rows = aligned(t.core(k) * own_rows, own_rows)
                for s in range(n):
                    at = aligned(t.member(s, t.core(k)) * cols, cols)
                    target[s, z] = both[rows, at]

    dims = (n, n_z, own_rows, cols)
    return call(
        kernel,
        table,
        [low, *pieces],
        [whole_block(low.shape)] + [whole_block(p.shape) for p in pieces],
        [shape(dims), shape(dims)],
        [whole_block(dims)] * 2,
        (1,),
        [pltpu.VMEM((cols, width), BF16)],
        0,
        "out_weights",
    )


def parts_along_z(plan, table, terms):
    n_z = plan.n_z
    rows = terms[0][0].shape[1]
    operands = [v for group in terms for v in group]
    lanes = sum(group[0].shape[2] for group in terms)

    def kernel(t, *refs):
        sources, outs = refs[: len(operands)], refs[len(operands) :]
        for j in range(n_z):

            @pl.when(pl.program_id(0) == j)
            def _(j=j):
                left, at = list(sources), 0
                target = outs[2 * j // n_z]
                for group in terms:
                    total = left.pop(0)[0].astype(F32)
                    for _ in group[1:]:
                        total += left.pop(0)[0].astype(F32)
                    end = at + total.shape[1]
                    target[j % (n_z // 2), :, at:end] = total.astype(BF16)
                    at = end

    def member(i, t):
        here = 0
        for k in range(plan.z_bits):
            here = here | ((i >> k) & 1) << (plan.z_bits - 1 - k)
        return (t.z ^ here, 0, 0)

    out = (n_z // 2, rows, lanes)
    return call(
        kernel,
        table,
        operands,
        [pl.BlockSpec((1,) + v.shape[1:], member) for v in operands],
        [shape(out)] * 2,
        [whole_block(out)] * 2,
        (n_z,),
        [],
        2,
        "parts_along_z",
    )


def split_by_core(plan, table, pieces, split):
    _, rows, lanes = pieces[0].shape
    half = split // 2
    n_pieces = len(pieces)

    def kernel(t, *refs):
        for k, target in enumerate(refs[n_pieces:]):
            size = half if k < 2 else lanes - split
            at = aligned(t.core(k) * half, half) if k < 2 else pl.ds(split, size)
            total = refs[0][0, :, at].astype(F32)
            for ref in refs[1:n_pieces]:
                total += ref[0, :, at].astype(F32)
            target[...] = total.astype(BF16)

    outs = [(rows, half), (rows, half), (rows, lanes - split)]
    return call(
        kernel,
        table,
        pieces,
        [whole_block(p.shape) for p in pieces],
        [shape(o) for o in outs],
        [whole_block(o) for o in outs],
        (1,),
        [],
        0,
        "split_by_core",
    )


def place(plan, table, near, far, outs, moves, name):
    n = plan.n_seq
    half = n // 2

    def kernel(t, near_ref, far_ref, *targets):
        for r in range(n):
            source = near_ref if r < half else far_ref
            for src, o, at in moves:
                targets[o][:, at(t, r)] = source[(r % half,) + src].astype(F32)

    return call(
        kernel,
        table,
        [near, far],
        [whole_block(near.shape)] * 2,
        [shape(o, F32) for o in outs],
        [whole_block(o) for o in outs],
        (1,),
        [],
        0,
        name,
    )


def local(
    plan,
    inputs,
    w_query,
    w_key,
    w_value,
    b_query,
    b_value,
    w_out,
    b_out,
    gain_one,
    shift_one,
    w_up,
    b_up,
    w_down,
    b_down,
    gain_two,
    shift_two,
    cotangent,
):
    n_dp, n, n_z = plan.n_dp, plan.n_seq, plan.n_z
    half = n // 2
    seqs, length, width = inputs.shape
    tokens = seqs * length
    own_rows, hidden = w_up.shape
    own_hidden = w_down.shape[0]
    cols = width // n
    cols3 = 3 * cols
    quarter = hidden // 2 // n
    assert n == n_z and quarter == own_hidden
    table = plan
    core = lax.axis_index("dp") % 2

    narrow = jnp.stack(
        [b_query, b_value, b_out, gain_one, shift_one, b_down, gain_two, shift_two]
    )
    vec = jnp.concatenate(
        [
            jnp.pad(narrow, ((0, 0), (0, 4 * cols - own_rows))),
            jnp.pad(b_up[None], ((0, 7), (0, 4 * cols - own_hidden))),
        ],
        0,
    )

    def column_block(t):
        return (pl.ds(0, own_rows), aligned(t.s * cols, cols))

    moves = [
        (i, column_block, 0, lambda t, i=i: (pl.ds(0, own_rows), pl.ds(i * cols, cols)))
        for i in range(4)
    ]
    moves.append((4, lambda t: (pl.ds(0, PAD),), 0, lambda t: (pl.ds(own_rows, PAD),)))
    (first,) = assemble(
        table,
        [w_query, w_key, w_value, w_out, vec],
        moves,
        [shape((own_rows + PAD, 4 * cols))],
        "pack_first",
    )

    def straight(block, j):
        return lax.ppermute(block, BOTH, plan.toward[j])

    near_x = inputs[None]
    for k in range(plan.bits - 1):
        near_x = plan.double(near_x, k)
    mine = [first, straight(first, 1)]

    top = plan.bits - 1

    def final(near, *ready):
        return near, lax.ppermute(after(near, *ready), BOTH, plan.stage[top])

    def begin(block, *ready):
        near = after(block, *ready)[None]
        for k in range(top - 1):
            near = plan.double(near, k)
        return near, lax.ppermute(near, BOTH, plan.stage[top - 1])

    def joined(started, *ready):
        return jnp.concatenate([after(started[0], *ready), started[1]], 0)

    def onward(block, *ready):
        return lax.ppermute(after(block, *ready), BOTH, plan.toward[1])

    ready = (near_x, mine[1])
    far_x = final(near_x, *ready)[1]
    mine.append(onward(mine[1], *ready))
    for j in range(3, n_z):
        mine.append(onward(mine[-1]))

    moves = []
    for z in range(n_z):
        moves.append(
            (
                0,
                lambda t, z=z: (
                    pl.ds(0, own_rows),
                    aligned((2 * z + (1 - t.c)) * quarter, quarter),
                ),
                0,
                lambda t, z=z: (pl.ds(0, own_rows), pl.ds(z * quarter, quarter)),
            )
        )
    moves.append(
        (
            1,
            lambda t: (pl.ds(0, own_rows),),
            0,
            lambda t: (pl.ds(0, own_rows), pl.ds(n * quarter, width)),
        )
    )
    (across,) = assemble(
        table,
        [after(w_up, mine[2]), w_out],
        moves,
        [shape((own_rows, n * quarter + width))],
        "pack_across",
    )
    come = plan.swap(across)


    def rows_at(start, size):
        return lambda t: (pl.ds(start, size), pl.ds(0, quarter))

    moves = [
        (
            0,
            lambda t: (
                pl.ds(0, own_rows),
                aligned((2 * t.s + t.c) * quarter, quarter),
            ),
            0,
            rows_at(0, own_rows),
        ),
        (
            1,
            lambda t: (pl.ds(0, own_rows), aligned(t.s * quarter, quarter)),
            0,
            rows_at(own_rows, own_rows),
        ),
    ]
    moves.append(
        (
            2,
            lambda t: (pl.ds(0, own_hidden), aligned(t.s * cols, cols)),
            1,
            lambda t: (pl.ds(0, own_hidden),),
        )
    )
    second, down = assemble(
        table,
        [w_up, come, w_down],
        moves,
        [shape((2 * own_rows, quarter)), shape((own_hidden, cols))],
        "pack_second",
    )
    ups = [onward(second)]

    ready = (far_x, second) + tuple(mine[1:])
    mine_all = jnp.stack([after(piece, *ready) for piece in mine])
    theirs = plan.swap(mine_all)
    outs = jnp.stack([after(piece, *ready)[:own_rows, cols3:] for piece in mine[1:]])
    outs_started = begin(outs)
    ups.append(onward(ups[0], *ready))
    downs = [onward(down, *ready)]
    w_qkv, vectors, up_bias = head_weights(plan, table, mine_all, theirs)
    qkv, lse = [], []

    def attend(g, before, *ready):
        out, *parts, total = attention_forward(
            plan, table, g, near_x, far_x, w_qkv, after(vectors, *ready), before
        )
        qkv.append(out)
        lse.append(total)
        return parts

    parts = attend(0, [])

    near_out = joined(outs_started, parts[0])
    ready = (near_out, parts[0], ups[1], downs[0])
    outs = final(near_out, *ready)
    ups.append(onward(ups[1], *ready))
    downs.append(onward(downs[0], *ready))
    two_started = begin(jnp.stack([after(piece, *ready) for piece in ups[:2]]))
    parts = attend(1, parts, *ready)

    near_two = joined(two_started, parts[0])
    ready = (near_two, outs[1], ups[2], downs[1], parts[0])
    for j in range(3, n_z - 1):
        ups.append(onward(ups[-1]))
        downs.append(onward(downs[-1]))
    others = [plan.swap(after(part, *ready)) for part in outs]
    up_two = final(near_two, *ready)
    downs.append(onward(downs[-1], *ready))
    three_started = begin(jnp.stack([after(piece, *ready) for piece in ups[2:]]))
    for g in range(2, seqs):
        parts = attend(g, parts, *ready)

    contexts = parts
    send = after(parts[1], up_two[1], three_started[1], *others)
    near_three = joined(three_started, send)
    up_three = final(near_three)
    pieces, where = distinct(plan.exchange(parts[0], send))
    pieces = [p.reshape(p.shape[0], tokens, cols) for p in pieces]
    downs = jnp.stack([after(piece, near_three) for piece in downs])
    downs_started = begin(downs, *pieces)
    first_sum, normed, low, full_out = output_norm(
        plan,
        table,
        pieces,
        where,
        after(inputs.reshape(tokens, width), downs),
        vectors,
        w_out,
        come,
        *outs,
        others,
    )

    other_low = plan.swap(after(low, up_three[1]))
    near_down = joined(downs_started, low)
    ready = (other_low, up_three[1], near_down)
    down_all = final(near_down, *ready)
    active, slope, up_kept = up_forward(
        plan, table, after(low, *ready), other_low, w_up, come, [up_two, up_three], up_bias
    )
    own, away, down_kept = down_forward(plan, table, active, w_down, [down_all])
    output, grad_second, low_two, sums_two = norm_two(
        table, normed, own, plan.swap(away), cotangent.reshape(tokens, width), vectors
    )

    def begun(send, k, *ready):
        return lax.ppermute(after(send, *ready), BOTH, plan.stage[k])

    def summed(keep, come, k, *ready):
        low = (1 << k) // 2
        come = after(come, *ready)
        return add(keep[:low], come[:low]), add(keep[low:], come[low:])

    def middle(keep, come, *ready):
        keep, send = summed(keep, come, top, *ready)
        for k in reversed(range(1, top)):
            keep, send = summed(keep, begun(send, k), k)
        return keep, send

    other_two = plan.swap(low_two)
    down_send = down_weights(plan, table, active, low_two, other_two, half)
    down_come = begun(down_send, top)
    down_keep = down_weights(plan, table, active, after(low_two, down_send), other_two, 0)
    grad_pre, sums_up, own, away = ffn_backward(
        plan, table, after(low_two, down_keep), other_two, down_kept, up_kept, slope
    )
    away = plan.swap(away)
    low = after(low, own)
    up_send = up_weights(plan, table, low, other_low, grad_pre, half)
    down_keep, down_send = middle(down_keep, down_come, up_send)
    down_last = begun(down_send, 0)
    grad_first, low_one, sums, *parts = norm_one_back(
        plan,
        table,
        grad_second,
        after(own, down_send),
        away,
        first_sum,
        vectors,
        full_out,
        sums_two,
    )
    up_keep = up_weights(plan, table, after(low, low_one), other_low, grad_pre, 0)
    parts = [p.reshape(half, seqs, length, cols) for p in parts]
    found = plan.exchange(parts[0], after(parts[1], down_last), up_keep)
    out_keep, out_send = out_weights(
        plan, table, pieces, where, after(low_one, found[half][0])
    )
    parts, up_where = distinct(found)
    parts = [after(part, out_keep) for part in parts]
    out_come = plan.swap(after(out_send, *parts))

    def sent_along_z(terms, *ready):
        terms = [[after(group[0], *ready)] + group[1:] for group in terms]
        keep, send = parts_along_z(plan, table, terms)
        return keep, lax.ppermute(send, BOTH, plan.along[0])

    def on_along_z(keep, come, *ready):
        for way in plan.along[1:]:
            low = keep.shape[0] // 2
            come = after(come, *ready)
            sent = add(keep[low:], come[low:])
            keep = add(keep[:low], come[:low])
            come = lax.ppermute(sent, BOTH, way)
        return keep, come

    def total(keep, come, *ready):
        return add(after(keep, *ready), come)[0]

    def back(g, before, *ready):
        return attention_backward(
            plan,
            table,
            g,
            seqs,
            after(qkv[g], *ready),
            lse[g],
            contexts,
            parts,
            up_where,
            w_qkv,
            before,
        )

    ready = (out_keep, out_come) + tuple(parts)
    up_come = begun(up_send, top, *ready)
    out_come = after(out_come, *ready)
    out_sent = add(out_keep[half:], out_come[half:])
    out_first = begun(out_sent, top)
    out_kept = add(out_keep[:half], out_come[:half])
    shared = back(0, [], out_sent, out_kept, *ready)
    down_along = sent_along_z([[down_keep[0], down_last[0]]], shared[0])
    shared = back(1, list(shared), down_along[0])
    up_keep, up_send = middle(up_keep, up_come, shared[0])
    up_last = begun(up_send, 0)
    down_along = on_along_z(*down_along, up_send)
    out_kept, out_sent = middle(out_kept, out_first, up_send)
    out_last = begun(out_sent, 0)
    for g in range(2, seqs):
        shared = back(g, list(shared), up_send, out_sent, down_along[0])
    grad_qkv, part_keep, part_send = shared
    up_along = sent_along_z(
        [[up_keep[0], up_last[0]], [out_kept[0], out_last[0]]], grad_qkv
    )

    part_come = begun(part_send, top, up_along[0])
    down_started = begin(total(*down_along, up_along[0]))
    last_keep, last_send = head_weights_backward(
        plan, table, near_x, far_x, after(grad_qkv, up_along[0], down_started[0]), sums, sums_up
    )
    down_near = joined(down_started, last_keep)
    down_far = plan.final(down_near)
    up_along = on_along_z(*up_along, last_keep)
    last_come = plan.swap(last_send)
    last_along = sent_along_z([[last_keep, last_come]], up_along[0])
    part_keep, part_send = middle(part_keep, part_come, last_along[0])
    part_last = begun(part_send, 0)

    def lanes(size):
        return lambda t, r: aligned(t.member(r, t.c) * size, size)

    grad_inputs = grad_first.reshape(inputs.shape) + (
        part_keep[0].astype(F32) + part_last[0].astype(F32)
    )
    (grad_down,) = place(
        plan,
        table,
        after(down_near, part_send),
        down_far,
        [(own_hidden, width)],
        [((slice(None),), 0, lanes(cols))],
        "place_down",
    )
    last_along = on_along_z(*last_along, part_last, grad_down)
    up_along = (after(up_along[0], last_along[0]), up_along[1])
    up_kept, up_sent, grad_out = split_by_core(plan, table, up_along, 2 * quarter)
    up_come = plan.swap(up_sent)
    up_near = plan.halfway(jnp.concatenate([up_kept, up_come, grad_out], 1))
    up_far = plan.final(up_near)
    grad_inputs = grad_first.reshape(inputs.shape) + (
        part_keep[0].astype(F32) + after(part_last[0], up_near).astype(F32)
    )
    last_near = plan.halfway(total(*last_along, grad_inputs))
    last_far = plan.final(last_near)
    grad_up, grad_out = place(
        plan,
        table,
        after(up_near, last_near),
        up_far,
        [(own_rows, hidden), (own_rows, width)],
        [
            (
                (slice(None), pl.ds(k * quarter, quarter)),
                0,
                lambda t, r, k=k: aligned(
                    (2 * t.member(r, t.c) + t.core(k)) * quarter, quarter
                ),
            )
            for k in range(2)
        ]
        + [((slice(None), pl.ds(2 * quarter, cols)), 1, lanes(cols))],
        "place_up",
    )
    grad_wq, grad_wk, grad_wv = place(
        plan,
        table,
        last_near,
        last_far,
        [(own_rows, width)] * 3,
        [
            ((pl.ds(0, own_rows), pl.ds(m * cols, cols)), m, lanes(cols))
            for m in range(3)
        ],
        "place_heads",
    )
    vec_out = jnp.sum(last_near[:, own_rows:].astype(F32), 0)
    vec_out += jnp.sum(last_far[:, own_rows:].astype(F32), 0)
    biases = vec_out[7].reshape(3, 2, own_rows)
    biases = jnp.where(core == 0, biases[:, 0], biases[:, 1])
    return (
        output.reshape(inputs.shape),
        grad_inputs,
        grad_wq,
        grad_wk,
        grad_wv,
        biases[0],
        biases[2],
        grad_out,
        vec_out[0, :own_rows],
        vec_out[1, :own_rows],
        vec_out[2, :own_rows],
        grad_up,
        vec_out[8, :own_hidden],
        grad_down,
        vec_out[3, :own_rows],
        vec_out[4, :own_rows],
        vec_out[5, :own_rows],
    )


def solution(mesh):
    plan = Plan(mesh.shape["dp"], mesh.shape["seq"])
    rows, vector, token = P("dp", None), P("dp"), P("dp", "seq", None)
    weights = (rows,) * 3 + (vector,) * 2 + (rows,) + (vector,) * 3
    weights += (rows, vector, rows) + (vector,) * 3
    return jax.shard_map(
        functools.partial(local, plan),
        mesh=mesh,
        in_specs=(token,) + weights + (token,),
        out_specs=(token, token) + weights,
        check_vma=False,
    )
```

```python
import functools

import jax
import jax.numpy as jnp
import numpy as np
from jax import lax
from jax.experimental import pallas as pl
from jax.experimental.pallas import tpu as pltpu
from jax.sharding import PartitionSpec as P

HEAD_DIM = 64
PAIR = 2 * HEAD_DIM
EPSILON = 1e-12
BOTH = ("dp", "seq")
PAD = 16
MICROSECOND = 500_000_000
F32 = jnp.float32
BF16 = jnp.bfloat16
ANY = pl.BlockSpec(memory_space=pl.ANY)


def dot(former, latter, former_dim=1, latter_dim=0):
    return lax.dot_general(
        former,
        latter,
        (((former_dim,), (latter_dim,)), ((), ())),
        preferred_element_type=F32,
    )


class Plan:
    def __init__(self, n_dp, n_seq):
        self.n_dp, self.n_seq, self.n_z = n_dp, n_seq, n_dp // 2
        self.bits = n_seq.bit_length() - 1
        order = [0] + list(range(1, self.n_z, 2))
        order += list(range(2, self.n_z, 2))[::-1]
        self.order = order
        self.place = [order.index(z) for z in range(self.n_z)]
        self.core = self.pairs(lambda z, c, s: (z, 1 - c, s))
        self.toward = [
            self.pairs(lambda z, c, s, j=j: (self.behind(z, -j), c, s))
            for j in range(self.n_z)
        ]
        self.z_bits = self.n_z.bit_length() - 1
        self.along = [
            self.pairs(lambda z, c, s, k=k: (z ^ 1 << k, c, s)) for k in range(self.z_bits)
        ]
        self.across = [
            self.pairs(lambda z, c, s, r=r: (z, c, s ^ self.mask(c, r)))
            for r in range(n_seq)
        ]
        self.stage = [
            self.pairs(lambda z, c, s, k=k: (z, c, s ^ self.mask(c, 1 << k)))
            for k in range(self.bits)
        ]
    def behind(self, z, j):
        return self.order[(self.place[z] - j) % self.n_z]

    def mask(self, c, r):
        out = 0
        for k in range(self.bits):
            if r >> k & 1:
                out |= 1 << ((k + c) % self.bits)
        return out

    def pairs(self, target):
        out = []
        for dp in range(self.n_dp):
            for s in range(self.n_seq):
                z, c, t = target(dp // 2, dp % 2, s)
                out.append((dp * self.n_seq + s, (2 * z + c) * self.n_seq + t))
        return out

    def swap(self, block):
        return lax.ppermute(block, BOTH, self.core)

    def trade(self, blocks):
        return [blocks[0]] + [
            lax.ppermute(block, BOTH, way) for block, way in zip(blocks[1:], self.across[1:])
        ]

    def exchange(self, keep, send, *ready):
        held = [(0, keep, 0)]
        for k in reversed(range(self.bits)):
            come = after(lax.ppermute(send, BOTH, self.stage[k]), *ready)
            width, ready = 1 << k, ()
            held = held + [
                (mask | width, come, i * width) for i, (mask, _, _) in enumerate(held)
            ]
            if k:
                low = width // 2
                send = jnp.concatenate([a[i + low : i + width] for _, a, i in held], 0)
        return [(a, i) for _, a, i in sorted(held, key=lambda item: item[0])]

    def gather(self, block):
        near = block[None]
        for k in range(self.bits - 1):
            near = self.double(near, k)
        return near, lax.ppermute(near, BOTH, self.stage[self.bits - 1])

    def halfway(self, block, *ready):
        near = after(block, *ready)[None]
        for k in range(self.bits - 1):
            near = self.double(near, k)
        return near

    def final(self, near, *ready):
        return lax.ppermute(after(near, *ready), BOTH, self.stage[self.bits - 1])

    def double(self, near, k):
        return jnp.concatenate([near, lax.ppermute(near, BOTH, self.stage[k])], 0)


def add(former, latter):
    return (former.astype(F32) + latter.astype(F32)).astype(BF16)


def after(value, *others):
    return lax.optimization_barrier((value,) + others)[0]


class Here:
    def __init__(self, plan):
        self.plan = plan
        dp = lax.axis_index("dp")
        self.z, self.c, self.s = lax.div(dp, 2), lax.rem(dp, 2), lax.axis_index("seq")

    def core(self, k):
        return self.c if k == 0 else 1 - self.c

    def behind(self, j):
        n = self.plan.n_z
        half = lax.div(self.z, 2)
        odd = lax.rem(self.z, 2)
        place = jnp.where(odd == 1, half + 1, lax.rem(n - half, n))
        at = lax.rem(place - j + n, n)
        return jnp.where(at <= n // 2, jnp.maximum(2 * at - 1, 0), 2 * (n - at))

    def member(self, r, core):
        n, bits = self.plan.n_seq, self.plan.bits
        turned = ((r << 1) & (n - 1)) | (r >> (bits - 1))
        return self.s ^ (r + core * (turned - r))


def shape(dims, dtype=BF16):
    return jax.ShapeDtypeStruct(tuple(dims), dtype)


def distinct(found):
    arrays = []
    for array, _ in found:
        if not any(array is other for other in arrays):
            arrays.append(array)
    at = [([array is other for other in arrays].index(True), i) for array, i in found]
    return arrays, at


def turned(i, bits):
    return sum((i >> k & 1) << (bits - 1 - k) for k in range(bits))


def aligned(start, size):
    return pl.ds(pl.multiple_of(start, size), size)


def whole_block(dims):
    return pl.BlockSpec(tuple(dims), lambda *_: (0,) * len(dims))


def call(
    kernel, plan, operands, in_specs, outs, out_specs, grid, scratch, micros, name, alias=None
):
    size = sum(int(np.prod(o.shape)) * o.dtype.itemsize for o in list(operands) + list(outs))
    size = size if micros else 0

    def placed(spec):
        if spec.index_map is None:
            return spec
        return pl.BlockSpec(spec.block_shape, lambda *i: spec.index_map(*i, Here(plan)))

    return pl.pallas_call(
        lambda *refs: kernel(Here(plan), *refs),
        out_shape=list(outs),
        grid=grid,
        in_specs=[placed(spec) for spec in in_specs],
        out_specs=[placed(spec) for spec in out_specs],
        scratch_shapes=scratch,
        cost_estimate=pl.CostEstimate(
            flops=micros * MICROSECOND, bytes_accessed=size, transcendentals=0
        ),
        input_output_aliases=alias or {},
        name=name,
    )(*operands)


def assemble(table, pieces, moves, outs, name):
    def kernel(table_ref, *refs):
        sources, targets, sems = refs[: len(pieces)], refs[len(pieces) : -1], refs[-1]
        copies = [
            pltpu.make_async_copy(
                sources[i].at[src(table_ref)], targets[o].at[at(table_ref)], sems.at[n]
            )
            for n, (i, src, o, at) in enumerate(moves)
        ]
        for copy in copies:
            copy.start()
        for copy in copies:
            copy.wait()

    return call(
        kernel,
        table,
        pieces,
        [ANY] * len(pieces),
        outs,
        [whole_block(o.shape) for o in outs],
        (1,),
        [pltpu.SemaphoreType.DMA((len(moves),))],
        0,
        name,
    )


def copies_of(moves, sems):
    return [pltpu.make_async_copy(src, at, sems.at[n]) for n, (src, at) in enumerate(moves)]


def lanes_of(half):
    lane = lax.broadcasted_iota(jnp.int32, (1, PAIR), 1)
    return lane < HEAD_DIM if half == 0 else lane >= HEAD_DIM


def only(block, half):
    return jnp.where(lanes_of(half), block, jnp.zeros_like(block))


def statistics(hidden):
    center = hidden - jnp.mean(hidden, -1, keepdims=True)
    spread = jnp.mean(center * center, -1, keepdims=True)
    root = lax.rsqrt(spread + EPSILON)
    return center * root, root


def norm_back(unit, root, gain_vec, upstream):
    scaled = upstream * gain_vec
    first = jnp.mean(scaled, -1, keepdims=True)
    second = jnp.mean(scaled * unit, -1, keepdims=True)
    return root * (scaled - first - unit * second)


def add_rows(target, row, value):
    target[row : row + 1, :] += jnp.sum(value, 0, keepdims=True)


def head_weights(plan, table, mine, theirs):
    n_z, n_dp = plan.n_z, plan.n_dp
    rows, lanes = mine.shape[1:]
    own_rows, cols3 = rows - PAD, lanes // 4 * 3
    width, span = n_dp * own_rows, lanes // 2

    def kernel(t, mine_ref, theirs_ref, w_ref, vec_ref, bias_ref, held, sems):
        moves = []
        for k, source in enumerate((mine_ref, theirs_ref)):
            for j in range(n_z):
                owner = 2 * t.behind(j) + t.core(k)
                moves.append((source.at[j, pl.ds(own_rows, PAD)], held.at[owner]))
                moves.append(
                    (
                        source.at[j, pl.ds(0, own_rows), pl.ds(0, cols3)],
                        w_ref.at[aligned(owner * own_rows, own_rows)],
                    )
                )
        copies = copies_of(moves, sems)
        for copy in copies:
            copy.start()
        for copy in copies:
            copy.wait()
        for owner in range(n_dp):
            values = held[owner].astype(F32)
            at = pl.ds(owner * own_rows, own_rows)
            vec_ref[:, at] = values[:8, :own_rows]
            bias_ref[owner] = values[8:9, :span]

    outs = [shape((width, cols3)), shape((8, width), F32), shape((n_dp, 1, span), F32)]
    return call(
        kernel,
        table,
        [mine, theirs],
        [ANY] * 2,
        outs,
        [whole_block(o.shape) for o in outs],
        (1,),
        [pltpu.VMEM((n_dp, PAD, lanes), BF16), pltpu.SemaphoreType.DMA((4 * n_z,))],
        3,
        "head_weights",
    )


def attention_forward(plan, table, g, near, far, weights, vectors, before):
    n = plan.n_seq
    half, seqs, length, width = near.shape
    n_before = len(before)
    cols3 = weights.shape[1]
    cols = cols3 // 3
    total = n * length
    tile, chunk = min(512, total), min(256, total)
    lse = (cols // PAIR, 8, total)
    scale = HEAD_DIM**-0.5

    def kernel(t, near_ref, far_ref, w_ref, vec_ref, *rest):
        qkv_ref, keep_ref, send_ref, lse_ref, context = rest[n_before:]
        here = aligned(t.s * cols, cols)
        bias = jnp.concatenate(
            [vec_ref[0:1, here], jnp.zeros((1, cols), F32), vec_ref[1:2, here]], 1
        )
        for part, source in enumerate((near_ref, far_ref)):
            rows = source[...].reshape(half * length, width)
            out = dot(rows, w_ref[...]) + bias
            qkv_ref[part * half * length : (part + 1) * half * length, :] = out.astype(BF16)
        def each_pair(pair, carry):
            q_at = aligned(pair * PAIR, PAIR)
            k_at = aligned(cols + pair * PAIR, PAIR)
            value = qkv_ref[:, aligned(2 * cols + pair * PAIR, PAIR)]
            value = value.astype(F32).T.astype(BF16)

            def each_tile(i, carry):
                rows = aligned(i * tile, tile)
                query = qkv_ref[rows, q_at] * jnp.asarray(scale, BF16)
                out = []
                for head in range(2):
                    one = only(query, head)

                    def scores(c):
                        return dot(qkv_ref[pl.ds(c * chunk, chunk), k_at], one, 1, 1)

                    top = None
                    for c in range(total // chunk):
                        here = jnp.max(scores(c), 0, keepdims=True)
                        top = here if c == 0 else jnp.maximum(top, here)
                    for c in range(total // chunk):
                        exponent = jnp.exp(scores(c) - top)
                        here = jnp.sum(exponent, 0, keepdims=True)
                        these = value[
                            head * HEAD_DIM : (head + 1) * HEAD_DIM,
                            c * chunk : (c + 1) * chunk,
                        ]
                        part = dot(these, exponent.astype(BF16))
                        bottom = here if c == 0 else bottom + here
                        acc = part if c == 0 else acc + part
                    out.append(acc * (1.0 / bottom))
                    lse_ref[pair, head : head + 1, rows] = top + jnp.log(bottom)
                context[rows, q_at] = jnp.concatenate(out, 0).T.astype(BF16)
                return carry

            lax.fori_loop(0, total // tile, each_tile, 0)
            return carry

        lax.fori_loop(0, cols // PAIR, each_pair, 0)
        for r in range(n):
            target = keep_ref if r < half else send_ref
            target[r % half, 0] = context[r * length : (r + 1) * length, :]

    block = pl.BlockSpec((half, 1, length, width), lambda i, t: (0, g, 0, 0))
    return call(
        kernel,
        table,
        [near, far, weights, vectors] + before,
        [block, block, whole_block(weights.shape), whole_block(vectors.shape)]
        + [ANY] * n_before,
        [shape((total, cols3))]
        + [shape((half, seqs, length, cols))] * 2
        + [shape(lse, F32)],
        [whole_block((total, cols3))]
        + [pl.BlockSpec((half, 1, length, cols), lambda i, t: (0, g, 0, 0))] * 2
        + [whole_block(lse)],
        (1,),
        [pltpu.VMEM((total, cols), BF16)],
        6,
        "attention_forward",
        {4 + i: 1 + i for i in range(n_before)},
    )


def attention_backward(
    plan, table, g, seqs, qkv, lse, contexts, upstream, where, w_qkv, before
):
    n = plan.n_seq
    half = n // 2
    width, cols3 = w_qkv.shape
    cols = cols3 // 3
    total = qkv.shape[0]
    length = total // n
    tile, chunk = min(512, total), min(256, total)
    scale = HEAD_DIM**-0.5
    n_before, n_up = len(before), len(upstream)

    def kernel(t, qkv_ref, w_ref, lse_ref, near_ref, far_ref, *rest):
        up_refs, rest = rest[:n_up], rest[n_up + n_before :]
        grad_ref, part_keep, part_send = rest[:3]
        up, context, key_acc, value_acc = rest[3:]
        for r, (a, i) in enumerate(where):
            rows = pl.ds(r * length, length)
            up[rows, :] = up_refs[a][i, 0]
            context[rows, :] = (near_ref if r < half else far_ref)[r % half, 0]
        def each_pair(pair, carry):
            q_at = aligned(pair * PAIR, PAIR)
            k_at = aligned(cols + pair * PAIR, PAIR)
            v_at = aligned(2 * cols + pair * PAIR, PAIR)
            value_acc[...] = jnp.zeros_like(value_acc)
            key_acc[...] = jnp.zeros_like(key_acc)

            turned_key = qkv_ref[:, k_at].astype(F32).T.astype(BF16)

            def each_tile(i, carry):
                rows = aligned(i * tile, tile)
                query = qkv_ref[rows, q_at] * jnp.asarray(scale, BF16)
                above = up[rows, q_at]
                both = (above.astype(F32) * context[rows, q_at].astype(F32)).T
                out = []
                for head in range(2):
                    lanes = slice(head * HEAD_DIM, (head + 1) * HEAD_DIM)
                    inner = jnp.sum(both[lanes], 0, keepdims=True)
                    log_total = lse_ref[pair, head : head + 1, rows]
                    one, upper = only(query, head), only(above, head)
                    for c in range(total // chunk):
                        here = pl.ds(c * chunk, chunk)
                        portions = jnp.exp(dot(qkv_ref[here, k_at], one, 1, 1) - log_total)
                        slope = dot(qkv_ref[here, v_at], upper, 1, 1)
                        slope = (portions * (slope - inner)).astype(BF16)
                        value_acc[here, :] += dot(portions.astype(BF16), upper)
                        key_acc[here, :] += dot(slope, one)
                        these = turned_key[lanes, c * chunk : (c + 1) * chunk]
                        part = dot(these, slope)
                        acc = part if c == 0 else acc + part
                    out.append(acc * scale)
                grad_ref[0, rows, q_at] = jnp.concatenate(out, 0).T.astype(BF16)
                return carry

            lax.fori_loop(0, total // tile, each_tile, 0)
            grad_ref[0, :, k_at] = key_acc[...].astype(BF16)
            grad_ref[0, :, v_at] = value_acc[...].astype(BF16)
            return carry

        lax.fori_loop(0, cols // PAIR, each_pair, 0)
        for target, base in ((part_send, half), (part_keep, 0)):

            def each_part(r, carry, target=target, base=base):
                rows = grad_ref[0, aligned((base + r) * length, length), :]
                target[r, 0] = dot(rows, w_ref[...], 1, 1).astype(BF16)
                return carry

            lax.fori_loop(0, half, each_part, 0)

    part = (half, seqs, length, width)
    outs = [shape((seqs, total, cols3)), shape(part), shape(part)]
    block = pl.BlockSpec((half, 1, length, width), lambda i, t: (0, g, 0, 0))
    operands = [qkv, w_qkv, lse, *contexts] + upstream + before
    first = len(operands) - n_before
    return call(
        kernel,
        table,
        operands,
        [whole_block(v.shape) for v in (qkv, w_qkv, lse)]
        + [pl.BlockSpec((half, 1, length, cols), lambda i, t: (0, g, 0, 0))] * 2
        + [
            pl.BlockSpec((v.shape[0], 1, length, cols), lambda i, t: (0, g, 0, 0))
            for v in upstream
        ]
        + [ANY] * n_before,
        outs,
        [pl.BlockSpec((1, total, cols3), lambda i, t: (g, 0, 0)), block, block],
        (1,),
        [
            pltpu.VMEM((total, cols), BF16),
            pltpu.VMEM((total, cols), BF16),
            pltpu.VMEM((total, PAIR), F32),
            pltpu.VMEM((total, PAIR), F32),
        ],
        8,
        "attention_backward",
        {first + i: i for i in range(n_before)},
    )


def head_weights_backward(plan, table, near, far, grad, narrow, wide):
    n, n_z = plan.n_seq, plan.n_z
    half, seqs, length, width = near.shape
    cols3 = grad.shape[2]
    own_rows = width // plan.n_dp
    total = n * length
    span = wide.shape[2]

    def kernel(t, near_ref, far_ref, grad_ref, narrow_ref, wide_ref, *rest):
        w_keep, w_send, w_acc, b_acc = rest
        step_id = pl.program_id(0)

        @pl.when(step_id == 0)
        def _():
            w_acc[...] = jnp.zeros_like(w_acc)
            b_acc[...] = jnp.zeros_like(b_acc)

        for part, source in enumerate((near_ref, far_ref)):
            rows = source[...].reshape(half * length, width)
            these = grad_ref[0, part * half * length : (part + 1) * half * length, :]
            w_acc[...] += dot(rows, these, 0, 0)
        b_acc[0:1, :] += jnp.sum(grad_ref[0].astype(F32), 0, keepdims=True)

        @pl.when(step_id == seqs - 1)
        def _():
            for target, k in ((w_keep, 0), (w_send, 1)):
                for z in range(n_z):
                    row = (2 * z + t.core(k)) * own_rows
                    target[z, :own_rows, :] = w_acc[aligned(row, own_rows), :].astype(BF16)
                    here = (t.s == z).astype(F32)
                    last = lax.broadcasted_iota(jnp.int32, (8, cols3), 0) == 7
                    rows = jnp.where(
                        last, b_acc[0:1, :] * here, narrow_ref[2 * z + t.core(k)]
                    )
                    target[z, own_rows : own_rows + 8, :] = rows.astype(BF16)
                    target[z, own_rows + 8 :, :] = jnp.zeros((PAD - 8, cols3), BF16)
                if k == 0:
                    for r in range(n):
                        rows = wide_ref[r].astype(BF16)
                        target[t.member(r, t.c), own_rows + 8 :, :span] = rows

    block = pl.BlockSpec((half, 1, length, width), lambda g, t: (0, g, 0, 0))
    w_out = (n_z, own_rows + PAD, cols3)
    return call(
        kernel,
        table,
        [near, far, grad, narrow, wide],
        [
            block,
            block,
            pl.BlockSpec((1, total, cols3), lambda g, t: (g, 0, 0)),
            whole_block(narrow.shape),
            whole_block(wide.shape),
        ],
        [shape(w_out), shape(w_out)],
        [whole_block(w_out), whole_block(w_out)],
        (seqs,),
        [pltpu.VMEM((width, cols3), F32), pltpu.VMEM((8, cols3), F32)],
        8,
        "head_weights_backward",
    )


def output_norm(plan, table, pieces, where, inputs, vectors, w_out, come, near, far, others):
    n, n_z = plan.n_seq, plan.n_z
    half = n // 2
    tokens, width = inputs.shape
    own_rows = w_out.shape[0]
    cols = width // n
    tile = 128
    n_moves = 2 + 2 * (n_z - 1) * n

    def kernel(t, in_ref, vec_ref, w_ref, come_ref, near_ref, far_ref, on_ref, of_ref, *rest):
        refs, rest = rest[: len(pieces)], rest[len(pieces) :]
        sum_ref, norm_ref, low_ref, full_ref, sems = rest

        def row(z, k):
            return aligned((z * 2 + t.core(k)) * own_rows, own_rows)

        moves = []
        for k, source in enumerate((w_ref, come_ref)):
            at = full_ref.at[row(t.behind(0), k)]
            lanes = source.shape[1] - width
            moves.append((source.at[pl.ds(0, own_rows), pl.ds(lanes, width)], at))
        for k, (first, second) in enumerate(((near_ref, far_ref), (on_ref, of_ref))):
            for j in range(1, n_z):
                for r in range(n):
                    source = first if r < half else second
                    at = full_ref.at[
                        row(t.behind(j), k),
                        aligned(t.member(r, t.core(k)) * cols, cols),
                    ]
                    moves.append((source.at[r % half, j - 1], at))
        copies = copies_of(moves, sems)
        for copy in copies:
            copy.start()
        for copy in copies:
            copy.wait()

        def each_tile(i, carry):
            rows = aligned(i * tile, tile)
            total = in_ref[rows, :].astype(F32) + vec_ref[2:3, :]
            for r, (a, m) in enumerate(where):
                weights = full_ref[aligned(t.member(r, t.c) * cols, cols), :]
                total += dot(refs[a][m, rows, :], weights)
            unit, _ = statistics(total)
            normed = unit * vec_ref[3:4, :] + vec_ref[4:5, :]
            sum_ref[rows, :] = total
            norm_ref[rows, :] = normed
            low_ref[rows, :] = normed.astype(BF16)
            return carry

        lax.fori_loop(0, tokens // tile, each_tile, 0)

    full = (tokens, width)
    return call(
        kernel,
        table,
        [inputs, vectors, w_out, come, near, far, *others, *pieces],
        [whole_block(full), whole_block(vectors.shape)]
        + [ANY] * 6
        + [whole_block(p.shape) for p in pieces],
        [shape(full, F32), shape(full, F32), shape(full), shape((width, width))],
        [whole_block(full)] * 3 + [whole_block((width, width))],
        (1,),
        [pltpu.SemaphoreType.DMA((n_moves,))],
        7,
        "output_norm",
    )


def flatten(remote):
    arrays, found = [], []
    for near, far in remote:
        found += [(len(arrays), i) for i in range(near.shape[1])]
        arrays += [near, far]
    return arrays, found


def gelu_parts(v):
    big = 0.5 + 0.5 * lax.erf(v * np.float32(np.sqrt(0.5)))
    small = jnp.exp(-0.5 * v * v) * np.float32(1.0 / np.sqrt(2.0 * np.pi))
    return v * big, big + v * small


def up_forward(plan, table, low, other_low, w_up, come, remote, bias):
    n, n_z = plan.n_seq, plan.n_z
    half = n // 2
    tokens, width = low.shape
    own_rows, hidden = w_up.shape
    quarter = hidden // 2 // n
    n_moves = 2 + n_z - 1
    tile = 128

    remote, found = flatten(remote)

    def kernel(t, low_ref, other_ref, up_ref, come_ref, bias_ref, *rest):
        remote_refs, rest = rest[: len(remote)], rest[len(remote) :]
        act_ref, slope_ref, w_hbm, w, sems, out_sem = rest
        step_id = pl.program_id(0)

        def moves(r):
            member = t.member(r, t.c)
            z = t.behind(0)
            at = w.at[r]

            def row(k):
                return aligned((z * 2 + t.core(k)) * own_rows, own_rows)

            lanes = aligned((member * 2 + t.c) * quarter, quarter)
            out = [(up_ref.at[:, lanes], at.at[row(0)])]
            lanes = aligned(member * quarter, quarter)
            out.append((come_ref.at[pl.ds(0, own_rows), lanes], at.at[row(1)]))
            for j in range(1, n_z):
                z_j = t.behind(j)
                a, i = found[j - 1]
                source = remote_refs[a + (r >= half)]
                for k in range(2):
                    rows = aligned((z_j * 2 + t.core(k)) * own_rows, own_rows)
                    out.append(
                        (
                            source.at[r % half, i, pl.ds(k * own_rows, own_rows)],
                            at.at[rows],
                        )
                    )
            return out

        def copies(r):
            return copies_of(moves(r), sems.at[r])

        @pl.when(step_id == 0)
        def _():
            for r in range(n):
                for copy in copies(r):
                    copy.start()

        for r in range(n):

            @pl.when(step_id == r)
            def _(r=r):
                for copy in copies(r):
                    copy.wait()

        def out_copy(r):
            return pltpu.make_async_copy(w.at[r], w_hbm.at[r], out_sem.at[r])

        for r in range(n):

            @pl.when(step_id == r)
            def _(r=r):
                out_copy(r).start()

        weights = w.at[step_id]
        for part, source in enumerate((low_ref, other_ref)):

            def step(i, carry, part=part, source=source):
                rows = pl.ds(pl.multiple_of(i * tile, tile), tile)
                pre = dot(source[rows, :], weights[...]) + bias_ref[0]
                active, slope = gelu_parts(pre)
                rows = pl.ds(pl.multiple_of(part * tokens + i * tile, tile), tile)
                act_ref[0, rows, :] = active.astype(BF16)
                slope_ref[0, rows, :] = slope.astype(BF16)
                return carry

            lax.fori_loop(0, tokens // tile, step, 0)

        @pl.when(step_id == n - 1)
        def _():
            for r in range(n):
                out_copy(r).wait()

    big = (n, 2 * tokens, quarter)
    block = pl.BlockSpec((1, 2 * tokens, quarter), lambda r, t: (r, 0, 0))
    return call(
        kernel,
        table,
        [low, other_low, w_up, come, bias] + remote,
        [whole_block(low.shape)] * 2
        + [ANY] * 2
        + [
            pl.BlockSpec(
                (1, 1, quarter),
                lambda r, t: (2 * t.member(r, t.c) + t.c, 0, 0),
            )
        ]
        + [ANY] * len(remote),
        [shape(big), shape(big), shape((n, width, quarter))],
        [block, block, ANY],
        (n,),
        [
            pltpu.VMEM((n, width, quarter), BF16),
            pltpu.SemaphoreType.DMA((n, 2 + 2 * (n_z - 1))),
            pltpu.SemaphoreType.DMA((n,)),
        ],
        15,
        "up_forward",
    )


def down_forward(plan, table, active, w_down, remote):
    n, n_z = plan.n_seq, plan.n_z
    half = n // 2
    tokens = active.shape[1] // 2
    quarter = active.shape[2]
    own_hidden, width = w_down.shape
    cols = width // n

    remote, found = flatten(remote)

    def kernel(t, act_ref, down_ref, *rest):
        remote_refs, rest = rest[: len(remote)], rest[len(remote) :]
        own_ref, other_ref, w_hbm, w, acc, sems, out_sem = rest
        step_id = pl.program_id(0)
        out_copy = pltpu.make_async_copy(w, w_hbm, out_sem)

        @pl.when(step_id == 0)
        def _():
            moves = [
                (down_ref, w.at[aligned(t.behind(0) * own_hidden, own_hidden)])
            ]
            for j in range(1, n_z):
                rows = aligned(t.behind(j) * own_hidden, own_hidden)
                a, i = found[j - 1]
                for r in range(n):
                    source = remote_refs[a + (r >= half)]
                    lanes = aligned(t.member(r, t.c) * cols, cols)
                    moves.append((source.at[r % half, i], w.at[rows, lanes]))
            copies = copies_of(moves, sems)
            for copy in copies:
                copy.start()
            acc[...] = jnp.zeros_like(acc)
            for copy in copies:
                copy.wait()
            out_copy.start()

        rows = aligned(t.member(step_id, t.c) * quarter, quarter)
        acc[...] += dot(act_ref[0], w[rows, :])

        @pl.when(step_id == n - 1)
        def _():
            own_ref[...] = acc[:tokens, :]
            other_ref[...] = acc[tokens:, :].astype(BF16)
            out_copy.wait()

    full = (tokens, width)
    return call(
        kernel,
        table,
        [active, w_down] + remote,
        [pl.BlockSpec((1, 2 * tokens, quarter), lambda r, t: (r, 0, 0))]
        + [ANY] * (1 + len(remote)),
        [shape(full, F32), shape(full), shape((n * quarter, width))],
        [whole_block(full), whole_block(full), ANY],
        (n,),
        [
            pltpu.VMEM((n * quarter, width), BF16),
            pltpu.VMEM((2 * tokens, width), F32),
            pltpu.SemaphoreType.DMA((1 + (n_z - 1) * n,)),
            pltpu.SemaphoreType.DMA,
        ],
        10,
        "down_forward",
    )


def norm_two(table, normed, own, come, cotangent, vectors):
    tokens, width = normed.shape
    tile = 128

    def kernel(t, norm_ref, own_ref, come_ref, cot_ref, vec_ref, *rest):
        out_ref, grad_ref, low_ref, sums = rest

        @pl.when(pl.program_id(0) == 0)
        def _():
            sums[...] = jnp.zeros_like(sums)

        second = norm_ref[...] + (own_ref[...] + come_ref[...].astype(F32) + vec_ref[5:6, :])
        unit, root = statistics(second)
        gain = vec_ref[6:7, :]
        out_ref[...] = (unit * gain + vec_ref[7:8, :]).astype(BF16)
        above = cot_ref[...].astype(F32)
        grad = norm_back(unit, root, gain, above)
        low = grad.astype(BF16)
        grad_ref[...] = grad
        low_ref[...] = low
        add_rows(sums, 0, low.astype(F32))
        add_rows(sums, 1, above * unit)
        add_rows(sums, 2, above)

    block = pl.BlockSpec((tile, width), lambda i, t: (i, 0))
    full = (tokens, width)
    return call(
        kernel,
        table,
        [normed, own, come, cotangent, vectors],
        [block] * 4 + [whole_block(vectors.shape)],
        [shape(full), shape(full, F32), shape(full), shape((8, width), F32)],
        [block] * 3 + [whole_block((8, width))],
        (tokens // tile,),
        [],
        6,
        "norm_two",
    )


def ffn_backward(plan, table, low, other_low, w_down, w_up, slope):
    n = plan.n_seq
    tokens, width = low.shape
    quarter = slope.shape[2]

    def kernel(t, low_ref, other_ref, down_ref, up_ref, slope_ref, *rest):
        pre_ref, sum_ref, own_ref, come_ref, acc = rest
        step_id = pl.program_id(0)

        @pl.when(step_id == 0)
        def _():
            acc[...] = jnp.zeros_like(acc)

        sums = jnp.zeros((1, quarter), F32)
        for part, source in enumerate((low_ref, other_ref)):
            rows = pl.ds(part * tokens, tokens)
            grad = dot(source[...], down_ref[...], 1, 1) * slope_ref[0, rows, :].astype(F32)
            grad = grad.astype(BF16)
            pre_ref[0, rows, :] = grad
            sums += jnp.sum(grad.astype(F32), 0, keepdims=True)
            acc[rows, :] += dot(grad, up_ref[0], 1, 1)
        row = lax.broadcasted_iota(jnp.int32, (8, quarter), 0)
        sum_ref[0] = jnp.where(row == 0, sums, 0.0)

        @pl.when(step_id == n - 1)
        def _():
            own_ref[...] = acc[:tokens, :]
            come_ref[...] = acc[tokens:, :].astype(BF16)

    big = pl.BlockSpec((1, 2 * tokens, quarter), lambda r, t: (r, 0, 0))
    full = (tokens, width)
    return call(
        kernel,
        table,
        [low, other_low, w_down, w_up, slope],
        [whole_block(full)] * 2
        + [
            pl.BlockSpec((quarter, width), lambda r, t: (t.member(r, t.c), 0)),
            pl.BlockSpec((1, width, quarter), lambda r, t: (r, 0, 0)),
            big,
        ],
        [shape(slope.shape), shape((n, 8, quarter), F32), shape(full, F32), shape(full)],
        [
            big,
            pl.BlockSpec((1, 8, quarter), lambda r, t: (r, 0, 0)),
            whole_block(full),
            whole_block(full),
        ],
        (n,),
        [pltpu.VMEM((2 * tokens, width), F32)],
        13,
        "ffn_backward",
    )


def down_weights(plan, table, active, low, other_low, base):
    n, n_z = plan.n_seq, plan.n_z
    half = n // 2
    tokens, width = low.shape
    quarter = active.shape[2]
    cols = width // n

    def kernel(t, act_ref, low_ref, other_ref, out_ref, grads):
        @pl.when(pl.program_id(0) == 0)
        def _():
            for r in range(half):
                lanes = aligned(t.member(base + r, t.c) * cols, cols)
                here = pl.ds(r * cols, cols)
                grads[:tokens, here] = low_ref[:, lanes]
                grads[tokens:, here] = other_ref[:, lanes]

        total = dot(act_ref[0], grads[...], 0, 0)
        for r in range(half):
            out_ref[r, 0] = total[:, r * cols : (r + 1) * cols].astype(BF16)

    return call(
        kernel,
        table,
        [active, low, other_low],
        [pl.BlockSpec((1, 2 * tokens, quarter), lambda r, t: (r, 0, 0))]
        + [whole_block((tokens, width))] * 2,
        [shape((half, n_z, quarter, cols))],
        [
            pl.BlockSpec(
                (half, 1, quarter, cols), lambda r, t: (0, t.member(r, t.c), 0, 0)
            )
        ],
        (n,),
        [pltpu.VMEM((2 * tokens, half * cols), BF16)],
        5,
        "down_weights",
    )[0]


def up_weights(plan, table, low, other_low, grad_pre, base):
    n, n_z = plan.n_seq, plan.n_z
    half = n // 2
    tokens, width = low.shape
    quarter = grad_pre.shape[2]
    own_rows = width // plan.n_dp

    def kernel(t, low_ref, other_ref, grad_ref, out_ref):
        for z in range(n_z):
            lanes = pl.ds(2 * z * own_rows, 2 * own_rows)
            total = dot(low_ref[:, lanes], grad_ref[0, :tokens, :], 0, 0)
            total += dot(other_ref[:, lanes], grad_ref[0, tokens:, :], 0, 0)
            total = total.astype(BF16)
            out_ref[0, z, :, :quarter] = total[:own_rows]
            out_ref[0, z, :, quarter:] = total[own_rows:]

    dims = (half, n_z, own_rows, 2 * quarter)
    return call(
        kernel,
        table,
        [low, other_low, grad_pre],
        [whole_block((tokens, width))] * 2
        + [pl.BlockSpec((1, 2 * tokens, quarter), lambda i, t: (base + i, 0, 0))],
        [shape(dims)],
        [pl.BlockSpec((1,) + dims[1:], lambda i, t: (i, 0, 0, 0))],
        (half,),
        [],
        6,
        "up_weights",
    )[0]


def norm_one_back(plan, table, grad_second, own, come, first_sum, vectors, w_out, sums_two):
    n = plan.n_seq
    tokens, width = own.shape
    cols = width // n
    tile = 128

    own_rows = width // plan.n_dp

    def kernel(t, grad_ref, own_ref, come_ref, sum_ref, vec_ref, w_ref, two_ref, *rest):
        first_ref, low_ref, narrow_ref = rest[:3]
        keep_ref, send_ref, sums = rest[3:]
        sums[0:3, :] = jnp.zeros((3, width), F32)
        sums[3:6, :] = two_ref[0:3, :]
        sums[6:8, :] = jnp.zeros((2, width), F32)

        def each_tile(i, carry):
            rows = aligned(i * tile, tile)
            above = grad_ref[rows, :] + (own_ref[rows, :] + come_ref[rows, :].astype(F32))
            unit, root = statistics(sum_ref[rows, :])
            grad = norm_back(unit, root, vec_ref[3:4, :], above)
            low = grad.astype(BF16)
            first_ref[rows, :] = grad
            low_ref[rows, :] = low
            add_rows(sums, 0, low.astype(F32))
            add_rows(sums, 1, above * unit)
            add_rows(sums, 2, above)
            for r in range(n):
                weights = w_ref[aligned(t.member(r, t.c) * cols, cols), :]
                target = keep_ref if r < half else send_ref
                target[r % half, rows, :] = dot(low, weights, 1, 1).astype(BF16)
            return carry

        lax.fori_loop(0, tokens // tile, each_tile, 0)
        narrow_ref[...] = jnp.zeros_like(narrow_ref)
        for owner in range(plan.n_dp):
            lanes = pl.ds(owner * own_rows, own_rows)
            narrow_ref[owner, :, 0:own_rows] = sums[:, lanes]

    full = (tokens, width)
    half = n // 2
    part = (half, tokens, cols)
    narrow = (plan.n_dp, 8, 3 * cols)
    return call(
        kernel,
        table,
        [grad_second, own, come, first_sum, vectors, w_out, sums_two],
        [whole_block(full)] * 4
        + [whole_block(v.shape) for v in (vectors, w_out, sums_two)],
        [shape(full, F32), shape(full), shape(narrow, F32)] + [shape(part)] * 2,
        [whole_block(full)] * 2 + [whole_block(narrow)] + [whole_block(part)] * 2,
        (1,),
        [pltpu.VMEM((8, width), F32)],
        8,
        "norm_one_back",
    )


def out_weights(plan, table, pieces, where, low):
    n, n_z = plan.n_seq, plan.n_z
    tokens, width = low.shape
    cols = width // n
    own_rows = width // plan.n_dp

    def kernel(t, low_ref, *rest):
        refs, (keep_ref, send_ref, both) = rest[: len(pieces)], rest[len(pieces) :]
        for r, (a, m) in enumerate(where):
            z = t.member(r, t.c)
            both[...] = dot(refs[a][m], low_ref[...], 0, 0).astype(BF16)
            for target, k in ((send_ref, 1), (keep_ref, 0)):
                rows = aligned(t.core(k) * own_rows, own_rows)
                for s in range(n):
                    at = aligned(t.member(s, t.core(k)) * cols, cols)
                    target[s, z] = both[rows, at]

    dims = (n, n_z, own_rows, cols)
    return call(
        kernel,
        table,
        [low, *pieces],
        [whole_block(low.shape)] + [whole_block(p.shape) for p in pieces],
        [shape(dims), shape(dims)],
        [whole_block(dims)] * 2,
        (1,),
        [pltpu.VMEM((cols, width), BF16)],
        0,
        "out_weights",
    )


def parts_along_z(plan, table, terms):
    n_z = plan.n_z
    rows = terms[0][0].shape[1]
    operands = [v for group in terms for v in group]
    lanes = sum(group[0].shape[2] for group in terms)

    def kernel(t, *refs):
        sources, outs = refs[: len(operands)], refs[len(operands) :]
        for j in range(n_z):

            @pl.when(pl.program_id(0) == j)
            def _(j=j):
                left, at = list(sources), 0
                target = outs[2 * j // n_z]
                for group in terms:
                    total = left.pop(0)[0].astype(F32)
                    for _ in group[1:]:
                        total += left.pop(0)[0].astype(F32)
                    end = at + total.shape[1]
                    target[j % (n_z // 2), :, at:end] = total.astype(BF16)
                    at = end

    def member(i, t):
        here = 0
        for k in range(plan.z_bits):
            here = here | ((i >> k) & 1) << (plan.z_bits - 1 - k)
        return (t.z ^ here, 0, 0)

    out = (n_z // 2, rows, lanes)
    return call(
        kernel,
        table,
        operands,
        [pl.BlockSpec((1,) + v.shape[1:], member) for v in operands],
        [shape(out)] * 2,
        [whole_block(out)] * 2,
        (n_z,),
        [],
        2,
        "parts_along_z",
    )


def split_by_core(plan, table, pieces, split):
    _, rows, lanes = pieces[0].shape
    half = split // 2
    n_pieces = len(pieces)

    def kernel(t, *refs):
        for k, target in enumerate(refs[n_pieces:]):
            size = half if k < 2 else lanes - split
            at = aligned(t.core(k) * half, half) if k < 2 else pl.ds(split, size)
            total = refs[0][0, :, at].astype(F32)
            for ref in refs[1:n_pieces]:
                total += ref[0, :, at].astype(F32)
            target[...] = total.astype(BF16)

    outs = [(rows, half), (rows, half), (rows, lanes - split)]
    return call(
        kernel,
        table,
        pieces,
        [whole_block(p.shape) for p in pieces],
        [shape(o) for o in outs],
        [whole_block(o) for o in outs],
        (1,),
        [],
        0,
        "split_by_core",
    )


def place(plan, table, near, far, outs, moves, name):
    n = plan.n_seq
    half = n // 2

    def kernel(t, near_ref, far_ref, *targets):
        for r in range(n):
            source = near_ref if r < half else far_ref
            for src, o, at in moves:
                targets[o][:, at(t, r)] = source[(r % half,) + src].astype(F32)

    return call(
        kernel,
        table,
        [near, far],
        [whole_block(near.shape)] * 2,
        [shape(o, F32) for o in outs],
        [whole_block(o) for o in outs],
        (1,),
        [],
        0,
        name,
    )


def local(
    plan,
    inputs,
    w_query,
    w_key,
    w_value,
    b_query,
    b_value,
    w_out,
    b_out,
    gain_one,
    shift_one,
    w_up,
    b_up,
    w_down,
    b_down,
    gain_two,
    shift_two,
    cotangent,
):
    n_dp, n, n_z = plan.n_dp, plan.n_seq, plan.n_z
    half = n // 2
    seqs, length, width = inputs.shape
    tokens = seqs * length
    own_rows, hidden = w_up.shape
    own_hidden = w_down.shape[0]
    cols = width // n
    cols3 = 3 * cols
    quarter = hidden // 2 // n
    assert n == n_z and quarter == own_hidden
    table = plan
    core = lax.axis_index("dp") % 2

    narrow = jnp.stack(
        [b_query, b_value, b_out, gain_one, shift_one, b_down, gain_two, shift_two]
    )
    vec = jnp.concatenate(
        [
            jnp.pad(narrow, ((0, 0), (0, 4 * cols - own_rows))),
            jnp.pad(b_up[None], ((0, 7), (0, 4 * cols - own_hidden))),
        ],
        0,
    )

    def column_block(t):
        return (pl.ds(0, own_rows), aligned(t.s * cols, cols))

    moves = [
        (i, column_block, 0, lambda t, i=i: (pl.ds(0, own_rows), pl.ds(i * cols, cols)))
        for i in range(4)
    ]
    moves.append((4, lambda t: (pl.ds(0, PAD),), 0, lambda t: (pl.ds(own_rows, PAD),)))
    (first,) = assemble(
        table,
        [w_query, w_key, w_value, w_out, vec],
        moves,
        [shape((own_rows + PAD, 4 * cols))],
        "pack_first",
    )

    def straight(block, j):
        return lax.ppermute(block, BOTH, plan.toward[j])

    near_x = inputs[None]
    for k in range(plan.bits - 1):
        near_x = plan.double(near_x, k)
    mine = [first, straight(first, 1)]

    top = plan.bits - 1

    def final(near, *ready):
        return near, lax.ppermute(after(near, *ready), BOTH, plan.stage[top])

    def begin(block, *ready):
        near = after(block, *ready)[None]
        for k in range(top - 1):
            near = plan.double(near, k)
        return near, lax.ppermute(near, BOTH, plan.stage[top - 1])

    def joined(started, *ready):
        return jnp.concatenate([after(started[0], *ready), started[1]], 0)

    def onward(block, *ready):
        return lax.ppermute(after(block, *ready), BOTH, plan.toward[1])

    ready = (near_x, mine[1])
    far_x = final(near_x, *ready)[1]
    mine.append(onward(mine[1], *ready))
    for j in range(3, n_z):
        mine.append(onward(mine[-1]))

    moves = []
    for z in range(n_z):
        moves.append(
            (
                0,
                lambda t, z=z: (
                    pl.ds(0, own_rows),
                    aligned((2 * z + (1 - t.c)) * quarter, quarter),
                ),
                0,
                lambda t, z=z: (pl.ds(0, own_rows), pl.ds(z * quarter, quarter)),
            )
        )
    moves.append(
        (
            1,
            lambda t: (pl.ds(0, own_rows),),
            0,
            lambda t: (pl.ds(0, own_rows), pl.ds(n * quarter, width)),
        )
    )
    (across,) = assemble(
        table,
        [after(w_up, mine[2]), w_out],
        moves,
        [shape((own_rows, n * quarter + width))],
        "pack_across",
    )
    come = plan.swap(across)


    def rows_at(start, size):
        return lambda t: (pl.ds(start, size), pl.ds(0, quarter))

    moves = [
        (
            0,
            lambda t: (
                pl.ds(0, own_rows),
                aligned((2 * t.s + t.c) * quarter, quarter),
            ),
            0,
            rows_at(0, own_rows),
        ),
        (
            1,
            lambda t: (pl.ds(0, own_rows), aligned(t.s * quarter, quarter)),
            0,
            rows_at(own_rows, own_rows),
        ),
    ]
    moves.append(
        (
            2,
            lambda t: (pl.ds(0, own_hidden), aligned(t.s * cols, cols)),
            1,
            lambda t: (pl.ds(0, own_hidden),),
        )
    )
    second, down = assemble(
        table,
        [w_up, come, w_down],
        moves,
        [shape((2 * own_rows, quarter)), shape((own_hidden, cols))],
        "pack_second",
    )
    ups = [onward(second)]

    ready = (far_x, second) + tuple(mine[1:])
    mine_all = jnp.stack([after(piece, *ready) for piece in mine])
    theirs = plan.swap(mine_all)
    outs = jnp.stack([after(piece, *ready)[:own_rows, cols3:] for piece in mine[1:]])
    outs_started = begin(outs)
    ups.append(onward(ups[0], *ready))
    downs = [onward(down, *ready)]
    w_qkv, vectors, up_bias = head_weights(plan, table, mine_all, theirs)
    qkv, lse = [], []

    def attend(g, before, *ready):
        out, *parts, total = attention_forward(
            plan, table, g, near_x, far_x, w_qkv, after(vectors, *ready), before
        )
        qkv.append(out)
        lse.append(total)
        return parts

    parts = attend(0, [])

    near_out = joined(outs_started, parts[0])
    ready = (near_out, parts[0], ups[1], downs[0])
    outs = final(near_out, *ready)
    ups.append(onward(ups[1], *ready))
    downs.append(onward(downs[0], *ready))
    two_started = begin(jnp.stack([after(piece, *ready) for piece in ups[:2]]))
    parts = attend(1, parts, *ready)

    near_two = joined(two_started, parts[0])
    ready = (near_two, outs[1], ups[2], downs[1], parts[0])
    for j in range(3, n_z - 1):
        ups.append(onward(ups[-1]))
        downs.append(onward(downs[-1]))
    others = [plan.swap(after(part, *ready)) for part in outs]
    up_two = final(near_two, *ready)
    downs.append(onward(downs[-1], *ready))
    three_started = begin(jnp.stack([after(piece, *ready) for piece in ups[2:]]))
    for g in range(2, seqs):
        parts = attend(g, parts, *ready)

    contexts = parts
    send = after(parts[1], up_two[1], three_started[1], *others)
    near_three = joined(three_started, send)
    up_three = final(near_three)
    pieces, where = distinct(plan.exchange(parts[0], send))
    pieces = [p.reshape(p.shape[0], tokens, cols) for p in pieces]
    downs = jnp.stack([after(piece, near_three) for piece in downs])
    downs_started = begin(downs, *pieces)
    first_sum, normed, low, full_out = output_norm(
        plan,
        table,
        pieces,
        where,
        after(inputs.reshape(tokens, width), downs),
        vectors,
        w_out,
        come,
        *outs,
        others,
    )

    other_low = plan.swap(after(low, up_three[1]))
    near_down = joined(downs_started, low)
    ready = (other_low, up_three[1], near_down)
    down_all = final(near_down, *ready)
    active, slope, up_kept = up_forward(
        plan, table, after(low, *ready), other_low, w_up, come, [up_two, up_three], up_bias
    )
    own, away, down_kept = down_forward(plan, table, active, w_down, [down_all])
    output, grad_second, low_two, sums_two = norm_two(
        table, normed, own, plan.swap(away), cotangent.reshape(tokens, width), vectors
    )

    def begun(send, k, *ready):
        return lax.ppermute(after(send, *ready), BOTH, plan.stage[k])

    def summed(keep, come, k, *ready):
        low = (1 << k) // 2
        come = after(come, *ready)
        return add(keep[:low], come[:low]), add(keep[low:], come[low:])

    def middle(keep, come, *ready):
        keep, send = summed(keep, come, top, *ready)
        for k in reversed(range(1, top)):
            keep, send = summed(keep, begun(send, k), k)
        return keep, send

    other_two = plan.swap(low_two)
    down_send = down_weights(plan, table, active, low_two, other_two, half)
    down_come = begun(down_send, top)
    down_keep = down_weights(plan, table, active, after(low_two, down_send), other_two, 0)
    grad_pre, sums_up, own, away = ffn_backward(
        plan, table, after(low_two, down_keep), other_two, down_kept, up_kept, slope
    )
    away = plan.swap(away)
    low = after(low, own)
    up_send = up_weights(plan, table, low, other_low, grad_pre, half)
    down_keep, down_send = middle(down_keep, down_come, up_send)
    down_last = begun(down_send, 0)
    grad_first, low_one, sums, *parts = norm_one_back(
        plan,
        table,
        grad_second,
        after(own, down_send),
        away,
        first_sum,
        vectors,
        full_out,
        sums_two,
    )
    up_keep = up_weights(plan, table, after(low, low_one), other_low, grad_pre, 0)
    parts = [p.reshape(half, seqs, length, cols) for p in parts]
    found = plan.exchange(parts[0], after(parts[1], down_last), up_keep)
    out_keep, out_send = out_weights(
        plan, table, pieces, where, after(low_one, found[half][0])
    )
    parts, up_where = distinct(found)
    parts = [after(part, out_keep) for part in parts]
    out_come = plan.swap(after(out_send, *parts))

    def sent_along_z(terms, *ready):
        terms = [[after(group[0], *ready)] + group[1:] for group in terms]
        keep, send = parts_along_z(plan, table, terms)
        return keep, lax.ppermute(send, BOTH, plan.along[0])

    def on_along_z(keep, come, *ready):
        for way in plan.along[1:]:
            low = keep.shape[0] // 2
            come = after(come, *ready)
            sent = add(keep[low:], come[low:])
            keep = add(keep[:low], come[:low])
            come = lax.ppermute(sent, BOTH, way)
        return keep, come

    def total(keep, come, *ready):
        return add(after(keep, *ready), come)[0]

    def back(g, before, *ready):
        return attention_backward(
            plan,
            table,
            g,
            seqs,
            after(qkv[g], *ready),
            lse[g],
            contexts,
            parts,
            up_where,
            w_qkv,
            before,
        )

    ready = (out_keep, out_come) + tuple(parts)
    up_come = begun(up_send, top, *ready)
    out_come = after(out_come, *ready)
    out_sent = add(out_keep[half:], out_come[half:])
    out_first = begun(out_sent, top)
    out_kept = add(out_keep[:half], out_come[:half])
    shared = back(0, [], out_sent, out_kept, *ready)
    down_along = sent_along_z([[down_keep[0], down_last[0]]], shared[0])
    shared = back(1, list(shared), down_along[0])
    up_keep, up_send = middle(up_keep, up_come, shared[0])
    up_last = begun(up_send, 0)
    down_along = on_along_z(*down_along, up_send)
    out_kept, out_sent = middle(out_kept, out_first, up_send)
    out_last = begun(out_sent, 0)
    for g in range(2, seqs):
        shared = back(g, list(shared), up_send, out_sent, down_along[0])
    grad_qkv, part_keep, part_send = shared
    up_along = sent_along_z(
        [[up_keep[0], up_last[0]], [out_kept[0], out_last[0]]], grad_qkv
    )

    part_come = begun(part_send, top, up_along[0])
    down_started = begin(total(*down_along, up_along[0]))
    last_keep, last_send = head_weights_backward(
        plan, table, near_x, far_x, after(grad_qkv, up_along[0], down_started[0]), sums, sums_up
    )
    down_near = joined(down_started, last_keep)
    down_far = plan.final(down_near)
    up_along = on_along_z(*up_along, last_keep)
    last_come = plan.swap(last_send)
    last_along = sent_along_z([[last_keep, last_come]], up_along[0])
    part_keep, part_send = middle(part_keep, part_come, last_along[0])
    part_last = begun(part_send, 0)

    def lanes(size):
        return lambda t, r: aligned(t.member(r, t.c) * size, size)

    grad_inputs = grad_first.reshape(inputs.shape) + (
        part_keep[0].astype(F32) + part_last[0].astype(F32)
    )
    (grad_down,) = place(
        plan,
        table,
        after(down_near, part_send),
        down_far,
        [(own_hidden, width)],
        [((slice(None),), 0, lanes(cols))],
        "place_down",
    )
    last_along = on_along_z(*last_along, part_last, grad_down)
    up_along = (after(up_along[0], last_along[0]), up_along[1])
    up_kept, up_sent, grad_out = split_by_core(plan, table, up_along, 2 * quarter)
    up_come = plan.swap(up_sent)
    up_near = plan.halfway(jnp.concatenate([up_kept, up_come, grad_out], 1))
    up_far = plan.final(up_near)
    grad_inputs = grad_first.reshape(inputs.shape) + (
        part_keep[0].astype(F32) + after(part_last[0], up_near).astype(F32)
    )
    last_near = plan.halfway(total(*last_along, grad_inputs))
    last_far = plan.final(last_near)
    grad_up, grad_out = place(
        plan,
        table,
        after(up_near, last_near),
        up_far,
        [(own_rows, hidden), (own_rows, width)],
        [
            (
                (slice(None), pl.ds(k * quarter, quarter)),
                0,
                lambda t, r, k=k: aligned(
                    (2 * t.member(r, t.c) + t.core(k)) * quarter, quarter
                ),
            )
            for k in range(2)
        ]
        + [((slice(None), pl.ds(2 * quarter, cols)), 1, lanes(cols))],
        "place_up",
    )
    grad_wq, grad_wk, grad_wv = place(
        plan,
        table,
        last_near,
        last_far,
        [(own_rows, width)] * 3,
        [
            ((pl.ds(0, own_rows), pl.ds(m * cols, cols)), m, lanes(cols))
            for m in range(3)
        ],
        "place_heads",
    )
    vec_out = jnp.sum(last_near[:, own_rows:].astype(F32), 0)
    vec_out += jnp.sum(last_far[:, own_rows:].astype(F32), 0)
    biases = vec_out[7].reshape(3, 2, own_rows)
    biases = jnp.where(core == 0, biases[:, 0], biases[:, 1])
    return (
        output.reshape(inputs.shape),
        grad_inputs,
        grad_wq,
        grad_wk,
        grad_wv,
        biases[0],
        biases[2],
        grad_out,
        vec_out[0, :own_rows],
        vec_out[1, :own_rows],
        vec_out[2, :own_rows],
        grad_up,
        vec_out[8, :own_hidden],
        grad_down,
        vec_out[3, :own_rows],
        vec_out[4, :own_rows],
        vec_out[5, :own_rows],
    )


def solution(mesh):
    plan = Plan(mesh.shape["dp"], mesh.shape["seq"])
    rows, vector, token = P("dp", None), P("dp"), P("dp", "seq", None)
    weights = (rows,) * 3 + (vector,) * 2 + (rows,) + (vector,) * 3
    weights += (rows, vector, rows) + (vector,) * 3
    return jax.shard_map(
        functools.partial(local, plan),
        mesh=mesh,
        in_specs=(token,) + weights + (token,),
        out_specs=(token, token) + weights,
        check_vma=False,
    )
```
